32 devices in a mesh: outer: 4 (over x, core), inner: 8 (over z, y).
Axes of the slice: x: 2, y: 2, z: 4, core: 2. Of those that a mesh axis runs over, the one named last changes fastest.
Arguments:
- query_tiles: bfloat16 [4096, 768], P(('outer', 'inner')), may hold values from -7 to 7
- key_tiles: bfloat16 [4096, 768], P(('outer', 'inner')), may hold values from -6 to 6
- value_tiles: bfloat16 [4096, 768], P(('outer', 'inner')), may hold values from -6 to 6
- cotangent: bfloat16 [4096, 768], P(('outer', 'inner')), may hold values from -6 to 6
- row_lengths: int32 [128], P(('outer', 'inner')), may hold values from 1 to 32
Outputs:
- attended: bfloat16 [4096, 768], P(('outer', 'inner'))
- query_grad: bfloat16 [4096, 768], P(('outer', 'inner'))
- key_grad: bfloat16 [4096, 768], P(('outer', 'inner'))
- value_grad: bfloat16 [4096, 768], P(('outer', 'inner'))
The draws below stay inside these ranges and needn't reach their ends.
All inputs are finite; a program needn't handle non-finite values.
Results may differ from the reference program's by a relative error of at most 0.0203.
Values may be sent and summed in bfloat16 or wider, within the bound.
A program may use at most 128 MiB of HBM per device.

```python
import jax
import jax.numpy as jnp
import numpy as np
from jax import lax

HEADS = 16
HEAD = 48
D = 768
TOK_DEV = 128
ROW = 32
STRIDE_GROUP = 4
STRIDE_SLIDE = 16
TOKENS = 4096
ROWS = 128
GROUP = 1024


def base_field(key, salt_value):
    field_key = jax.random.fold_in(key, salt_value)
    return jnp.clip(1.4 * jax.random.normal(field_key, (TOKENS, HEADS, HEAD), jnp.float32), -6.0, 6.0)


def draw_query_tiles(key, part):
    field_values = base_field(key, 11)
    return field_values.reshape(TOKENS, HEADS * HEAD).astype(jnp.bfloat16)


def draw_key_tiles(key, part):
    field_values = base_field(key, 23)
    return field_values.reshape(TOKENS, HEADS * HEAD).astype(jnp.bfloat16)


def place_ends(values, rng, smallest, high):
    place = [jax.random.randint(jax.random.fold_in(rng, axis), (), 0, length) for axis, length in enumerate(values.shape)]
    widest = values.shape.index(max(values.shape))
    neighbour = place[:widest] + [(place[widest] + 1) % values.shape[widest]] + place[widest + 1:]
    return values.at[tuple(place)].set(smallest).at[tuple(neighbour)].set(high)


def steps_of(key, shape, cuts, smallest, high):
    loudness, own = 1.0, jax.random.fold_in(key, 6)
    for dim, parts in cuts:
        draws = jnp.exp(jax.random.uniform(jax.random.fold_in(own, dim), (parts,), jnp.float32, smallest / len(cuts), high / len(cuts)))
        loudness = loudness * jnp.repeat(draws, shape[dim] // parts).reshape([-1 if axis == dim else 1 for axis in range(len(shape))])
    return loudness


def normal_values(own_key, dims, deviation, bound, split=(), kind=jnp.bfloat16):
    entries = deviation * jax.random.normal(own_key, dims, jnp.float32)
    if split:
        entries = entries * steps_of(own_key, dims, split, -0.22, 0.18)
    return jnp.clip(entries, -bound, bound).astype(kind)


def setup_inputs(seed: int = 0) -> dict:
    seeds = jax.random.split(jax.random.key(seed), 6)
    query_tiles = draw_query_tiles(jax.random.fold_in(seeds[5], 71), 0)
    key_tiles = draw_key_tiles(jax.random.fold_in(seeds[5], 71), 0)
    value_tiles = normal_values(seeds[2], (TOKENS, D), 1.0, 6.0, ((0, 32),))
    cotangent = normal_values(seeds[3], (TOKENS, D), 1.0, 6.0, ((0, 32),))
    row_lengths = place_ends(jax.random.randint(seeds[4], (ROWS,), 1, ROW + 1), jax.random.fold_in(seeds[4], 1), 1, ROW).astype(jnp.int32)
    return dict(query_tiles=query_tiles, key_tiles=key_tiles, value_tiles=value_tiles, cotangent=cotangent, row_lengths=row_lengths)


NEGATIVE_FILL = -1.0e30


def settle(values_in):
    return lax.optimization_barrier(values_in.astype(jnp.bfloat16)).astype(jnp.float32)


def scores_of(query_heads, key_heads, score_scale):
    return jnp.einsum("qhd,khd->hqk", query_heads.astype(jnp.float32), key_heads.astype(jnp.float32)) * score_scale


def branch_stats(query_heads, key_heads, value_heads, key_valid, score_scale):
    raw_scores = scores_of(query_heads, key_heads, score_scale)
    key_keep = jnp.transpose(key_valid)[:, None, :]
    masked = jnp.where(key_keep, raw_scores, NEGATIVE_FILL)
    row_peak = jnp.max(masked, axis=2)
    weights = jnp.where(key_keep, jnp.exp(masked - row_peak[:, :, None]), 0.0)
    row_total = jnp.sum(weights, axis=2)
    weighted = jnp.einsum("hqk,khd->qhd", settle(weights), value_heads.astype(jnp.float32))
    return jnp.transpose(row_peak), jnp.transpose(row_total), weighted


def branch_grads(query_heads, key_heads, value_heads, cotan_heads, log_norm, out_dot, key_valid, score_scale):
    raw_scores = scores_of(query_heads, key_heads, score_scale)
    key_keep = jnp.transpose(key_valid)[:, None, :]
    weights = jnp.where(key_keep, jnp.exp(raw_scores - jnp.transpose(log_norm)[:, :, None]), 0.0)
    weight_grads = jnp.einsum("qhd,khd->hqk", cotan_heads.astype(jnp.float32), value_heads.astype(jnp.float32))
    score_grads = weights * (weight_grads - jnp.transpose(out_dot)[:, :, None])
    low_weights = settle(weights)
    low_grads = settle(score_grads)
    query_part = score_scale * jnp.einsum("hqk,khd->qhd", low_grads, key_heads.astype(jnp.float32))
    key_part = score_scale * jnp.einsum("hqk,qhd->khd", low_grads, query_heads.astype(jnp.float32))
    value_part = jnp.einsum("hqk,qhd->khd", low_weights, cotan_heads.astype(jnp.float32))
    return query_part, key_part, value_part


def head_offsets(head_total, stride):
    return (np.arange(head_total) * stride) // head_total


def select_rows(array_in, stride):
    head_total = array_in.shape[1]
    folded = array_in.reshape((array_in.shape[0] // stride, stride) + array_in.shape[1:])
    return folded[:, head_offsets(head_total, stride), np.arange(head_total)]


def spread_rows(array_in, stride, fill_value):
    head_total = array_in.shape[1]
    chosen = np.arange(stride)[:, None] == head_offsets(head_total, stride)[None, :]
    chosen = chosen.reshape((1, stride, head_total) + (1,) * (array_in.ndim - 2))
    full = jnp.where(chosen, array_in[:, None], fill_value)
    return full.reshape((array_in.shape[0] * stride,) + array_in.shape[1:])


def add_picked(full, addend, stride):
    head_total = full.shape[1]
    folded = full.reshape((full.shape[0] // stride, stride) + full.shape[1:])
    folded = folded.at[:, head_offsets(head_total, stride), np.arange(head_total)].add(addend)
    return folded.reshape(full.shape)


def by_heads(array_in):
    return jnp.moveaxis(array_in, 1, 0)[:, :, None]


def from_heads(array_in):
    return jnp.moveaxis(array_in[:, :, 0], 0, 1)


def reference(query_tiles, key_tiles, value_tiles, cotangent, row_lengths):
    tile_count = query_tiles.shape[0]
    score_scale = HEAD ** -0.5
    head_shape = (tile_count, HEADS, HEAD)
    query_heads = query_tiles.reshape(head_shape)
    key_heads = key_tiles.reshape(head_shape)
    value_heads = value_tiles.reshape(head_shape)
    cotan_heads = cotangent.reshape(head_shape)
    tile_slot = jnp.arange(tile_count, dtype=jnp.int32)
    tile_valid = (tile_slot % ROW) < jnp.repeat(row_lengths, ROW, total_repeat_length=tile_count)
    valid_heads = jnp.broadcast_to(tile_valid[:, None], (tile_count, HEADS))
    block_count = tile_count // TOK_DEV
    group_count = tile_count // GROUP

    def by_blocks(array_in):
        return array_in.reshape((block_count, TOK_DEV) + array_in.shape[1:])

    def by_groups(array_in):
        picked = select_rows(array_in, STRIDE_GROUP)
        return picked.reshape((group_count, picked.shape[0] // group_count) + picked.shape[1:])

    def by_slide(array_in):
        return by_heads(select_rows(array_in, STRIDE_SLIDE))

    def stats_of(members):
        return branch_stats(members[0], members[1], members[2], members[3], score_scale)

    def grads_of(members):
        return branch_grads(members[0], members[1], members[2], members[3], members[4], members[5], members[6], score_scale)

    near_peak, near_total, near_sum = lax.map(stats_of, (by_blocks(query_heads), by_blocks(key_heads), by_blocks(value_heads), by_blocks(valid_heads)))
    near_peak = near_peak.reshape(tile_count, HEADS)
    near_total = near_total.reshape(tile_count, HEADS)
    near_sum = near_sum.reshape(head_shape)
    group_peak, group_total, group_sum = lax.map(stats_of, (by_groups(query_heads), by_groups(key_heads), by_groups(value_heads), by_groups(valid_heads)))
    group_peak = group_peak.reshape(-1, HEADS)
    group_total = group_total.reshape(-1, HEADS)
    group_sum = group_sum.reshape(-1, HEADS, HEAD)
    slide_peak, slide_total, slide_sum = lax.map(stats_of, (by_slide(query_heads), by_slide(key_heads), by_slide(value_heads), by_slide(valid_heads)))
    slide_peak = from_heads(slide_peak)
    slide_total = from_heads(slide_total)
    slide_sum = from_heads(slide_sum)
    group_peak_full = spread_rows(group_peak, STRIDE_GROUP, NEGATIVE_FILL)
    slide_peak_full = spread_rows(slide_peak, STRIDE_SLIDE, NEGATIVE_FILL)
    best_peak = jnp.maximum(jnp.maximum(near_peak, group_peak_full), slide_peak_full)
    near_weight = jnp.exp(near_peak - best_peak)
    group_weight = jnp.exp(group_peak_full - best_peak)
    slide_weight = jnp.exp(slide_peak_full - best_peak)
    denominator = near_total * near_weight + spread_rows(group_total, STRIDE_GROUP, 0.0) * group_weight + spread_rows(slide_total, STRIDE_SLIDE, 0.0) * slide_weight
    numerator = near_sum * near_weight[:, :, None]
    numerator = add_picked(numerator, group_sum * select_rows(group_weight, STRIDE_GROUP)[:, :, None], STRIDE_GROUP)
    numerator = add_picked(numerator, slide_sum * select_rows(slide_weight, STRIDE_SLIDE)[:, :, None], STRIDE_SLIDE)
    attended = (numerator / denominator[:, :, None]).astype(jnp.bfloat16)
    log_norm = best_peak + jnp.log(denominator)
    out_dot = jnp.sum(cotan_heads.astype(jnp.float32) * lax.optimization_barrier(attended).astype(jnp.float32), axis=2)

    near_grads = lax.map(grads_of, (by_blocks(query_heads), by_blocks(key_heads), by_blocks(value_heads), by_blocks(cotan_heads), by_blocks(log_norm), by_blocks(out_dot), by_blocks(valid_heads)))
    query_grad = near_grads[0].reshape(head_shape)
    key_grad = near_grads[1].reshape(head_shape)
    value_grad = near_grads[2].reshape(head_shape)
    group_grads = lax.map(grads_of, (by_groups(query_heads), by_groups(key_heads), by_groups(value_heads), by_groups(cotan_heads), by_groups(log_norm), by_groups(out_dot), by_groups(valid_heads)))
    query_grad = add_picked(query_grad, group_grads[0].reshape(-1, HEADS, HEAD), STRIDE_GROUP)
    key_grad = add_picked(key_grad, group_grads[1].reshape(-1, HEADS, HEAD), STRIDE_GROUP)
    value_grad = add_picked(value_grad, group_grads[2].reshape(-1, HEADS, HEAD), STRIDE_GROUP)
    slide_grads = lax.map(grads_of, (by_slide(query_heads), by_slide(key_heads), by_slide(value_heads), by_slide(cotan_heads), by_slide(log_norm), by_slide(out_dot), by_slide(valid_heads)))
    query_grad = add_picked(query_grad, from_heads(slide_grads[0]), STRIDE_SLIDE)
    key_grad = add_picked(key_grad, from_heads(slide_grads[1]), STRIDE_SLIDE)
    value_grad = add_picked(value_grad, from_heads(slide_grads[2]), STRIDE_SLIDE)
    flat_shape = (tile_count, HEADS * HEAD)
    return (attended.reshape(flat_shape), query_grad.astype(jnp.bfloat16).reshape(flat_shape), key_grad.astype(jnp.bfloat16).reshape(flat_shape), value_grad.astype(jnp.bfloat16).reshape(flat_shape))
```

```python
import jax
import jax.numpy as jnp
import numpy as np
from jax import lax
from jax.experimental import pallas as pl
from jax.experimental.pallas import tpu as pltpu
from jax.sharding import PartitionSpec as P

HEADS = 16
HEAD = 48
ROW = 32
STRIDE_GROUP = 4
STRIDE_SLIDE = 16


NEGATIVE_FILL = -1e30
heads_at_once = 4


def as_sent(value):

    def short(part):
        return part.astype(jnp.bfloat16) if part.dtype == jnp.float32 else part

    return jax.tree.map(short, value)


def head_ranges(head_total):
    step_size = min(head_total, heads_at_once)
    return [(first_head, first_head + step_size) for first_head in range(0, head_total, step_size)]


def scores_of(query_block, key_block, score_scale):
    return (
        jnp.einsum("hdq,hdk->hqk", query_block, key_block, preferred_element_type=jnp.float32)
        * score_scale
    )


def branch_stats(query_heads, key_heads, value_heads, key_valid, score_scale):
    peak_list, total_list, sum_list = ([], [], [])
    for first_head, last_head in head_ranges(query_heads.shape[0]):
        raw_scores = scores_of(
            query_heads[first_head:last_head], key_heads[first_head:last_head], score_scale
        )
        key_keep = key_valid[first_head:last_head][:, None, :]
        masked = jnp.where(key_keep, raw_scores, NEGATIVE_FILL)
        row_peak = jnp.max(masked, axis=2)
        weights = jnp.where(key_keep, jnp.exp(masked - row_peak[:, :, None]), 0.0)
        peak_list.append(row_peak)
        total_list.append(jnp.sum(weights, axis=2))
        sum_list.append(
            jnp.einsum(
                "hqk,hdk->hdq",
                weights.astype(jnp.bfloat16),
                value_heads[first_head:last_head],
                preferred_element_type=jnp.float32,
            )
        )
    return (
        jnp.concatenate(peak_list, axis=0),
        jnp.concatenate(total_list, axis=0),
        jnp.concatenate(sum_list, axis=0),
    )


def branch_grads(
    query_heads,
    key_heads,
    value_heads,
    cotan_heads,
    log_norm,
    out_dot,
    key_valid,
    score_scale,
    want_query,
    want_keys,
):
    query_list, key_list, value_list = ([], [], [])
    for first_head, last_head in head_ranges(query_heads.shape[0]):
        query_block = query_heads[first_head:last_head]
        key_block = key_heads[first_head:last_head]
        cotan_block = cotan_heads[first_head:last_head]
        raw_scores = scores_of(query_block, key_block, score_scale)
        key_keep = key_valid[first_head:last_head][:, None, :]
        weights = jnp.where(
            key_keep, jnp.exp(raw_scores - log_norm[first_head:last_head][:, :, None]), 0.0
        )
        weight_grads = jnp.einsum(
            "hdq,hdk->hqk",
            cotan_block,
            value_heads[first_head:last_head],
            preferred_element_type=jnp.float32,
        )
        low_grads = (weights * (weight_grads - out_dot[first_head:last_head][:, :, None])).astype(
            jnp.bfloat16
        )
        if want_query:
            query_list.append(
                score_scale
                * jnp.einsum(
                    "hqk,hdk->hdq", low_grads, key_block, preferred_element_type=jnp.float32
                )
            )
        if want_keys:
            key_list.append(
                score_scale
                * jnp.einsum(
                    "hqk,hdq->hdk", low_grads, query_block, preferred_element_type=jnp.float32
                )
            )
            value_list.append(
                jnp.einsum(
                    "hqk,hdq->hdk",
                    weights.astype(jnp.bfloat16),
                    cotan_block,
                    preferred_element_type=jnp.float32,
                )
            )
    query_part = jnp.concatenate(query_list, axis=0) if want_query else None
    key_part = jnp.concatenate(key_list, axis=0) if want_keys else None
    value_part = jnp.concatenate(value_list, axis=0) if want_keys else None
    return (query_part, key_part, value_part)


def head_offsets(head_total, stride):
    return np.arange(head_total) * stride // head_total


def select_rows(array_in, stride):
    head_total = array_in.shape[0]
    offsets = head_offsets(head_total, stride)
    folded = array_in.reshape(array_in.shape[:-1] + (array_in.shape[-1] // stride, stride))
    return jnp.stack(
        [folded[head_index, ..., int(offsets[head_index])] for head_index in range(head_total)]
    )


def spread_rows(array_in, stride, fill_value):
    head_total = array_in.shape[0]
    chosen = np.arange(stride)[None, :] == head_offsets(head_total, stride)[:, None]
    chosen = chosen.reshape((head_total,) + (1,) * (array_in.ndim - 1) + (stride,))
    full = jnp.where(chosen, array_in[..., None], fill_value)
    return full.reshape(array_in.shape[:-1] + (array_in.shape[-1] * stride,))


def to_heads(flat_in):
    return jnp.transpose(flat_in.reshape(flat_in.shape[0], HEADS, -1), (1, 2, 0))


def to_flat(heads_in):
    return jnp.transpose(heads_in, (2, 0, 1)).reshape(heads_in.shape[2], -1)


def local(query_tiles, key_tiles, value_tiles, cotangent, row_lengths):
    tile_count = query_tiles.shape[0]
    score_scale = HEAD ** (-0.5)
    query_heads = to_heads(query_tiles)
    key_heads = to_heads(key_tiles)
    value_heads = to_heads(value_tiles)
    cotan_heads = to_heads(cotangent)
    tile_slot = jnp.arange(tile_count, dtype=jnp.int32)
    tile_valid = tile_slot % ROW < jnp.repeat(row_lengths, ROW, total_repeat_length=tile_count)
    valid_heads = jnp.broadcast_to(tile_valid[None, :], (HEADS, tile_count))
    group_query = select_rows(query_heads, STRIDE_GROUP)
    group_key = select_rows(key_heads, STRIDE_GROUP)
    group_value = select_rows(value_heads, STRIDE_GROUP)
    group_cotan = select_rows(cotan_heads, STRIDE_GROUP)
    group_valid = select_rows(valid_heads, STRIDE_GROUP)
    group_flag = group_valid.astype(jnp.bfloat16)[:, None, :]
    slide_query = select_rows(query_heads, STRIDE_SLIDE)
    slide_key = select_rows(key_heads, STRIDE_SLIDE)
    slide_value = select_rows(value_heads, STRIDE_SLIDE)
    slide_flag = select_rows(valid_heads, STRIDE_SLIDE).astype(jnp.bfloat16)[:, None, :]
    owned_query, owned_key, owned_value, owned_flag = (
        lax.all_to_all(slide_query, "outer", split_axis=0, concat_axis=2, tiled=True),
        lax.all_to_all(slide_key, "outer", split_axis=0, concat_axis=2, tiled=True),
        lax.all_to_all(slide_value, "outer", split_axis=0, concat_axis=2, tiled=True),
        lax.all_to_all(slide_flag, "outer", split_axis=0, concat_axis=2, tiled=True),
    )
    got_group = (
        lax.all_gather(group_key, "inner", axis=2, tiled=True),
        lax.all_gather(group_value, "inner", axis=2, tiled=True),
        lax.all_gather(group_flag, "inner", axis=2, tiled=True),
    )
    got_slide = (
        lax.all_gather(owned_key, "inner", axis=2, tiled=True),
        lax.all_gather(owned_value, "inner", axis=2, tiled=True),
        lax.all_gather(owned_flag, "inner", axis=2, tiled=True),
    )
    near_peak, near_total, near_sum = branch_stats(
        query_heads, key_heads, value_heads, valid_heads, score_scale
    )
    remote_group_key = got_group[0]
    remote_group_value = got_group[1]
    remote_group_valid = got_group[2][:, 0, :] > 0.5
    group_peak, group_total, group_sum = branch_stats(
        group_query, remote_group_key, remote_group_value, remote_group_valid, score_scale
    )
    slide_all_key = got_slide[0]
    slide_all_value = got_slide[1]
    slide_all_valid = got_slide[2][:, 0, :] > 0.5
    owner_peak, owner_total, owner_sum = branch_stats(
        owned_query, slide_all_key, slide_all_value, slide_all_valid, score_scale
    )
    slide_peak, slide_total, slide_sum = (
        lax.all_to_all(owner_peak[:, None, :], "outer", split_axis=2, concat_axis=0, tiled=True),
        lax.all_to_all(owner_total[:, None, :], "outer", split_axis=2, concat_axis=0, tiled=True),
        lax.all_to_all(owner_sum, "outer", split_axis=2, concat_axis=0, tiled=True),
    )
    slide_peak = slide_peak[:, 0, :]
    slide_total = slide_total[:, 0, :]
    group_peak_full = spread_rows(group_peak, STRIDE_GROUP, NEGATIVE_FILL)
    slide_peak_full = spread_rows(slide_peak, STRIDE_SLIDE, NEGATIVE_FILL)
    best_peak = jnp.maximum(jnp.maximum(near_peak, group_peak_full), slide_peak_full)
    near_weight = jnp.exp(near_peak - best_peak)
    group_weight = jnp.exp(group_peak_full - best_peak)
    slide_weight = jnp.exp(slide_peak_full - best_peak)
    denominator = (
        near_total * near_weight
        + spread_rows(group_total, STRIDE_GROUP, 0.0) * group_weight
        + spread_rows(slide_total, STRIDE_SLIDE, 0.0) * slide_weight
    )
    numerator = (
        near_sum * near_weight[:, None, :]
        + spread_rows(group_sum, STRIDE_GROUP, 0.0) * group_weight[:, None, :]
        + spread_rows(slide_sum, STRIDE_SLIDE, 0.0) * slide_weight[:, None, :]
    )
    attended = (numerator / denominator[:, None, :]).astype(jnp.bfloat16)
    log_norm = best_peak + jnp.log(denominator)
    out_dot = jnp.sum(cotan_heads.astype(jnp.float32) * attended.astype(jnp.float32), axis=1)
    near_query, near_key, near_value = branch_grads(
        query_heads,
        key_heads,
        value_heads,
        cotan_heads,
        log_norm,
        out_dot,
        valid_heads,
        score_scale,
        True,
        True,
    )
    group_lse = select_rows(log_norm, STRIDE_GROUP)
    group_dot = select_rows(out_dot, STRIDE_GROUP)
    group_query_grad = branch_grads(
        group_query,
        remote_group_key,
        remote_group_value,
        group_cotan,
        group_lse,
        group_dot,
        remote_group_valid,
        score_scale,
        True,
        False,
    )[0]
    got_group_rows = (
        lax.all_gather(group_query, "inner", axis=2, tiled=True),
        lax.all_gather(group_cotan, "inner", axis=2, tiled=True),
    )
    got_group_stats = (
        lax.all_gather(group_lse, "inner", axis=1, tiled=True),
        lax.all_gather(group_dot, "inner", axis=1, tiled=True),
    )
    unused_group, group_key_grad, group_value_grad = branch_grads(
        got_group_rows[0],
        group_key,
        group_value,
        got_group_rows[1],
        got_group_stats[0],
        got_group_stats[1],
        group_valid,
        score_scale,
        False,
        True,
    )
    slide_cotan = select_rows(cotan_heads, STRIDE_SLIDE)
    slide_lse = select_rows(log_norm, STRIDE_SLIDE)
    slide_dot = select_rows(out_dot, STRIDE_SLIDE)
    owned_cotan = lax.all_to_all(slide_cotan, "outer", split_axis=0, concat_axis=2, tiled=True)
    owned_lse, owned_dot = (
        lax.all_to_all(slide_lse, "outer", split_axis=0, concat_axis=1, tiled=True),
        lax.all_to_all(slide_dot, "outer", split_axis=0, concat_axis=1, tiled=True),
    )
    owned_query_grad, partial_key, partial_value = branch_grads(
        owned_query,
        slide_all_key,
        slide_all_value,
        owned_cotan,
        owned_lse,
        owned_dot,
        slide_all_valid,
        score_scale,
        True,
        True,
    )
    owned_key_grad, owned_value_grad = (
        lax.psum_scatter(
            partial_key.astype(jnp.bfloat16), "inner", scatter_dimension=2, tiled=True
        ).astype(jnp.float32),
        lax.psum_scatter(
            partial_value.astype(jnp.bfloat16), "inner", scatter_dimension=2, tiled=True
        ).astype(jnp.float32),
    )
    slide_query_grad, slide_key_grad, slide_value_grad = (
        lax.all_to_all(
            as_sent(owned_query_grad), "outer", split_axis=2, concat_axis=0, tiled=True
        ).astype(owned_query_grad.dtype),
        lax.all_to_all(
            owned_key_grad.astype(jnp.bfloat16), "outer", split_axis=2, concat_axis=0, tiled=True
        ).astype(owned_key_grad.dtype),
        lax.all_to_all(
            owned_value_grad.astype(jnp.bfloat16), "outer", split_axis=2, concat_axis=0, tiled=True
        ).astype(owned_value_grad.dtype),
    )
    query_grad = (
        near_query
        + spread_rows(group_query_grad, STRIDE_GROUP, 0.0)
        + spread_rows(slide_query_grad, STRIDE_SLIDE, 0.0)
    )
    key_grad = (
        near_key
        + spread_rows(group_key_grad, STRIDE_GROUP, 0.0)
        + spread_rows(slide_key_grad, STRIDE_SLIDE, 0.0)
    )
    value_grad = (
        near_value
        + spread_rows(group_value_grad, STRIDE_GROUP, 0.0)
        + spread_rows(slide_value_grad, STRIDE_SLIDE, 0.0)
    )
    return (
        to_flat(attended),
        to_flat(query_grad.astype(jnp.bfloat16)),
        to_flat(key_grad.astype(jnp.bfloat16)),
        to_flat(value_grad.astype(jnp.bfloat16)),
    )


BF = jnp.bfloat16
F32 = jnp.float32
LANES = 128
SCALE = HEAD ** (-0.5)
PAIR = 2 * HEAD
PAIRS = HEADS // 2
MESH = pl.DeviceIdType.MESH


def iota2(shape, axis):
    return lax.broadcasted_iota(jnp.int32, shape, axis)


def original_tile(j):
    return (j & 7) * 16 + ((j >> 3) & 3) * 4 + (j >> 5)


def permute_matrix(inverse):
    shape = (LANES, LANES)
    j, i = (iota2(shape, 1), iota2(shape, 0)) if inverse else (iota2(shape, 0), iota2(shape, 1))
    return (original_tile(j) == i).astype(F32).astype(BF)


def identity(size):
    shape = (size, size)
    return (iota2(shape, 0) == iota2(shape, 1)).astype(F32).astype(BF)


def key_bias(len_ref):
    tile = original_tile(iota2((LANES, LANES), 0))
    row = tile >> 5
    length = jnp.full((LANES, LANES), len_ref[0], jnp.int32)
    for index in range(1, 4):
        length = jnp.where(row == index, len_ref[index], length)
    return jnp.where((tile & 31) < length, 0.0, NEGATIVE_FILL).astype(F32)


def mm(a, b):
    return jnp.dot(a, b, preferred_element_type=F32)


def mm_t(a, b):
    return lax.dot_general(a, b, (((1,), (1,)), ((), ())), preferred_element_type=F32)


def slide_row(r):
    return (r % 4) * 32 + (r // 4) * 8


def head_lanes(lane, p, e):
    return ((lane - (PAIR * p + HEAD * e)) & (LANES - 1)) < HEAD


def flag_lane(p):
    return (PAIR * (p + 1)) & (LANES - 1)


def as_mask(keep):
    return keep.astype(F32).astype(BF)


def head_masks(p):
    lane = iota2((1, LANES), 1)
    masks = [as_mask(head_lanes(lane, p, e)) for e in range(2)]
    flags = [as_mask(lane == flag_lane(p) + e) for e in range(2)]
    return masks, flags


def two_heads(x, masks, flags=None):
    parts = [x * masks[e] for e in range(2)]
    if flags is not None:
        parts = [parts[e] + flags[e] for e in range(2)]
    return jnp.concatenate(parts, axis=0)


def pieces_of(p):
    base, spot = p // 4 * 3, p % 4
    if spot == 0:
        return [(base, 0, 96)]
    if spot == 1:
        return [(base, 96, 128), (base + 1, 0, 64)]
    if spot == 2:
        return [(base + 1, 64, 128), (base + 2, 0, 32)]
    return [(base + 2, 32, 128)]


def pair_tile(x, p):
    parts = pieces_of(p)
    tiles = [x[:, t * LANES : (t + 1) * LANES] for t, _, _ in parts]
    if len(tiles) == 1:
        return tiles[0]
    lane = iota2(tiles[0].shape, 1)
    return jnp.where(lane >= parts[0][1], tiles[0], tiles[1])


K_ROW, Q_ROW, V_ROW, S_ROW, C_ROW, G_ROWS = 0, 32, 64, 96, 112, 144


def prep_pair(x, p, bias=None):
    tile = pair_tile(x, p)
    lane = iota2(tile.shape, 1)
    flag = flag_lane(p)
    if bias is not None:
        tile = jnp.where((lane == flag) | (lane == flag + 1), bias, tile)
    first, second = [tile[slide_row(2 * p + e) :][:8] for e in range(2)]
    lane = iota2(first.shape, 1)
    slide = jnp.where(head_lanes(lane, p, 1) | (lane == flag + 1), second, first)
    return tile, slide


def near_early(p, tp_ref, pn_ref, ad_ref, kt_ref, vt_ref, eye):
    k, q, v, c = [tp_ref[a, p] for a in range(4)]
    masks, flags = head_masks(p)
    s = mm_t(k, two_heads(q, masks, flags)) * SCALE
    dp = mm_t(v, two_heads(c, masks))
    kt_ref[p] = mm_t(eye, two_heads(k, masks)).astype(BF)
    vt_ref[p] = mm_t(eye, two_heads(v, masks)).astype(BF)
    peak = jnp.max(s, axis=0, keepdims=True)
    weights = jnp.exp(s - peak)
    total = jnp.sum(weights, axis=0, keepdims=True)
    weights = weights * (1.0 / total)
    delta = jnp.sum(weights * dp, axis=0, keepdims=True)
    pn_ref[p] = weights
    ad_ref[p] = weights * (dp - delta)
    return peak + jnp.log(total), delta


def turn(x, shift):
    return pltpu.roll(x, shift & (LANES - 1), 1)


def near_stats(p, me, lse, delta):
    shape = (8, LANES)
    row, lane = iota2(shape, 0), iota2(shape, 1)

    def wide(x, e):
        return jnp.broadcast_to(x[:, e * LANES : (e + 1) * LANES], shape)

    high = row < 4
    heads = [jnp.where(high, wide(lse, e), wide(delta, e)) for e in range(2)]
    group = turn(jnp.where((row & 3) == 0, heads[0], heads[1]), ((me & 3) - p // 2) * 32)
    spots = [turn(heads[e], e * 64 + me * 8 - slide_row(2 * p + e)) for e in range(2)]
    slide = jnp.where(lane < 64, spots[0], spots[1])
    return jnp.where((row & 3) == 2, slide, group)


def near_late(p, me, r2_ref, tp_ref, pn_ref, ad_ref, kt_ref, vt_ref, late_ref, turned_ref):
    tile = r2_ref[p]
    lane = iota2((1, LANES), 1)
    start = p // 2 * 32
    group = turn(tile, start - (me & 3) * 32)
    in_group = (lane >= start) & (lane < start + 32)
    scales, shifts = [], []
    for e in range(2):
        at = slide_row(2 * p + e)
        slide = turn(tile, at - e * 64 - me * 8)
        in_slide = (lane >= at) & (lane < at + 8)
        for index, (found, fill) in enumerate(((scales, 1.0), (shifts, 0.0))):
            value = jnp.where(in_slide, slide[4 * index + 2 : 4 * index + 3], fill)
            found.append(jnp.where(in_group, group[4 * index + e : 4 * index + e + 1], value))
    scale = jnp.concatenate(scales, axis=1)
    shift = jnp.concatenate(shifts, axis=1)
    weights = pn_ref[p]
    low = (weights * scale).astype(BF)
    grads = (ad_ref[p] * (scale * SCALE) - weights * (scale * shift * SCALE)).astype(BF)
    masks, _ = head_masks(p)
    late_ref[0, p] = mm(grads, two_heads(tp_ref[1, p], masks))
    late_ref[1, p] = mm(low, two_heads(tp_ref[3, p], masks))

    def stacked(x):
        return jnp.concatenate([x[:, :LANES], x[:, LANES:]], axis=0)

    for index, value in enumerate((mm(vt_ref[p], stacked(low)), mm(kt_ref[p], stacked(grads)))):
        value = value.astype(BF)
        for t, first, last in pieces_of(p):
            turned_ref[index, t * LANES + first : t * LANES + last] = value[first:last]


def branch(s, dp):
    peak = jnp.max(s, axis=0, keepdims=True)
    weights = jnp.exp(s - peak)
    total = jnp.sum(weights, axis=0, keepdims=True)
    delta = jnp.sum(weights * dp, axis=0, keepdims=True) / total
    return weights, peak, peak + jnp.log(total), delta


def rows_of(row, first, second, third):
    first, second, third = [jnp.broadcast_to(x, row.shape) for x in (first, second, third)]
    return jnp.where(row == 0, first, jnp.where(row == 1, second, third))


def slide_scores(masks, flags, gr_ref, skv_ref):
    kv = skv_ref[...].reshape(-1, LANES)
    sources = gr_ref.shape[0]
    wide = gr_ref[:, S_ROW:C_ROW].astype(F32)
    q, c = [wide[:, a : a + 8].reshape(sources * 8, LANES).astype(BF) for a in (0, 8)]
    q2, c2 = two_heads(q, masks, flags), two_heads(c, masks)
    both = mm_t(kv, jnp.concatenate([q2, c2], axis=0)).reshape(-1, 16, 2 * LANES)
    s = both[:, 0:8, :LANES].reshape(-1, LANES) * SCALE
    dp = both[:, 8:16, LANES:].reshape(-1, LANES)
    return kv, q2, c2, s, dp


def near_of(row, lane, ns_ref):
    slide = ns_ref[0]
    for source in range(1, 8):
        slide = jnp.where(((lane & 63) >> 3) == source, ns_ref[source], slide)
    found = []
    for j in range(2):
        group = ns_ref[4 * j]
        for q in range(1, 4):
            group = jnp.where((lane >> 5) == q, ns_ref[4 * j + q], group)
        both = jnp.where((row & 3) == 2, slide, group)
        found.append((both, pltpu.roll(both, 4, 0)))
    return found


def crossed(row, lane, p, slide, group):
    first = lax.rem(2 * p, 5) == 0
    second = lax.rem(2 * p + 1, 5) == 0
    e = jnp.where(second, 1, 0)
    any_head = jnp.logical_or(first, second)
    at = p // 2 * 8
    source = jnp.where(row < 4, *slide)
    found, to_slide = [], None
    for j in range(2):
        pair = [jnp.where(row < 4, *group[2 * head + j]) for head in range(2)]
        chosen = jnp.where(second, pair[1], pair[0])
        to_group = None
        for q in range(4):
            here, there = q * 32 + at, (4 * j + q) * 8 + e * 64
            moved = turn(source, here - there + LANES)
            to_group = moved if q == 0 else jnp.where((lane >> 5) == q, moved, to_group)
            moved = turn(chosen, there - here + LANES)
            same = ((lane & 63) >> 3) == 4 * j + q
            to_slide = moved if to_slide is None else jnp.where(same, moved, to_slide)
        found.append(to_group)
    edge = row & 3
    in_group = (edge == e) & ((lane & 31) >> 3 == p // 2) & any_head
    in_slide = (edge == 2) & ((lane >> 6) == e) & any_head
    results = []
    for to_group in found:
        both = jnp.where(edge == 2, to_slide, to_group)
        both = jnp.where(in_group | in_slide, both, jnp.where(row < 4, NEGATIVE_FILL, 0.0))
        results.append((both, pltpu.roll(both, 4, 0)))
    return results


class Exchange:
    def __init__(self, count, make):
        self.count, self.make = count, make

    def start(self):
        @pl.loop(1, self.count)
        def _(step):
            self.make(step).start()

    def wait_recv(self):
        @pl.loop(1, self.count)
        def _(step):
            self.make(step).wait_recv()

    def wait_send(self):
        @pl.loop(1, self.count)
        def _(step):
            self.make(step).wait_send()


def wrapped(value, count):
    return jnp.where(value >= count, value - count, value)


def whole_kernel(
    inner, outers, len_hbm, q_hbm, k_hbm, v_hbm, c_hbm, att_ref, dq_ref, dk_ref, dv_ref,
    len_ref, loaded, load_sem, tp, gm, gr, skv_s, skv, pn, ad, kt, vt, ns_s, ns_r, r2_s, r2_r,
    r4_s, r4_r, xs, xr, sg_s, sg_r, late, turned, acc, send_sem, recv_sem, x_send, x_recv,
):
    outer, me = lax.axis_index("outer"), lax.axis_index("inner")
    p = me

    def scope(name):
        return jax.named_scope(name)

    def exchange(index, source, target):
        def make(step):
            peer = wrapped(me + step, inner)
            return pltpu.make_async_remote_copy(
                src_ref=source(peer),
                dst_ref=target(me),
                send_sem=send_sem.at[index, step],
                recv_sem=recv_sem.at[index, step],
                device_id=(outer, peer),
                device_id_type=MESH,
            )

        return Exchange(inner, make)

    def across(index, source, target):
        def make(step):
            peer = wrapped(outer + step, outers)
            return pltpu.make_async_remote_copy(
                src_ref=source(peer),
                dst_ref=target,
                send_sem=x_send.at[index, step],
                recv_sem=x_recv.at[index, step],
                device_id=(peer, me),
                device_id_type=MESH,
            )

        return Exchange(outers, make)

    def rows_exchange(index, src, dst, first, last):
        rows = pl.ds(first, last - first)
        return exchange(index, lambda peer: src.at[peer, rows], lambda mine: dst.at[mine, rows])

    send_skv = exchange(0, lambda peer: skv_s.at[peer], lambda mine: skv.at[outer, mine])
    send_k = rows_exchange(1, gm, gr, K_ROW, Q_ROW)
    send_qv = rows_exchange(2, gm, gr, Q_ROW, S_ROW)
    send_c = rows_exchange(3, gm, gr, S_ROW, G_ROWS)
    send_ns = [exchange(4, lambda peer: ns_s.at[peer], lambda mine: ns_r.at[mine])]
    send_r2 = exchange(5, lambda peer: r2_s.at[peer >> 2], lambda mine: r2_r.at[mine])
    send_oq = rows_exchange(6, r4_s, r4_r, 0, 80)
    send_kv = rows_exchange(7, r4_s, r4_r, 80, G_ROWS)
    send_sg = exchange(8, lambda peer: sg_s.at[peer], lambda mine: sg_r.at[mine])
    forward = across(0, lambda peer: skv.at[outer], skv.at[outer])
    backward = across(1, lambda peer: xs.at[peer], xr.at[outer])

    barrier = pltpu.get_barrier_semaphore()
    with scope("load_start"):
        loads = [
            pltpu.make_async_copy(ref, loaded.at[a], load_sem.at[a])
            for a, ref in enumerate((k_hbm, q_hbm, v_hbm, c_hbm))
        ]
        loads.append(pltpu.make_async_copy(len_hbm, len_ref, load_sem.at[4]))
        for index in (4, 0, 2, 1, 3):
            loads[index].start()
    with scope("greet"):

        @pl.loop(1, inner)
        def _(step):
            pl.semaphore_signal(
                barrier, inc=1, device_id=(outer, wrapped(me + step, inner)), device_id_type=MESH
            )

        @pl.loop(1, outers)
        def _(step):
            pl.semaphore_signal(
                barrier, inc=1, device_id=(wrapped(outer + step, outers), me), device_id_type=MESH
            )

    perm = permute_matrix(False)
    eye = identity(LANES)
    with scope("load_wait"):
        loads[4].wait()
        loads[0].wait()
        loads[2].wait()
    with scope("prep_kv"):
        bias = key_bias(len_ref)
        xk = mm(perm, loaded[0])
        xv = mm(perm, loaded[2])
        for h in range(PAIRS):
            rows = slice(h // 2 * 32, h // 2 * 32 + 32)
            tile, key_slide = prep_pair(xk, h, bias)
            tp[0, h] = tile.astype(BF)
            gm[h, K_ROW:Q_ROW] = tile[rows].astype(BF)
            tile, value_slide = prep_pair(xv, h)
            tp[2, h] = tile.astype(BF)
            gm[h, V_ROW:S_ROW] = tile[rows].astype(BF)
            skv_s[h] = jnp.concatenate([key_slide, value_slide], axis=0).astype(BF)
    with scope("barrier_wait"):
        pl.semaphore_wait(barrier, inner - 1 + outers - 1)
    with scope("send_kv"):
        send_skv.start()
        send_k.start()
        skv[outer, me] = skv_s[me]
    with scope("prep_qc"):
        loads[1].wait()
        loads[3].wait()
        xq = mm(perm, loaded[1])
        xc = mm(perm, loaded[3])
        for h in range(PAIRS):
            rows = slice(h // 2 * 32, h // 2 * 32 + 32)
            tile, query_slide = prep_pair(xq, h)
            tp[1, h] = tile.astype(BF)
            gm[h, Q_ROW:V_ROW] = tile[rows].astype(BF)
            tile, cotan_slide = prep_pair(xc, h)
            tp[3, h] = tile.astype(BF)
            gm[h, C_ROW:G_ROWS] = tile[rows].astype(BF)
            gm[h, S_ROW:C_ROW] = jnp.concatenate([query_slide, cotan_slide], axis=0).astype(BF)
    with scope("send_qc"):
        send_qv.start()
        send_c.start()
        gr[me] = gm[me]

    def early(h):
        lse, delta = near_early(h, tp, pn, ad, kt, vt, eye)
        ns_s[h] = near_stats(h, me, lse, delta)

    with scope("near_early"):
        for h in range(PAIRS):
            early(h)
    with scope("send_ns"):
        send_ns[0].start()
        ns_r[me] = ns_s[me]
    with scope("skv_wait"):
        send_skv.wait_recv()
    with scope("forward"):
        forward.start()
    masks, flags = head_masks(p)
    row, lane = iota2((8, LANES), 0), iota2((8, LANES), 1)
    with scope("group_wait"):
        send_k.wait_recv()
        send_qv.wait_recv()
        send_c.wait_recv()
    with scope("group_scores"):
        k, q, v, c = [
            gr[:, at : at + 32].reshape(inner * 32, LANES) for at in (K_ROW, Q_ROW, V_ROW, C_ROW)
        ]
        q2, c2 = two_heads(q, masks, flags), two_heads(c, masks)
        chunks = []
        for index in range(4):
            part = slice(index * LANES, (index + 1) * LANES)
            dp = mm_t(v, c2[part])
            chunks.append(branch(mm_t(k, q2[part]) * SCALE, dp) + (dp,))
        kt2 = mm_t(eye, two_heads(k, masks)).astype(BF)
        vt2 = mm_t(eye, two_heads(v, masks)).astype(BF)
    with scope("forward_wait"):
        forward.wait_recv()
    with scope("slide_scores"):
        skv_all, qs2, cs2, s, slide_dp = slide_scores(masks, flags, gr, skv)
        slide_weights, slide_peak, slide_lse, slide_delta = branch(s, slide_dp)
        skv_t = mm_t(eye, skv_all).astype(BF)
    with scope("ns_wait"):
        send_ns[0].wait_recv()
    with scope("merge"):
        near = near_of(row, lane, ns_r)
        other = crossed(
            row,
            lane,
            p,
            [jnp.broadcast_to(x, row.shape) for x in (slide_lse, slide_delta)],
            [[jnp.broadcast_to(x, row.shape) for x in chunk[2:4]] for chunk in chunks],
        )
        factors, deltas = [], []
        for j in range(2):
            own = [
                rows_of(row, chunks[j][i], chunks[2 + j][i], last)
                for i, last in ((1, slide_peak), (2, slide_lse), (3, slide_delta))
            ]
            best = jnp.maximum(jnp.maximum(near[j][0], own[1]), other[j][0])
            parts = [jnp.exp(x - best) for x in (near[j][0], own[1], other[j][0])]
            total = parts[0] + parts[1] + parts[2]
            inverse = 1.0 / total
            lse = best + jnp.log(total)
            delta = (parts[0] * near[j][1] + parts[1] * own[2] + parts[2] * other[j][1]) * inverse
            factors.append(jnp.exp(own[0] - lse))
            deltas.append(delta)
            r2_s[j] = jnp.where(row < 4, parts[0] * inverse, pltpu.roll(delta - near[j][1], 4, 0))
    with scope("send_r2"):
        send_r2.start()
        r2_r[me] = r2_s[me >> 2]
    with scope("slide_bwd"):
        weights = slide_weights * factors[0][2:3]
        grads = weights * (slide_dp - deltas[0][2:3]) * SCALE
        blocks = [x.reshape(-1, 8, LANES) for x in (grads, weights)]
        empty = jnp.zeros_like(blocks[0])
        mixed = jnp.concatenate(
            [
                jnp.concatenate([blocks[0], empty], axis=2),
                jnp.concatenate([empty, blocks[1]], axis=2),
            ],
            axis=1,
        )
        mixed = mixed.reshape(-1, 2 * LANES).astype(BF)
        xs[...] = mm(mixed, jnp.concatenate([qs2, cs2], axis=0)).astype(BF).reshape(xs.shape)
    with scope("send_x"):
        backward.start()
    with scope("slide_q"):
        both = mm_t(identity(2 * LANES), mm(skv_t, mixed).astype(BF))
        quarter = LANES // 2
        head0 = head_lanes(iota2((quarter, LANES), 1), p, 0)
        query = jnp.where(head0, both[0:quarter], both[quarter:LANES])
        out = jnp.where(head0, both[LANES : 3 * quarter], both[3 * quarter : 4 * quarter])
        blocks = [x.reshape(inner, 8, LANES) for x in (out, query)]
        r4_s[:, 64:80] = jnp.concatenate(blocks, axis=1).astype(BF)
    with scope("group_bwd_q"):
        lows, grads = [], []
        for index, (weights, _, _, _, dp) in enumerate(chunks):
            e, j = divmod(index, 2)
            weights = weights * factors[j][e : e + 1]
            lows.append(weights.astype(BF))
            grads.append((weights * (dp - deltas[j][e : e + 1]) * SCALE).astype(BF))
        for j in range(2):
            for at, wide, parts in ((0, vt2, lows), (32, kt2, grads)):
                value = mm(wide, jnp.concatenate([parts[j], parts[2 + j]], axis=0)).astype(BF)
                value = mm_t(eye, value).astype(BF)
                r4_s[4 * j : 4 * j + 4, at : at + 32] = value.reshape(4, 32, LANES)
    with scope("send_oq"):
        send_oq.start()
    with scope("group_bwd_kv"):
        for at, parts, rows in ((80, grads, q2), (112, lows, c2)):
            value = mm(jnp.concatenate(parts, axis=1), rows).astype(BF)
            r4_s[:, at : at + 32] = value.reshape(inner, 32, LANES)
    with scope("send_kv"):
        send_kv.start()
        r4_r[me] = r4_s[me]
    with scope("r2_wait"):
        send_r2.wait_recv()
    with scope("near_late0"):
        for h in range(PAIRS // 2):
            near_late(h, me, r2_r, tp, pn, ad, kt, vt, late, turned)
    with scope("x_wait"):
        backward.wait_recv()
    with scope("x_sum"):
        total = xs[outer].astype(F32)
        for step in range(1, outers):
            total = total + xr[wrapped(outer + step, outers)].astype(F32)
        sg_s[...] = total.astype(BF)
    with scope("send_sg"):
        send_sg.start()
        sg_r[me] = sg_s[me]
    with scope("near_late1"):
        for h in range(PAIRS // 2, PAIRS):
            near_late(h, me, r2_r, tp, pn, ad, kt, vt, late, turned)
    with scope("collect"):
        acc[0:2] = jnp.zeros((2,) + acc.shape[1:], F32)
        for a in range(2):
            for t in range(D_TILES):
                value = None
                for h in range(PAIRS):
                    for tile, first, last in pieces_of(h):
                        if tile == t:
                            piece = late[a, h]
                            lane_full = iota2(piece.shape, 1)
                            value = piece if value is None else jnp.where(lane_full >= first, piece, value)
                acc[2 + a, :, t * LANES : (t + 1) * LANES] = value
    with scope("drain"):
        for sent in (send_skv, send_k, send_qv, send_c, send_ns[0], forward, send_r2, backward):
            sent.wait_send()
    with scope("oq_wait"):
        send_oq.wait_recv()
    with scope("add_oq"):
        for h in range(PAIRS):
            add_block(acc, (0, 1), h, r4_r[h, 0:64], r4_r[h, 64:80])
    with scope("kv_wait"):
        send_kv.wait_recv()
        send_sg.wait_recv()
    with scope("add_kv"):
        for h in range(PAIRS):
            add_block(acc, (2, 3), h, r4_r[h, 80:G_ROWS], sg_r[h])
    with scope("final"):
        back = permute_matrix(True)
        for a, ref in enumerate((att_ref, dq_ref, dk_ref, dv_ref)):
            value = mm(back, acc[a].astype(BF))
            if a < 2:
                value = value + mm_t(back, turned[a])
            ref[...] = value.astype(BF)
    with scope("drain_last"):
        for sent in (send_oq, send_kv, send_sg):
            sent.wait_send()


D_TILES = HEADS * HEAD // LANES


def add_block(acc, outs, h, group, slide):
    group, slide = group.astype(F32), slide.astype(F32)
    start = h // 2 * 32
    lane = iota2((32, LANES), 1)
    lane8 = iota2((8, LANES), 1)
    for index, a in enumerate(outs):
        block = group[32 * index : 32 * index + 32]
        small = slide[8 * index : 8 * index + 8]
        for t, first, last in pieces_of(h):
            cols = slice(t * LANES, (t + 1) * LANES)
            keep = (lane >= first) & (lane < last)
            acc[a, start : start + 32, cols] += jnp.where(keep, block, 0.0)
            for e in range(2):
                at = slide_row(2 * h + e)
                keep8 = (lane8 >= first) & (lane8 < last) & head_lanes(lane8, h, e)
                acc[a, at : at + 8, cols] += jnp.where(keep8, small, 0.0)


def fast_local(inner, outers, *args):
    row_lengths, tiles_in = args[4], args[:4]
    tiles, width = tiles_in[0].shape
    vmem = pl.BlockSpec(memory_space=pltpu.VMEM)
    anywhere = pl.BlockSpec(memory_space=pl.ANY)

    def both(shape, dtype):
        return [pltpu.VMEM(shape, dtype)] * 2

    scratch = [
        pltpu.SMEM(row_lengths.shape, jnp.int32),
        pltpu.VMEM((4, tiles, width), BF),
        pltpu.SemaphoreType.DMA((5,)),
        pltpu.VMEM((4, PAIRS, tiles, LANES), BF),
    ]
    scratch += both((inner, G_ROWS, LANES), BF)
    scratch += [pltpu.VMEM((inner, 16, LANES), BF), pltpu.VMEM((outers, inner, 16, LANES), BF)]
    scratch += both((PAIRS, tiles, 2 * LANES), F32)
    scratch += both((PAIRS, LANES, 2 * LANES), BF)
    scratch += both((inner, 8, LANES), F32)
    scratch += [pltpu.VMEM((2, 8, LANES), F32), pltpu.VMEM((inner, 8, LANES), F32)]
    scratch += both((inner, G_ROWS, LANES), BF)
    scratch += both((outers, inner, 16, LANES), BF)
    scratch += both((inner, 16, LANES), BF)
    scratch += [
        pltpu.VMEM((2, PAIRS, tiles, LANES), F32),
        pltpu.VMEM((2, width, tiles), BF),
        pltpu.VMEM((4, tiles, width), F32),
    ]
    scratch += [pltpu.SemaphoreType.DMA((9, inner))] * 2 + [pltpu.SemaphoreType.DMA((2, outers))] * 2
    return tuple(
        pl.pallas_call(
            lambda *refs: whole_kernel(inner, outers, *refs),
            out_shape=[jax.ShapeDtypeStruct((tiles, width), BF)] * 4,
            in_specs=[anywhere] * 5,
            out_specs=[vmem] * 4,
            scratch_shapes=scratch,
            compiler_params=pltpu.CompilerParams(
                collective_id=0, has_side_effects=True, vmem_limit_bytes=60 * 1024 * 1024
            ),
        )(row_lengths, *tiles_in)
    )


def solution(mesh):
    in_specs = (P(("outer", "inner"), None),) * 4 + (P(("outer", "inner")),)
    out_specs = (P(("outer", "inner"), None),) * 4
    inner, outers = mesh.shape["inner"], mesh.shape["outer"]

    def step(*args):
        fits = inner == PAIRS and outers == 4
        if fits and args[0].shape == (LANES, HEADS * HEAD):
            return fast_local(inner, outers, *args)
        return local(*args)

    return jax.shard_map(step, mesh=mesh, in_specs=in_specs, out_specs=out_specs, check_vma=False)
```

```python
import jax
import jax.numpy as jnp
import numpy as np
from jax import lax
from jax.experimental import pallas as pl
from jax.experimental.pallas import tpu as pltpu
from jax.sharding import PartitionSpec as P

HEADS = 16
HEAD = 48
ROW = 32
STRIDE_GROUP = 4
STRIDE_SLIDE = 16


NEGATIVE_FILL = -1e30
heads_at_once = 4


def as_sent(value):

    def short(part):
        return part.astype(jnp.bfloat16) if part.dtype == jnp.float32 else part

    return jax.tree.map(short, value)


def head_ranges(head_total):
    step_size = min(head_total, heads_at_once)
    return [(first_head, first_head + step_size) for first_head in range(0, head_total, step_size)]


def scores_of(query_block, key_block, score_scale):
    return (
        jnp.einsum("hdq,hdk->hqk", query_block, key_block, preferred_element_type=jnp.float32)
        * score_scale
    )


def branch_stats(query_heads, key_heads, value_heads, key_valid, score_scale):
    peak_list, total_list, sum_list = ([], [], [])
    for first_head, last_head in head_ranges(query_heads.shape[0]):
        raw_scores = scores_of(
            query_heads[first_head:last_head], key_heads[first_head:last_head], score_scale
        )
        key_keep = key_valid[first_head:last_head][:, None, :]
        masked = jnp.where(key_keep, raw_scores, NEGATIVE_FILL)
        row_peak = jnp.max(masked, axis=2)
        weights = jnp.where(key_keep, jnp.exp(masked - row_peak[:, :, None]), 0.0)
        peak_list.append(row_peak)
        total_list.append(jnp.sum(weights, axis=2))
        sum_list.append(
            jnp.einsum(
                "hqk,hdk->hdq",
                weights.astype(jnp.bfloat16),
                value_heads[first_head:last_head],
                preferred_element_type=jnp.float32,
            )
        )
    return (
        jnp.concatenate(peak_list, axis=0),
        jnp.concatenate(total_list, axis=0),
        jnp.concatenate(sum_list, axis=0),
    )


def branch_grads(
    query_heads,
    key_heads,
    value_heads,
    cotan_heads,
    log_norm,
    out_dot,
    key_valid,
    score_scale,
    want_query,
    want_keys,
):
    query_list, key_list, value_list = ([], [], [])
    for first_head, last_head in head_ranges(query_heads.shape[0]):
        query_block = query_heads[first_head:last_head]
        key_block = key_heads[first_head:last_head]
        cotan_block = cotan_heads[first_head:last_head]
        raw_scores = scores_of(query_block, key_block, score_scale)
        key_keep = key_valid[first_head:last_head][:, None, :]
        weights = jnp.where(
            key_keep, jnp.exp(raw_scores - log_norm[first_head:last_head][:, :, None]), 0.0
        )
        weight_grads = jnp.einsum(
            "hdq,hdk->hqk",
            cotan_block,
            value_heads[first_head:last_head],
            preferred_element_type=jnp.float32,
        )
        low_grads = (weights * (weight_grads - out_dot[first_head:last_head][:, :, None])).astype(
            jnp.bfloat16
        )
        if want_query:
            query_list.append(
                score_scale
                * jnp.einsum(
                    "hqk,hdk->hdq", low_grads, key_block, preferred_element_type=jnp.float32
                )
            )
        if want_keys:
            key_list.append(
                score_scale
                * jnp.einsum(
                    "hqk,hdq->hdk", low_grads, query_block, preferred_element_type=jnp.float32
                )
            )
            value_list.append(
                jnp.einsum(
                    "hqk,hdq->hdk",
                    weights.astype(jnp.bfloat16),
                    cotan_block,
                    preferred_element_type=jnp.float32,
                )
            )
    query_part = jnp.concatenate(query_list, axis=0) if want_query else None
    key_part = jnp.concatenate(key_list, axis=0) if want_keys else None
    value_part = jnp.concatenate(value_list, axis=0) if want_keys else None
    return (query_part, key_part, value_part)


def head_offsets(head_total, stride):
    return np.arange(head_total) * stride // head_total


def select_rows(array_in, stride):
    head_total = array_in.shape[0]
    offsets = head_offsets(head_total, stride)
    folded = array_in.reshape(array_in.shape[:-1] + (array_in.shape[-1] // stride, stride))
    return jnp.stack(
        [folded[head_index, ..., int(offsets[head_index])] for head_index in range(head_total)]
    )


def spread_rows(array_in, stride, fill_value):
    head_total = array_in.shape[0]
    chosen = np.arange(stride)[None, :] == head_offsets(head_total, stride)[:, None]
    chosen = chosen.reshape((head_total,) + (1,) * (array_in.ndim - 1) + (stride,))
    full = jnp.where(chosen, array_in[..., None], fill_value)
    return full.reshape(array_in.shape[:-1] + (array_in.shape[-1] * stride,))


def to_heads(flat_in):
    return jnp.transpose(flat_in.reshape(flat_in.shape[0], HEADS, -1), (1, 2, 0))


def to_flat(heads_in):
    return jnp.transpose(heads_in, (2, 0, 1)).reshape(heads_in.shape[2], -1)


def local(query_tiles, key_tiles, value_tiles, cotangent, row_lengths):
    tile_count = query_tiles.shape[0]
    score_scale = HEAD ** (-0.5)
    query_heads = to_heads(query_tiles)
    key_heads = to_heads(key_tiles)
    value_heads = to_heads(value_tiles)
    cotan_heads = to_heads(cotangent)
    tile_slot = jnp.arange(tile_count, dtype=jnp.int32)
    tile_valid = tile_slot % ROW < jnp.repeat(row_lengths, ROW, total_repeat_length=tile_count)
    valid_heads = jnp.broadcast_to(tile_valid[None, :], (HEADS, tile_count))
    group_query = select_rows(query_heads, STRIDE_GROUP)
    group_key = select_rows(key_heads, STRIDE_GROUP)
    group_value = select_rows(value_heads, STRIDE_GROUP)
    group_cotan = select_rows(cotan_heads, STRIDE_GROUP)
    group_valid = select_rows(valid_heads, STRIDE_GROUP)
    group_flag = group_valid.astype(jnp.bfloat16)[:, None, :]
    slide_query = select_rows(query_heads, STRIDE_SLIDE)
    slide_key = select_rows(key_heads, STRIDE_SLIDE)
    slide_value = select_rows(value_heads, STRIDE_SLIDE)
    slide_flag = select_rows(valid_heads, STRIDE_SLIDE).astype(jnp.bfloat16)[:, None, :]
    owned_query, owned_key, owned_value, owned_flag = (
        lax.all_to_all(slide_query, "outer", split_axis=0, concat_axis=2, tiled=True),
        lax.all_to_all(slide_key, "outer", split_axis=0, concat_axis=2, tiled=True),
        lax.all_to_all(slide_value, "outer", split_axis=0, concat_axis=2, tiled=True),
        lax.all_to_all(slide_flag, "outer", split_axis=0, concat_axis=2, tiled=True),
    )
    got_group = (
        lax.all_gather(group_key, "inner", axis=2, tiled=True),
        lax.all_gather(group_value, "inner", axis=2, tiled=True),
        lax.all_gather(group_flag, "inner", axis=2, tiled=True),
    )
    got_slide = (
        lax.all_gather(owned_key, "inner", axis=2, tiled=True),
        lax.all_gather(owned_value, "inner", axis=2, tiled=True),
        lax.all_gather(owned_flag, "inner", axis=2, tiled=True),
    )
    near_peak, near_total, near_sum = branch_stats(
        query_heads, key_heads, value_heads, valid_heads, score_scale
    )
    remote_group_key = got_group[0]
    remote_group_value = got_group[1]
    remote_group_valid = got_group[2][:, 0, :] > 0.5
    group_peak, group_total, group_sum = branch_stats(
        group_query, remote_group_key, remote_group_value, remote_group_valid, score_scale
    )
    slide_all_key = got_slide[0]
    slide_all_value = got_slide[1]
    slide_all_valid = got_slide[2][:, 0, :] > 0.5
    owner_peak, owner_total, owner_sum = branch_stats(
        owned_query, slide_all_key, slide_all_value, slide_all_valid, score_scale
    )
    slide_peak, slide_total, slide_sum = (
        lax.all_to_all(owner_peak[:, None, :], "outer", split_axis=2, concat_axis=0, tiled=True),
        lax.all_to_all(owner_total[:, None, :], "outer", split_axis=2, concat_axis=0, tiled=True),
        lax.all_to_all(owner_sum, "outer", split_axis=2, concat_axis=0, tiled=True),
    )
    slide_peak = slide_peak[:, 0, :]
    slide_total = slide_total[:, 0, :]
    group_peak_full = spread_rows(group_peak, STRIDE_GROUP, NEGATIVE_FILL)
    slide_peak_full = spread_rows(slide_peak, STRIDE_SLIDE, NEGATIVE_FILL)
    best_peak = jnp.maximum(jnp.maximum(near_peak, group_peak_full), slide_peak_full)
    near_weight = jnp.exp(near_peak - best_peak)
    group_weight = jnp.exp(group_peak_full - best_peak)
    slide_weight = jnp.exp(slide_peak_full - best_peak)
    denominator = (
        near_total * near_weight
        + spread_rows(group_total, STRIDE_GROUP, 0.0) * group_weight
        + spread_rows(slide_total, STRIDE_SLIDE, 0.0) * slide_weight
    )
    numerator = (
        near_sum * near_weight[:, None, :]
        + spread_rows(group_sum, STRIDE_GROUP, 0.0) * group_weight[:, None, :]
        + spread_rows(slide_sum, STRIDE_SLIDE, 0.0) * slide_weight[:, None, :]
    )
    attended = (numerator / denominator[:, None, :]).astype(jnp.bfloat16)
    log_norm = best_peak + jnp.log(denominator)
    out_dot = jnp.sum(cotan_heads.astype(jnp.float32) * attended.astype(jnp.float32), axis=1)
    near_query, near_key, near_value = branch_grads(
        query_heads,
        key_heads,
        value_heads,
        cotan_heads,
        log_norm,
        out_dot,
        valid_heads,
        score_scale,
        True,
        True,
    )
    group_lse = select_rows(log_norm, STRIDE_GROUP)
    group_dot = select_rows(out_dot, STRIDE_GROUP)
    group_query_grad = branch_grads(
        group_query,
        remote_group_key,
        remote_group_value,
        group_cotan,
        group_lse,
        group_dot,
        remote_group_valid,
        score_scale,
        True,
        False,
    )[0]
    got_group_rows = (
        lax.all_gather(group_query, "inner", axis=2, tiled=True),
        lax.all_gather(group_cotan, "inner", axis=2, tiled=True),
    )
    got_group_stats = (
        lax.all_gather(group_lse, "inner", axis=1, tiled=True),
        lax.all_gather(group_dot, "inner", axis=1, tiled=True),
    )
    unused_group, group_key_grad, group_value_grad = branch_grads(
        got_group_rows[0],
        group_key,
        group_value,
        got_group_rows[1],
        got_group_stats[0],
        got_group_stats[1],
        group_valid,
        score_scale,
        False,
        True,
    )
    slide_cotan = select_rows(cotan_heads, STRIDE_SLIDE)
    slide_lse = select_rows(log_norm, STRIDE_SLIDE)
    slide_dot = select_rows(out_dot, STRIDE_SLIDE)
    owned_cotan = lax.all_to_all(slide_cotan, "outer", split_axis=0, concat_axis=2, tiled=True)
    owned_lse, owned_dot = (
        lax.all_to_all(slide_lse, "outer", split_axis=0, concat_axis=1, tiled=True),
        lax.all_to_all(slide_dot, "outer", split_axis=0, concat_axis=1, tiled=True),
    )
    owned_query_grad, partial_key, partial_value = branch_grads(
        owned_query,
        slide_all_key,
        slide_all_value,
        owned_cotan,
        owned_lse,
        owned_dot,
        slide_all_valid,
        score_scale,
        True,
        True,
    )
    owned_key_grad, owned_value_grad = (
        lax.psum_scatter(
            partial_key.astype(jnp.bfloat16), "inner", scatter_dimension=2, tiled=True
        ).astype(jnp.float32),
        lax.psum_scatter(
            partial_value.astype(jnp.bfloat16), "inner", scatter_dimension=2, tiled=True
        ).astype(jnp.float32),
    )
    slide_query_grad, slide_key_grad, slide_value_grad = (
        lax.all_to_all(
            as_sent(owned_query_grad), "outer", split_axis=2, concat_axis=0, tiled=True
        ).astype(owned_query_grad.dtype),
        lax.all_to_all(
            owned_key_grad.astype(jnp.bfloat16), "outer", split_axis=2, concat_axis=0, tiled=True
        ).astype(owned_key_grad.dtype),
        lax.all_to_all(
            owned_value_grad.astype(jnp.bfloat16), "outer", split_axis=2, concat_axis=0, tiled=True
        ).astype(owned_value_grad.dtype),
    )
    query_grad = (
        near_query
        + spread_rows(group_query_grad, STRIDE_GROUP, 0.0)
        + spread_rows(slide_query_grad, STRIDE_SLIDE, 0.0)
    )
    key_grad = (
        near_key
        + spread_rows(group_key_grad, STRIDE_GROUP, 0.0)
        + spread_rows(slide_key_grad, STRIDE_SLIDE, 0.0)
    )
    value_grad = (
        near_value
        + spread_rows(group_value_grad, STRIDE_GROUP, 0.0)
        + spread_rows(slide_value_grad, STRIDE_SLIDE, 0.0)
    )
    return (
        to_flat(attended),
        to_flat(query_grad.astype(jnp.bfloat16)),
        to_flat(key_grad.astype(jnp.bfloat16)),
        to_flat(value_grad.astype(jnp.bfloat16)),
    )


BF = jnp.bfloat16
F32 = jnp.float32
LANES = 128
SCALE = HEAD ** (-0.5)
PAIR = 2 * HEAD
PAIRS = HEADS // 2
MESH = pl.DeviceIdType.MESH


def iota2(shape, axis):
    return lax.broadcasted_iota(jnp.int32, shape, axis)


def original_tile(j):
    return (j & 7) * 16 + ((j >> 3) & 3) * 4 + (j >> 5)


def permute_matrix(inverse):
    shape = (LANES, LANES)
    j, i = (iota2(shape, 1), iota2(shape, 0)) if inverse else (iota2(shape, 0), iota2(shape, 1))
    return (original_tile(j) == i).astype(F32).astype(BF)


def identity(size):
    shape = (size, size)
    return (iota2(shape, 0) == iota2(shape, 1)).astype(F32).astype(BF)


def key_bias(len_ref):
    tile = original_tile(iota2((LANES, LANES), 0))
    row = tile >> 5
    length = jnp.full((LANES, LANES), len_ref[0], jnp.int32)
    for index in range(1, 4):
        length = jnp.where(row == index, len_ref[index], length)
    return jnp.where((tile & 31) < length, 0.0, NEGATIVE_FILL).astype(F32)


def mm(a, b):
    return jnp.dot(a, b, preferred_element_type=F32)


def mm_t(a, b):
    return lax.dot_general(a, b, (((1,), (1,)), ((), ())), preferred_element_type=F32)


def slide_row(r):
    return (r % 4) * 32 + (r // 4) * 8


def head_lanes(lane, p, e):
    return ((lane - (PAIR * p + HEAD * e)) & (LANES - 1)) < HEAD


def flag_lane(p):
    return (PAIR * (p + 1)) & (LANES - 1)


def as_mask(keep):
    return keep.astype(F32).astype(BF)


def head_masks(p):
    lane = iota2((1, LANES), 1)
    masks = [as_mask(head_lanes(lane, p, e)) for e in range(2)]
    flags = [as_mask(lane == flag_lane(p) + e) for e in range(2)]
    return masks, flags


def two_heads(x, masks, flags=None):
    parts = [x * masks[e] for e in range(2)]
    if flags is not None:
        parts = [parts[e] + flags[e] for e in range(2)]
    return jnp.concatenate(parts, axis=0)


def pieces_of(p):
    base, spot = p // 4 * 3, p % 4
    if spot == 0:
        return [(base, 0, 96)]
    if spot == 1:
        return [(base, 96, 128), (base + 1, 0, 64)]
    if spot == 2:
        return [(base + 1, 64, 128), (base + 2, 0, 32)]
    return [(base + 2, 32, 128)]


def pair_tile(x, p):
    parts = pieces_of(p)
    tiles = [x[:, t * LANES : (t + 1) * LANES] for t, _, _ in parts]
    if len(tiles) == 1:
        return tiles[0]
    lane = iota2(tiles[0].shape, 1)
    return jnp.where(lane >= parts[0][1], tiles[0], tiles[1])


K_ROW, Q_ROW, V_ROW, S_ROW, C_ROW, G_ROWS = 0, 32, 64, 96, 112, 144


def prep_pair(x, p, bias=None):
    tile = pair_tile(x, p)
    lane = iota2(tile.shape, 1)
    flag = flag_lane(p)
    if bias is not None:
        tile = jnp.where((lane == flag) | (lane == flag + 1), bias, tile)
    first, second = [tile[slide_row(2 * p + e) :][:8] for e in range(2)]
    lane = iota2(first.shape, 1)
    slide = jnp.where(head_lanes(lane, p, 1) | (lane == flag + 1), second, first)
    return tile, slide


def near_early(p, tp_ref, pn_ref, ad_ref, kt_ref, vt_ref, eye):
    k, q, v, c = [tp_ref[a, p] for a in range(4)]
    masks, flags = head_masks(p)
    s = mm_t(k, two_heads(q, masks, flags)) * SCALE
    dp = mm_t(v, two_heads(c, masks))
    kt_ref[p] = mm_t(eye, two_heads(k, masks)).astype(BF)
    vt_ref[p] = mm_t(eye, two_heads(v, masks)).astype(BF)
    peak = jnp.max(s, axis=0, keepdims=True)
    weights = jnp.exp(s - peak)
    total = jnp.sum(weights, axis=0, keepdims=True)
    weights = weights * (1.0 / total)
    delta = jnp.sum(weights * dp, axis=0, keepdims=True)
    pn_ref[p] = weights
    ad_ref[p] = weights * (dp - delta)
    return peak + jnp.log(total), delta


def turn(x, shift):
    return pltpu.roll(x, shift & (LANES - 1), 1)


def near_stats(p, me, lse, delta):
    shape = (8, LANES)
    row, lane = iota2(shape, 0), iota2(shape, 1)

    def wide(x, e):
        return jnp.broadcast_to(x[:, e * LANES : (e + 1) * LANES], shape)

    high = row < 4
    heads = [jnp.where(high, wide(lse, e), wide(delta, e)) for e in range(2)]
    group = turn(jnp.where((row & 3) == 0, heads[0], heads[1]), ((me & 3) - p // 2) * 32)
    spots = [turn(heads[e], e * 64 + me * 8 - slide_row(2 * p + e)) for e in range(2)]
    slide = jnp.where(lane < 64, spots[0], spots[1])
    return jnp.where((row & 3) == 2, slide, group)


def near_late(p, me, r2_ref, tp_ref, pn_ref, ad_ref, kt_ref, vt_ref, late_ref, turned_ref):
    tile = r2_ref[p]
    lane = iota2((1, LANES), 1)
    start = p // 2 * 32
    group = turn(tile, start - (me & 3) * 32)
    in_group = (lane >= start) & (lane < start + 32)
    scales, shifts = [], []
    for e in range(2):
        at = slide_row(2 * p + e)
        slide = turn(tile, at - e * 64 - me * 8)
        in_slide = (lane >= at) & (lane < at + 8)
        for index, (found, fill) in enumerate(((scales, 1.0), (shifts, 0.0))):
            value = jnp.where(in_slide, slide[4 * index + 2 : 4 * index + 3], fill)
            found.append(jnp.where(in_group, group[4 * index + e : 4 * index + e + 1], value))
    scale = jnp.concatenate(scales, axis=1)
    shift = jnp.concatenate(shifts, axis=1)
    weights = pn_ref[p]
    low = (weights * scale).astype(BF)
    grads = (ad_ref[p] * (scale * SCALE) - weights * (scale * shift * SCALE)).astype(BF)
    masks, _ = head_masks(p)
    late_ref[0, p] = mm(grads, two_heads(tp_ref[1, p], masks))
    late_ref[1, p] = mm(low, two_heads(tp_ref[3, p], masks))

    def stacked(x):
        return jnp.concatenate([x[:, :LANES], x[:, LANES:]], axis=0)

    for index, value in enumerate((mm(vt_ref[p], stacked(low)), mm(kt_ref[p], stacked(grads)))):
        value = value.astype(BF)
        for t, first, last in pieces_of(p):
            turned_ref[index, t * LANES + first : t * LANES + last] = value[first:last]


def branch(s, dp):
    peak = jnp.max(s, axis=0, keepdims=True)
    weights = jnp.exp(s - peak)
    total = jnp.sum(weights, axis=0, keepdims=True)
    delta = jnp.sum(weights * dp, axis=0, keepdims=True) / total
    return weights, peak, peak + jnp.log(total), delta


def rows_of(row, first, second, third):
    first, second, third = [jnp.broadcast_to(x, row.shape) for x in (first, second, third)]
    return jnp.where(row == 0, first, jnp.where(row == 1, second, third))


def slide_scores(masks, flags, gr_ref, skv_ref):
    kv = skv_ref[...].reshape(-1, LANES)
    sources = gr_ref.shape[0]
    wide = gr_ref[:, S_ROW:C_ROW].astype(F32)
    q, c = [wide[:, a : a + 8].reshape(sources * 8, LANES).astype(BF) for a in (0, 8)]
    q2, c2 = two_heads(q, masks, flags), two_heads(c, masks)
    both = mm_t(kv, jnp.concatenate([q2, c2], axis=0)).reshape(-1, 16, 2 * LANES)
    s = both[:, 0:8, :LANES].reshape(-1, LANES) * SCALE
    dp = both[:, 8:16, LANES:].reshape(-1, LANES)
    return kv, q2, c2, s, dp


def near_of(row, lane, ns_ref):
    slide = ns_ref[0]
    for source in range(1, 8):
        slide = jnp.where(((lane & 63) >> 3) == source, ns_ref[source], slide)
    found = []
    for j in range(2):
        group = ns_ref[4 * j]
        for q in range(1, 4):
            group = jnp.where((lane >> 5) == q, ns_ref[4 * j + q], group)
        both = jnp.where((row & 3) == 2, slide, group)
        found.append((both, pltpu.roll(both, 4, 0)))
    return found


def crossed(row, lane, p, slide, group):
    first = lax.rem(2 * p, 5) == 0
    second = lax.rem(2 * p + 1, 5) == 0
    e = jnp.where(second, 1, 0)
    any_head = jnp.logical_or(first, second)
    at = p // 2 * 8
    source = jnp.where(row < 4, *slide)
    found, to_slide = [], None
    for j in range(2):
        pair = [jnp.where(row < 4, *group[2 * head + j]) for head in range(2)]
        chosen = jnp.where(second, pair[1], pair[0])
        to_group = None
        for q in range(4):
            here, there = q * 32 + at, (4 * j + q) * 8 + e * 64
            moved = turn(source, here - there + LANES)
            to_group = moved if q == 0 else jnp.where((lane >> 5) == q, moved, to_group)
            moved = turn(chosen, there - here + LANES)
            same = ((lane & 63) >> 3) == 4 * j + q
            to_slide = moved if to_slide is None else jnp.where(same, moved, to_slide)
        found.append(to_group)
    edge = row & 3
    in_group = (edge == e) & ((lane & 31) >> 3 == p // 2) & any_head
    in_slide = (edge == 2) & ((lane >> 6) == e) & any_head
    results = []
    for to_group in found:
        both = jnp.where(edge == 2, to_slide, to_group)
        both = jnp.where(in_group | in_slide, both, jnp.where(row < 4, NEGATIVE_FILL, 0.0))
        results.append((both, pltpu.roll(both, 4, 0)))
    return results


class Exchange:
    def __init__(self, count, make, every):
        self.count, self.make, self.every = count, make, every

    def start(self):
        @pl.loop(1, self.count)
        def _(step):
            self.make(step).start()

    def wait_recv(self):
        self.every.wait_recv()

    def wait_send(self):
        self.every.wait_send()


def wrapped(value, count):
    return jnp.where(value >= count, value - count, value)


def whole_kernel(
    inner, outers, len_hbm, q_hbm, k_hbm, v_hbm, c_hbm, turned, acc,
    len_ref, loaded, load_sem, tp, gm, gr, skv_s, skv, pn, ad, kt, vt, ns_s, ns_r, r2_s, r2_r,
    r4_s, r4_r, xs, xr, sg_s, sg_r, late, send_sem, recv_sem, x_send, x_recv,
):
    outer, me = lax.axis_index("outer"), lax.axis_index("inner")
    p = me

    def scope(name):
        return jax.named_scope(name)

    def copy_to(src, dst, sems, index, device):
        return pltpu.make_async_remote_copy(
            src_ref=src,
            dst_ref=dst,
            send_sem=sems[0].at[index],
            recv_sem=sems[1].at[index],
            device_id=device,
            device_id_type=MESH,
        )

    def exchange(index, source, target, size):
        sems, next_place = (send_sem, recv_sem), wrapped(me + 1, inner)

        def make(step):
            peer = wrapped(me + step, inner)
            return copy_to(source(peer), target(me), sems, index, (outer, peer))

        return Exchange(inner, make, copy_to(size, size, sems, index, (outer, next_place)))

    def across(index, source, target, size):
        sems, next_place = (x_send, x_recv), wrapped(outer + 1, outers)

        def make(step):
            peer = wrapped(outer + step, outers)
            return copy_to(source(peer), target, sems, index, (peer, me))

        return Exchange(outers, make, copy_to(size, size, sems, index, (next_place, me)))

    def blocks_exchange(index, src, dst):
        size = dst.at[pl.ds(0, inner - 1)]
        return exchange(index, lambda peer: src.at[peer], lambda mine: dst.at[mine], size)

    def rows_exchange(index, src, dst, first, last):
        rows = pl.ds(first, last - first)
        size = dst.at[pl.ds(0, inner - 1), rows]
        return exchange(index, lambda peer: src.at[peer, rows], lambda mine: dst.at[mine, rows], size)

    some = pl.ds(0, inner - 1)
    send_skv = exchange(0, lambda peer: skv_s.at[peer], lambda mine: skv.at[outer, mine], skv.at[0, some])
    send_k = rows_exchange(1, gm, gr, K_ROW, Q_ROW)
    send_qv = rows_exchange(2, gm, gr, Q_ROW, S_ROW)
    send_c = rows_exchange(3, gm, gr, S_ROW, G_ROWS)
    send_ns = [blocks_exchange(4, ns_s, ns_r)]
    send_r2 = exchange(5, lambda peer: r2_s.at[peer >> 2], lambda mine: r2_r.at[mine], r2_r.at[some])
    send_oq = rows_exchange(6, r4_s, r4_r, 0, 80)
    send_kv = rows_exchange(7, r4_s, r4_r, 80, G_ROWS)
    send_sg = blocks_exchange(8, sg_s, sg_r)
    forward = across(0, lambda peer: skv.at[outer], skv.at[outer], skv.at[pl.ds(0, outers - 1)])
    backward = across(1, lambda peer: xs.at[peer], xr.at[outer], xr.at[pl.ds(0, outers - 1)])

    barrier = pltpu.get_barrier_semaphore()
    with scope("load_start"):
        loads = [
            pltpu.make_async_copy(ref, loaded.at[a], load_sem.at[a])
            for a, ref in enumerate((k_hbm, q_hbm, v_hbm, c_hbm))
        ]
        loads.append(pltpu.make_async_copy(len_hbm, len_ref, load_sem.at[4]))
        for index in (4, 0, 2, 1, 3):
            loads[index].start()
    with scope("greet"):

        @pl.loop(1, inner)
        def _(step):
            pl.semaphore_signal(
                barrier, inc=1, device_id=(outer, wrapped(me + step, inner)), device_id_type=MESH
            )

        @pl.loop(1, outers)
        def _(step):
            pl.semaphore_signal(
                barrier, inc=1, device_id=(wrapped(outer + step, outers), me), device_id_type=MESH
            )

    perm = permute_matrix(False)
    eye = identity(LANES)
    with scope("load_wait"):
        loads[4].wait()
        loads[0].wait()
        loads[2].wait()
    with scope("prep_kv"):
        bias = key_bias(len_ref)
        xk = mm(perm, loaded[0])
        xv = mm(perm, loaded[2])
        for h in range(PAIRS):
            rows = slice(h // 2 * 32, h // 2 * 32 + 32)
            tile, key_slide = prep_pair(xk, h, bias)
            tp[0, h] = tile.astype(BF)
            gm[h, K_ROW:Q_ROW] = tile[rows].astype(BF)
            tile, value_slide = prep_pair(xv, h)
            tp[2, h] = tile.astype(BF)
            gm[h, V_ROW:S_ROW] = tile[rows].astype(BF)
            skv_s[h] = jnp.concatenate([key_slide, value_slide], axis=0).astype(BF)
    with scope("barrier_wait"):
        pl.semaphore_wait(barrier, inner - 1 + outers - 1)
    with scope("send_kv"):
        send_skv.start()
        send_k.start()
        skv[outer, me] = skv_s[me]
    with scope("prep_qc"):
        loads[1].wait()
        loads[3].wait()
        xq = mm(perm, loaded[1])
        xc = mm(perm, loaded[3])
        for h in range(PAIRS):
            rows = slice(h // 2 * 32, h // 2 * 32 + 32)
            tile, query_slide = prep_pair(xq, h)
            tp[1, h] = tile.astype(BF)
            gm[h, Q_ROW:V_ROW] = tile[rows].astype(BF)
            tile, cotan_slide = prep_pair(xc, h)
            tp[3, h] = tile.astype(BF)
            gm[h, C_ROW:G_ROWS] = tile[rows].astype(BF)
            gm[h, S_ROW:C_ROW] = jnp.concatenate([query_slide, cotan_slide], axis=0).astype(BF)
    with scope("send_qc"):
        send_qv.start()
        send_c.start()
        gr[me] = gm[me]

    def early(h):
        lse, delta = near_early(h, tp, pn, ad, kt, vt, eye)
        ns_s[h] = near_stats(h, me, lse, delta)

    with scope("near_early"):
        for h in range(PAIRS):
            early(h)
    with scope("send_ns"):
        send_ns[0].start()
        ns_r[me] = ns_s[me]
    with scope("skv_wait"):
        send_skv.wait_recv()
    with scope("forward"):
        forward.start()
    masks, flags = head_masks(p)
    row, lane = iota2((8, LANES), 0), iota2((8, LANES), 1)
    with scope("group_wait"):
        send_k.wait_recv()
        send_qv.wait_recv()
        send_c.wait_recv()
    with scope("group_scores"):
        k, q, v, c = [
            gr[:, at : at + 32].reshape(inner * 32, LANES) for at in (K_ROW, Q_ROW, V_ROW, C_ROW)
        ]
        q2, c2 = two_heads(q, masks, flags), two_heads(c, masks)
        chunks = []
        for index in range(4):
            part = slice(index * LANES, (index + 1) * LANES)
            dp = mm_t(v, c2[part])
            chunks.append(branch(mm_t(k, q2[part]) * SCALE, dp) + (dp,))
        kt2 = mm_t(eye, two_heads(k, masks)).astype(BF)
        vt2 = mm_t(eye, two_heads(v, masks)).astype(BF)
    with scope("forward_wait"):
        forward.wait_recv()
    with scope("slide_scores"):
        skv_all, qs2, cs2, s, slide_dp = slide_scores(masks, flags, gr, skv)
        slide_weights, slide_peak, slide_lse, slide_delta = branch(s, slide_dp)
        skv_t = mm_t(eye, skv_all).astype(BF)
    with scope("ns_wait"):
        send_ns[0].wait_recv()
    with scope("merge"):
        near = near_of(row, lane, ns_r)
        other = crossed(
            row,
            lane,
            p,
            [jnp.broadcast_to(x, row.shape) for x in (slide_lse, slide_delta)],
            [[jnp.broadcast_to(x, row.shape) for x in chunk[2:4]] for chunk in chunks],
        )
        factors, deltas = [], []
        for j in range(2):
            own = [
                rows_of(row, chunks[j][i], chunks[2 + j][i], last)
                for i, last in ((1, slide_peak), (2, slide_lse), (3, slide_delta))
            ]
            best = jnp.maximum(jnp.maximum(near[j][0], own[1]), other[j][0])
            parts = [jnp.exp(x - best) for x in (near[j][0], own[1], other[j][0])]
            total = parts[0] + parts[1] + parts[2]
            inverse = 1.0 / total
            lse = best + jnp.log(total)
            delta = (parts[0] * near[j][1] + parts[1] * own[2] + parts[2] * other[j][1]) * inverse
            factors.append(jnp.exp(own[0] - lse))
            deltas.append(delta)
            r2_s[j] = jnp.where(row < 4, parts[0] * inverse, pltpu.roll(delta - near[j][1], 4, 0))
    with scope("send_r2"):
        send_r2.start()
        r2_r[me] = r2_s[me >> 2]
    with scope("slide_bwd"):
        weights = slide_weights * factors[0][2:3]
        grads = weights * (slide_dp - deltas[0][2:3]) * SCALE
        blocks = [x.reshape(-1, 8, LANES) for x in (grads, weights)]
        empty = jnp.zeros_like(blocks[0])
        mixed = jnp.concatenate(
            [
                jnp.concatenate([blocks[0], empty], axis=2),
                jnp.concatenate([empty, blocks[1]], axis=2),
            ],
            axis=1,
        )
        mixed = mixed.reshape(-1, 2 * LANES).astype(BF)
        xs[...] = mm(mixed, jnp.concatenate([qs2, cs2], axis=0)).astype(BF).reshape(xs.shape)
    with scope("send_x"):
        backward.start()
    with scope("slide_q"):
        both = mm_t(identity(2 * LANES), mm(skv_t, mixed).astype(BF))
        quarter = LANES // 2
        head0 = head_lanes(iota2((quarter, LANES), 1), p, 0)
        query = jnp.where(head0, both[0:quarter], both[quarter:LANES])
        out = jnp.where(head0, both[LANES : 3 * quarter], both[3 * quarter : 4 * quarter])
        blocks = [x.reshape(inner, 8, LANES) for x in (out, query)]
        r4_s[:, 64:80] = jnp.concatenate(blocks, axis=1).astype(BF)
    with scope("group_bwd_q"):
        lows, grads = [], []
        for index, (weights, _, _, _, dp) in enumerate(chunks):
            e, j = divmod(index, 2)
            weights = weights * factors[j][e : e + 1]
            lows.append(weights.astype(BF))
            grads.append((weights * (dp - deltas[j][e : e + 1]) * SCALE).astype(BF))
        for j in range(2):
            for at, wide, parts in ((0, vt2, lows), (32, kt2, grads)):
                value = mm(wide, jnp.concatenate([parts[j], parts[2 + j]], axis=0)).astype(BF)
                value = mm_t(eye, value).astype(BF)
                r4_s[4 * j : 4 * j + 4, at : at + 32] = value.reshape(4, 32, LANES)
    with scope("send_oq"):
        send_oq.start()
    with scope("group_bwd_kv"):
        for at, parts, rows in ((80, grads, q2), (112, lows, c2)):
            value = mm(jnp.concatenate(parts, axis=1), rows).astype(BF)
            r4_s[:, at : at + 32] = value.reshape(inner, 32, LANES)
    with scope("send_kv"):
        send_kv.start()
        r4_r[me] = r4_s[me]
    with scope("r2_wait"):
        send_r2.wait_recv()
    with scope("near_late0"):
        for h in range(PAIRS // 2):
            near_late(h, me, r2_r, tp, pn, ad, kt, vt, late, turned)
    with scope("x_wait"):
        backward.wait_recv()
    with scope("x_sum"):
        total = xs[outer].astype(F32)
        for step in range(1, outers):
            total = total + xr[wrapped(outer + step, outers)].astype(F32)
        sg_s[...] = total.astype(BF)
    with scope("send_sg"):
        send_sg.start()
        sg_r[me] = sg_s[me]
    with scope("near_late1"):
        for h in range(PAIRS // 2, PAIRS):
            near_late(h, me, r2_r, tp, pn, ad, kt, vt, late, turned)
    with scope("collect"):
        acc[0:2] = jnp.zeros((2,) + acc.shape[1:], F32)
        for a in range(2):
            for t in range(D_TILES):
                value = None
                for h in range(PAIRS):
                    for tile, first, last in pieces_of(h):
                        if tile == t:
                            piece = late[a, h]
                            lane_full = iota2(piece.shape, 1)
                            value = piece if value is None else jnp.where(lane_full >= first, piece, value)
                acc[2 + a, :, t * LANES : (t + 1) * LANES] = value
    with scope("drain"):
        for sent in (send_skv, send_k, send_qv, send_c, send_ns[0], forward, send_r2, backward):
            sent.wait_send()
    with scope("oq_wait"):
        send_oq.wait_recv()
    with scope("add_oq"):
        for h in range(PAIRS):
            add_block(acc, (0, 1), h, r4_r[h, 0:64], r4_r[h, 64:80])
    with scope("kv_wait"):
        send_kv.wait_recv()
        send_sg.wait_recv()
    with scope("add_kv"):
        for h in range(PAIRS):
            add_block(acc, (2, 3), h, r4_r[h, 80:G_ROWS], sg_r[h])
    with scope("drain_last"):
        for sent in (send_oq, send_kv, send_sg):
            sent.wait_send()


D_TILES = HEADS * HEAD // LANES


def final_kernel(turned, acc, att_hbm, dq_hbm, dk_hbm, dv_hbm, done, sems):
    back = permute_matrix(True)
    copies = []
    for a, ref in enumerate((att_hbm, dq_hbm, dk_hbm, dv_hbm)):
        value = mm(back, acc[a].astype(BF))
        if a < 2:
            value = value + mm_t(back, turned[a])
        done[a] = value.astype(BF)
        copies.append(pltpu.make_async_copy(done.at[a], ref, sems.at[a]))
        copies[-1].start()
    for copy in copies:
        copy.wait()


def add_block(acc, outs, h, group, slide):
    group, slide = group.astype(F32), slide.astype(F32)
    start = h // 2 * 32
    lane = iota2((32, LANES), 1)
    lane8 = iota2((8, LANES), 1)
    for index, a in enumerate(outs):
        block = group[32 * index : 32 * index + 32]
        small = slide[8 * index : 8 * index + 8]
        for t, first, last in pieces_of(h):
            cols = slice(t * LANES, (t + 1) * LANES)
            keep = (lane >= first) & (lane < last)
            acc[a, start : start + 32, cols] += jnp.where(keep, block, 0.0)
            for e in range(2):
                at = slide_row(2 * h + e)
                keep8 = (lane8 >= first) & (lane8 < last) & head_lanes(lane8, h, e)
                acc[a, at : at + 8, cols] += jnp.where(keep8, small, 0.0)


def fast_local(inner, outers, *args):
    row_lengths, tiles_in = args[4], args[:4]
    tiles, width = tiles_in[0].shape
    vmem = pl.BlockSpec(memory_space=pltpu.VMEM)
    hbm = pl.BlockSpec(memory_space=pltpu.HBM)

    def both(shape, dtype):
        return [pltpu.VMEM(shape, dtype)] * 2

    scratch = [
        pltpu.SMEM(row_lengths.shape, jnp.int32),
        pltpu.VMEM((4, tiles, width), BF),
        pltpu.SemaphoreType.DMA((5,)),
        pltpu.VMEM((4, PAIRS, tiles, LANES), BF),
    ]
    scratch += both((inner, G_ROWS, LANES), BF)
    scratch += [pltpu.VMEM((inner, 16, LANES), BF), pltpu.VMEM((outers, inner, 16, LANES), BF)]
    scratch += both((PAIRS, tiles, 2 * LANES), F32)
    scratch += both((PAIRS, LANES, 2 * LANES), BF)
    scratch += both((inner, 8, LANES), F32)
    scratch += [pltpu.VMEM((2, 8, LANES), F32), pltpu.VMEM((inner, 8, LANES), F32)]
    scratch += both((inner, G_ROWS, LANES), BF)
    scratch += both((outers, inner, 16, LANES), BF)
    scratch += both((inner, 16, LANES), BF)
    scratch += [pltpu.VMEM((2, PAIRS, tiles, LANES), F32)]
    scratch += [pltpu.SemaphoreType.DMA((9,))] * 2 + [pltpu.SemaphoreType.DMA((2,))] * 2
    in_hbm = [pltpu.with_memory_space_constraint(x, pltpu.HBM) for x in (row_lengths, *tiles_in)]
    shapes = (((2, width, tiles), BF), ((4, tiles, width), F32))
    between = pl.pallas_call(
        lambda *refs: whole_kernel(inner, outers, *refs),
        out_shape=[pltpu.VMEM(shape, dtype) for shape, dtype in shapes],
        in_specs=[hbm] * 5,
        out_specs=[vmem] * 2,
        scratch_shapes=scratch,
        compiler_params=pltpu.CompilerParams(
            collective_id=0, has_side_effects=True, vmem_limit_bytes=32 * 1024 * 1024
        ),
    )(*in_hbm)
    return tuple(
        pl.pallas_call(
            final_kernel,
            out_shape=[pltpu.HBM((tiles, width), BF)] * 4,
            in_specs=[vmem] * 2,
            out_specs=[hbm] * 4,
            scratch_shapes=[pltpu.VMEM((4, tiles, width), BF), pltpu.SemaphoreType.DMA((4,))],
            compiler_params=pltpu.CompilerParams(vmem_limit_bytes=32 * 1024 * 1024),
        )(*between)
    )


def solution(mesh):
    in_specs = (P(("outer", "inner"), None),) * 4 + (P(("outer", "inner")),)
    out_specs = (P(("outer", "inner"), None),) * 4
    inner, outers = mesh.shape["inner"], mesh.shape["outer"]

    def step(*args):
        fits = inner == PAIRS and outers == 4
        if fits and args[0].shape == (LANES, HEADS * HEAD):
            return fast_local(inner, outers, *args)
        return local(*args)

    return jax.shard_map(step, mesh=mesh, in_specs=in_specs, out_specs=out_specs, check_vma=False)
```

```python
import jax
import jax.numpy as jnp
import numpy as np
from jax import lax
from jax.experimental import pallas as pl
from jax.experimental.pallas import tpu as pltpu
from jax.sharding import PartitionSpec as P

HEADS = 16
HEAD = 48
ROW = 32
STRIDE_GROUP = 4
STRIDE_SLIDE = 16


NEGATIVE_FILL = -1e30
heads_at_once = 4


def as_sent(value):

    def short(part):
        return part.astype(jnp.bfloat16) if part.dtype == jnp.float32 else part

    return jax.tree.map(short, value)


def head_ranges(head_total):
    step_size = min(head_total, heads_at_once)
    return [(first_head, first_head + step_size) for first_head in range(0, head_total, step_size)]


def scores_of(query_block, key_block, score_scale):
    return (
        jnp.einsum("hdq,hdk->hqk", query_block, key_block, preferred_element_type=jnp.float32)
        * score_scale
    )


def branch_stats(query_heads, key_heads, value_heads, key_valid, score_scale):
    peak_list, total_list, sum_list = ([], [], [])
    for first_head, last_head in head_ranges(query_heads.shape[0]):
        raw_scores = scores_of(
            query_heads[first_head:last_head], key_heads[first_head:last_head], score_scale
        )
        key_keep = key_valid[first_head:last_head][:, None, :]
        masked = jnp.where(key_keep, raw_scores, NEGATIVE_FILL)
        row_peak = jnp.max(masked, axis=2)
        weights = jnp.where(key_keep, jnp.exp(masked - row_peak[:, :, None]), 0.0)
        peak_list.append(row_peak)
        total_list.append(jnp.sum(weights, axis=2))
        sum_list.append(
            jnp.einsum(
                "hqk,hdk->hdq",
                weights.astype(jnp.bfloat16),
                value_heads[first_head:last_head],
                preferred_element_type=jnp.float32,
            )
        )
    return (
        jnp.concatenate(peak_list, axis=0),
        jnp.concatenate(total_list, axis=0),
        jnp.concatenate(sum_list, axis=0),
    )


def branch_grads(
    query_heads,
    key_heads,
    value_heads,
    cotan_heads,
    log_norm,
    out_dot,
    key_valid,
    score_scale,
    want_query,
    want_keys,
):
    query_list, key_list, value_list = ([], [], [])
    for first_head, last_head in head_ranges(query_heads.shape[0]):
        query_block = query_heads[first_head:last_head]
        key_block = key_heads[first_head:last_head]
        cotan_block = cotan_heads[first_head:last_head]
        raw_scores = scores_of(query_block, key_block, score_scale)
        key_keep = key_valid[first_head:last_head][:, None, :]
        weights = jnp.where(
            key_keep, jnp.exp(raw_scores - log_norm[first_head:last_head][:, :, None]), 0.0
        )
        weight_grads = jnp.einsum(
            "hdq,hdk->hqk",
            cotan_block,
            value_heads[first_head:last_head],
            preferred_element_type=jnp.float32,
        )
        low_grads = (weights * (weight_grads - out_dot[first_head:last_head][:, :, None])).astype(
            jnp.bfloat16
        )
        if want_query:
            query_list.append(
                score_scale
                * jnp.einsum(
                    "hqk,hdk->hdq", low_grads, key_block, preferred_element_type=jnp.float32
                )
            )
        if want_keys:
            key_list.append(
                score_scale
                * jnp.einsum(
                    "hqk,hdq->hdk", low_grads, query_block, preferred_element_type=jnp.float32
                )
            )
            value_list.append(
                jnp.einsum(
                    "hqk,hdq->hdk",
                    weights.astype(jnp.bfloat16),
                    cotan_block,
                    preferred_element_type=jnp.float32,
                )
            )
    query_part = jnp.concatenate(query_list, axis=0) if want_query else None
    key_part = jnp.concatenate(key_list, axis=0) if want_keys else None
    value_part = jnp.concatenate(value_list, axis=0) if want_keys else None
    return (query_part, key_part, value_part)


def head_offsets(head_total, stride):
    return np.arange(head_total) * stride // head_total


def select_rows(array_in, stride):
    head_total = array_in.shape[0]
    offsets = head_offsets(head_total, stride)
    folded = array_in.reshape(array_in.shape[:-1] + (array_in.shape[-1] // stride, stride))
    return jnp.stack(
        [folded[head_index, ..., int(offsets[head_index])] for head_index in range(head_total)]
    )


def spread_rows(array_in, stride, fill_value):
    head_total = array_in.shape[0]
    chosen = np.arange(stride)[None, :] == head_offsets(head_total, stride)[:, None]
    chosen = chosen.reshape((head_total,) + (1,) * (array_in.ndim - 1) + (stride,))
    full = jnp.where(chosen, array_in[..., None], fill_value)
    return full.reshape(array_in.shape[:-1] + (array_in.shape[-1] * stride,))


def to_heads(flat_in):
    return jnp.transpose(flat_in.reshape(flat_in.shape[0], HEADS, -1), (1, 2, 0))


def to_flat(heads_in):
    return jnp.transpose(heads_in, (2, 0, 1)).reshape(heads_in.shape[2], -1)


def local(query_tiles, key_tiles, value_tiles, cotangent, row_lengths):
    tile_count = query_tiles.shape[0]
    score_scale = HEAD ** (-0.5)
    query_heads = to_heads(query_tiles)
    key_heads = to_heads(key_tiles)
    value_heads = to_heads(value_tiles)
    cotan_heads = to_heads(cotangent)
    tile_slot = jnp.arange(tile_count, dtype=jnp.int32)
    tile_valid = tile_slot % ROW < jnp.repeat(row_lengths, ROW, total_repeat_length=tile_count)
    valid_heads = jnp.broadcast_to(tile_valid[None, :], (HEADS, tile_count))
    group_query = select_rows(query_heads, STRIDE_GROUP)
    group_key = select_rows(key_heads, STRIDE_GROUP)
    group_value = select_rows(value_heads, STRIDE_GROUP)
    group_cotan = select_rows(cotan_heads, STRIDE_GROUP)
    group_valid = select_rows(valid_heads, STRIDE_GROUP)
    group_flag = group_valid.astype(jnp.bfloat16)[:, None, :]
    slide_query = select_rows(query_heads, STRIDE_SLIDE)
    slide_key = select_rows(key_heads, STRIDE_SLIDE)
    slide_value = select_rows(value_heads, STRIDE_SLIDE)
    slide_flag = select_rows(valid_heads, STRIDE_SLIDE).astype(jnp.bfloat16)[:, None, :]
    owned_query, owned_key, owned_value, owned_flag = (
        lax.all_to_all(slide_query, "outer", split_axis=0, concat_axis=2, tiled=True),
        lax.all_to_all(slide_key, "outer", split_axis=0, concat_axis=2, tiled=True),
        lax.all_to_all(slide_value, "outer", split_axis=0, concat_axis=2, tiled=True),
        lax.all_to_all(slide_flag, "outer", split_axis=0, concat_axis=2, tiled=True),
    )
    got_group = (
        lax.all_gather(group_key, "inner", axis=2, tiled=True),
        lax.all_gather(group_value, "inner", axis=2, tiled=True),
        lax.all_gather(group_flag, "inner", axis=2, tiled=True),
    )
    got_slide = (
        lax.all_gather(owned_key, "inner", axis=2, tiled=True),
        lax.all_gather(owned_value, "inner", axis=2, tiled=True),
        lax.all_gather(owned_flag, "inner", axis=2, tiled=True),
    )
    near_peak, near_total, near_sum = branch_stats(
        query_heads, key_heads, value_heads, valid_heads, score_scale
    )
    remote_group_key = got_group[0]
    remote_group_value = got_group[1]
    remote_group_valid = got_group[2][:, 0, :] > 0.5
    group_peak, group_total, group_sum = branch_stats(
        group_query, remote_group_key, remote_group_value, remote_group_valid, score_scale
    )
    slide_all_key = got_slide[0]
    slide_all_value = got_slide[1]
    slide_all_valid = got_slide[2][:, 0, :] > 0.5
    owner_peak, owner_total, owner_sum = branch_stats(
        owned_query, slide_all_key, slide_all_value, slide_all_valid, score_scale
    )
    slide_peak, slide_total, slide_sum = (
        lax.all_to_all(owner_peak[:, None, :], "outer", split_axis=2, concat_axis=0, tiled=True),
        lax.all_to_all(owner_total[:, None, :], "outer", split_axis=2, concat_axis=0, tiled=True),
        lax.all_to_all(owner_sum, "outer", split_axis=2, concat_axis=0, tiled=True),
    )
    slide_peak = slide_peak[:, 0, :]
    slide_total = slide_total[:, 0, :]
    group_peak_full = spread_rows(group_peak, STRIDE_GROUP, NEGATIVE_FILL)
    slide_peak_full = spread_rows(slide_peak, STRIDE_SLIDE, NEGATIVE_FILL)
    best_peak = jnp.maximum(jnp.maximum(near_peak, group_peak_full), slide_peak_full)
    near_weight = jnp.exp(near_peak - best_peak)
    group_weight = jnp.exp(group_peak_full - best_peak)
    slide_weight = jnp.exp(slide_peak_full - best_peak)
    denominator = (
        near_total * near_weight
        + spread_rows(group_total, STRIDE_GROUP, 0.0) * group_weight
        + spread_rows(slide_total, STRIDE_SLIDE, 0.0) * slide_weight
    )
    numerator = (
        near_sum * near_weight[:, None, :]
        + spread_rows(group_sum, STRIDE_GROUP, 0.0) * group_weight[:, None, :]
        + spread_rows(slide_sum, STRIDE_SLIDE, 0.0) * slide_weight[:, None, :]
    )
    attended = (numerator / denominator[:, None, :]).astype(jnp.bfloat16)
    log_norm = best_peak + jnp.log(denominator)
    out_dot = jnp.sum(cotan_heads.astype(jnp.float32) * attended.astype(jnp.float32), axis=1)
    near_query, near_key, near_value = branch_grads(
        query_heads,
        key_heads,
        value_heads,
        cotan_heads,
        log_norm,
        out_dot,
        valid_heads,
        score_scale,
        True,
        True,
    )
    group_lse = select_rows(log_norm, STRIDE_GROUP)
    group_dot = select_rows(out_dot, STRIDE_GROUP)
    group_query_grad = branch_grads(
        group_query,
        remote_group_key,
        remote_group_value,
        group_cotan,
        group_lse,
        group_dot,
        remote_group_valid,
        score_scale,
        True,
        False,
    )[0]
    got_group_rows = (
        lax.all_gather(group_query, "inner", axis=2, tiled=True),
        lax.all_gather(group_cotan, "inner", axis=2, tiled=True),
    )
    got_group_stats = (
        lax.all_gather(group_lse, "inner", axis=1, tiled=True),
        lax.all_gather(group_dot, "inner", axis=1, tiled=True),
    )
    unused_group, group_key_grad, group_value_grad = branch_grads(
        got_group_rows[0],
        group_key,
        group_value,
        got_group_rows[1],
        got_group_stats[0],
        got_group_stats[1],
        group_valid,
        score_scale,
        False,
        True,
    )
    slide_cotan = select_rows(cotan_heads, STRIDE_SLIDE)
    slide_lse = select_rows(log_norm, STRIDE_SLIDE)
    slide_dot = select_rows(out_dot, STRIDE_SLIDE)
    owned_cotan = lax.all_to_all(slide_cotan, "outer", split_axis=0, concat_axis=2, tiled=True)
    owned_lse, owned_dot = (
        lax.all_to_all(slide_lse, "outer", split_axis=0, concat_axis=1, tiled=True),
        lax.all_to_all(slide_dot, "outer", split_axis=0, concat_axis=1, tiled=True),
    )
    owned_query_grad, partial_key, partial_value = branch_grads(
        owned_query,
        slide_all_key,
        slide_all_value,
        owned_cotan,
        owned_lse,
        owned_dot,
        slide_all_valid,
        score_scale,
        True,
        True,
    )
    owned_key_grad, owned_value_grad = (
        lax.psum_scatter(
            partial_key.astype(jnp.bfloat16), "inner", scatter_dimension=2, tiled=True
        ).astype(jnp.float32),
        lax.psum_scatter(
            partial_value.astype(jnp.bfloat16), "inner", scatter_dimension=2, tiled=True
        ).astype(jnp.float32),
    )
    slide_query_grad, slide_key_grad, slide_value_grad = (
        lax.all_to_all(
            as_sent(owned_query_grad), "outer", split_axis=2, concat_axis=0, tiled=True
        ).astype(owned_query_grad.dtype),
        lax.all_to_all(
            owned_key_grad.astype(jnp.bfloat16), "outer", split_axis=2, concat_axis=0, tiled=True
        ).astype(owned_key_grad.dtype),
        lax.all_to_all(
            owned_value_grad.astype(jnp.bfloat16), "outer", split_axis=2, concat_axis=0, tiled=True
        ).astype(owned_value_grad.dtype),
    )
    query_grad = (
        near_query
        + spread_rows(group_query_grad, STRIDE_GROUP, 0.0)
        + spread_rows(slide_query_grad, STRIDE_SLIDE, 0.0)
    )
    key_grad = (
        near_key
        + spread_rows(group_key_grad, STRIDE_GROUP, 0.0)
        + spread_rows(slide_key_grad, STRIDE_SLIDE, 0.0)
    )
    value_grad = (
        near_value
        + spread_rows(group_value_grad, STRIDE_GROUP, 0.0)
        + spread_rows(slide_value_grad, STRIDE_SLIDE, 0.0)
    )
    return (
        to_flat(attended),
        to_flat(query_grad.astype(jnp.bfloat16)),
        to_flat(key_grad.astype(jnp.bfloat16)),
        to_flat(value_grad.astype(jnp.bfloat16)),
    )


BF = jnp.bfloat16
F32 = jnp.float32
LANES = 128
SCALE = HEAD ** (-0.5)
PAIR = 2 * HEAD
PAIRS = HEADS // 2
MESH = pl.DeviceIdType.MESH


def iota2(shape, axis):
    return lax.broadcasted_iota(jnp.int32, shape, axis)


def original_tile(j):
    return (j & 7) * 16 + ((j >> 3) & 3) * 4 + (j >> 5)


def permute_matrix(inverse):
    shape = (LANES, LANES)
    j, i = (iota2(shape, 1), iota2(shape, 0)) if inverse else (iota2(shape, 0), iota2(shape, 1))
    return (original_tile(j) == i).astype(F32).astype(BF)


def identity(size):
    shape = (size, size)
    return (iota2(shape, 0) == iota2(shape, 1)).astype(F32).astype(BF)


def key_bias(len_ref):
    tile = original_tile(iota2((LANES, LANES), 0))
    row = tile >> 5
    length = jnp.full((LANES, LANES), len_ref[0], jnp.int32)
    for index in range(1, 4):
        length = jnp.where(row == index, len_ref[index], length)
    return jnp.where((tile & 31) < length, 0.0, NEGATIVE_FILL).astype(F32)


def mm(a, b):
    return jnp.dot(a, b, preferred_element_type=F32)


def mm_t(a, b):
    return lax.dot_general(a, b, (((1,), (1,)), ((), ())), preferred_element_type=F32)


def slide_row(r):
    return (r % 4) * 32 + (r // 4) * 8


def head_lanes(lane, p, e):
    return ((lane - (PAIR * p + HEAD * e)) & (LANES - 1)) < HEAD


def flag_lane(p):
    return (PAIR * (p + 1)) & (LANES - 1)


def as_mask(keep):
    return keep.astype(F32).astype(BF)


def head_masks(p):
    lane = iota2((1, LANES), 1)
    masks = [as_mask(head_lanes(lane, p, e)) for e in range(2)]
    flags = [as_mask(lane == flag_lane(p) + e) for e in range(3)]
    return masks, flags


def two_heads(x, masks, flags=None):
    parts = [x * masks[e] for e in range(2)]
    if flags is not None:
        parts = [part + flag for part, flag in zip(parts, flags)]
    return jnp.concatenate(parts, axis=0)


def pieces_of(p):
    base, spot = p // 4 * 3, p % 4
    if spot == 0:
        return [(base, 0, 96)]
    if spot == 1:
        return [(base, 96, 128), (base + 1, 0, 64)]
    if spot == 2:
        return [(base + 1, 64, 128), (base + 2, 0, 32)]
    return [(base + 2, 32, 128)]


def pair_tile(x, p):
    parts = pieces_of(p)
    tiles = [x[:, t * LANES : (t + 1) * LANES] for t, _, _ in parts]
    if len(tiles) == 1:
        return tiles[0]
    lane = iota2(tiles[0].shape, 1)
    return jnp.where(lane >= parts[0][1], tiles[0], tiles[1])


K_ROW, Q_ROW, V_ROW, S_ROW, G_ROWS = 0, 32, 64, 96, 112


def free_lanes(lane, p):
    return ((lane - flag_lane(p)) & (LANES - 1)) < 32


def packed(x, spare, part, p):
    moved = pltpu.roll(spare, 32 * (3 - part), 1)
    return jnp.where(free_lanes(iota2(x.shape, 1), p), moved, x)


def unpack_matrix(p):
    row, col = iota2((3 * LANES, LANES), 0), iota2((3 * LANES, LANES), 1)
    lane = row & (LANES - 1)
    target = (lane - 32 * (3 - (row >> 7))) & (LANES - 1)
    return as_mask(free_lanes(lane, p) & (target == col))


def prep_pair(x, p, bias=None):
    tile = pair_tile(x, p)
    lane = iota2(tile.shape, 1)
    flag = flag_lane(p)
    if bias is not None:
        tile = jnp.where((lane == flag) | (lane == flag + 1), bias, tile)
    first, second = [tile[slide_row(2 * p + e) :][:8] for e in range(2)]
    lane = iota2(first.shape, 1)
    slide = jnp.where(head_lanes(lane, p, 1) | (lane == flag + 1), second, first)
    return tile, slide


def near_early(p, tp_ref, pn_ref, ad_ref, kt_ref, vt_ref, eye):
    k, q, v, c = [tp_ref[a, p] for a in range(4)]
    masks, flags = head_masks(p)
    s = mm_t(k, two_heads(q, masks, flags)) * SCALE
    dp = mm_t(v, two_heads(c, masks))
    kt_ref[p] = mm_t(eye, two_heads(k, masks)).astype(BF)
    vt_ref[p] = mm_t(eye, two_heads(v, masks)).astype(BF)
    peak = jnp.max(s, axis=0, keepdims=True)
    weights = jnp.exp(s - peak)
    total = jnp.sum(weights, axis=0, keepdims=True)
    weights = weights * (1.0 / total)
    delta = jnp.sum(weights * dp, axis=0, keepdims=True)
    pn_ref[p] = weights
    ad_ref[p] = weights * (dp - delta)
    return peak + jnp.log(total), delta


def turn(x, shift):
    return pltpu.roll(x, shift & (LANES - 1), 1)


def near_stats(p, me, lse, delta):
    shape = (8, LANES)
    row, lane = iota2(shape, 0), iota2(shape, 1)

    def wide(x, e):
        return jnp.broadcast_to(x[:, e * LANES : (e + 1) * LANES], shape)

    high = row < 4
    heads = [jnp.where(high, wide(lse, e), wide(delta, e)) for e in range(2)]
    group = turn(jnp.where((row & 3) == 0, heads[0], heads[1]), ((me & 3) - p // 2) * 32)
    spots = [turn(heads[e], e * 64 + me * 8 - slide_row(2 * p + e)) for e in range(2)]
    slide = jnp.where(lane < 64, spots[0], spots[1])
    return jnp.where((row & 3) == 2, slide, group)


def near_late(p, me, r2_ref, tp_ref, pn_ref, ad_ref, kt_ref, vt_ref, late_ref, turned_ref):
    tile = r2_ref[p]
    lane = iota2((1, LANES), 1)
    start = p // 2 * 32
    group = turn(tile, start - (me & 3) * 32)
    in_group = (lane >= start) & (lane < start + 32)
    scales, shifts = [], []
    for e in range(2):
        at = slide_row(2 * p + e)
        slide = turn(tile, at - e * 64 - me * 8)
        in_slide = (lane >= at) & (lane < at + 8)
        for index, (found, fill) in enumerate(((scales, 1.0), (shifts, 0.0))):
            value = jnp.where(in_slide, slide[4 * index + 2 : 4 * index + 3], fill)
            found.append(jnp.where(in_group, group[4 * index + e : 4 * index + e + 1], value))
    scale = jnp.concatenate(scales, axis=1)
    shift = jnp.concatenate(shifts, axis=1)
    weights = pn_ref[p]
    low = (weights * scale).astype(BF)
    grads = (ad_ref[p] * (scale * SCALE) - weights * (scale * shift * SCALE)).astype(BF)
    masks, _ = head_masks(p)
    late_ref[0, p] = mm(grads, two_heads(tp_ref[1, p], masks))
    late_ref[1, p] = mm(low, two_heads(tp_ref[3, p], masks))

    def stacked(x):
        return jnp.concatenate([x[:, :LANES], x[:, LANES:]], axis=0)

    for index, value in enumerate((mm(vt_ref[p], stacked(low)), mm(kt_ref[p], stacked(grads)))):
        value = value.astype(BF)
        for t, first, last in pieces_of(p):
            turned_ref[index, t * LANES + first : t * LANES + last] = value[first:last]


def branch(s):
    peak = jnp.max(s, axis=0, keepdims=True)
    weights = jnp.exp(s - peak)
    total = jnp.sum(weights, axis=0, keepdims=True)
    return weights, peak, total, peak + jnp.log(total)


def rows_of(row, first, second, third):
    first, second, third = [jnp.broadcast_to(x, row.shape) for x in (first, second, third)]
    return jnp.where(row == 0, first, jnp.where(row == 1, second, third))


def slide_scores(masks, flags, gr_ref, skv_ref):
    kv = skv_ref[...].reshape(-1, LANES)
    sources = gr_ref.shape[0]
    wide = gr_ref[:, S_ROW:G_ROWS].astype(F32)
    q, c = [wide[:, a : a + 8].reshape(sources * 8, LANES).astype(BF) for a in (0, 8)]
    q2, c2 = two_heads(q, masks, flags), two_heads(c, masks)
    both = mm_t(kv, jnp.concatenate([q2, c2], axis=0)).reshape(-1, 16, 2 * LANES)
    s = both[:, 0:8, :LANES].reshape(-1, LANES) * SCALE
    dp = both[:, 8:16, LANES:].reshape(-1, LANES)
    return kv, q2, c2, s, dp


def near_of(row, lane, ns_ref):
    slide = ns_ref[0]
    for source in range(1, 8):
        slide = jnp.where(((lane & 63) >> 3) == source, ns_ref[source], slide)
    found = []
    for j in range(2):
        group = ns_ref[4 * j]
        for q in range(1, 4):
            group = jnp.where((lane >> 5) == q, ns_ref[4 * j + q], group)
        both = jnp.where((row & 3) == 2, slide, group)
        found.append((both, pltpu.roll(both, 4, 0)))
    return found


def crossed(row, lane, p, slide, group, fill):
    first = lax.rem(2 * p, 5) == 0
    second = lax.rem(2 * p + 1, 5) == 0
    e = jnp.where(second, 1, 0)
    any_head = jnp.logical_or(first, second)
    at = p // 2 * 8
    source = jnp.broadcast_to(slide, row.shape)
    found, to_slide = [], None
    for j in range(2):
        pair = [jnp.broadcast_to(group[2 * head + j], row.shape) for head in range(2)]
        chosen = jnp.where(second, pair[1], pair[0])
        to_group = None
        for q in range(4):
            here, there = q * 32 + at, (4 * j + q) * 8 + e * 64
            moved = turn(source, here - there + LANES)
            to_group = moved if q == 0 else jnp.where((lane >> 5) == q, moved, to_group)
            moved = turn(chosen, there - here + LANES)
            same = ((lane & 63) >> 3) == 4 * j + q
            to_slide = moved if to_slide is None else jnp.where(same, moved, to_slide)
        found.append(to_group)
    in_group = (row == e) & ((lane & 31) >> 3 == p // 2) & any_head
    in_slide = (row == 2) & ((lane >> 6) == e) & any_head
    return [
        jnp.where(in_group | in_slide, jnp.where(row == 2, to_slide, to_group), fill)
        for to_group in found
    ]


class Exchange:
    def __init__(self, count, make, every):
        self.count, self.make, self.every = count, make, every

    def start(self):
        @pl.loop(1, self.count)
        def _(step):
            self.make(step).start()

    def wait_recv(self):
        self.every.wait_recv()

    def wait_send(self):
        self.every.wait_send()


def wrapped(value, count):
    return jnp.where(value >= count, value - count, value)


def whole_kernel(
    inner, outers, len_hbm, q_hbm, k_hbm, v_hbm, c_hbm, turned, acc,
    len_ref, loaded, load_sem, tp, gm, gr, skv_s, skv, pn, ad, kt, vt, ns_s, ns_r, r2_s, r2_r,
    r4_s, r4_r, xs, xr, sg_s, sg_r, late, send_sem, recv_sem, x_send, x_recv,
):
    outer, me = lax.axis_index("outer"), lax.axis_index("inner")
    p = me

    def scope(name):
        return jax.named_scope(name)

    def copy_to(src, dst, sems, index, device):
        return pltpu.make_async_remote_copy(
            src_ref=src,
            dst_ref=dst,
            send_sem=sems[0].at[index],
            recv_sem=sems[1].at[index],
            device_id=device,
            device_id_type=MESH,
        )

    def exchange(index, source, target, size):
        sems, next_place = (send_sem, recv_sem), wrapped(me + 1, inner)

        def make(step):
            peer = wrapped(me + step, inner)
            return copy_to(source(peer), target(me), sems, index, (outer, peer))

        return Exchange(inner, make, copy_to(size, size, sems, index, (outer, next_place)))

    def across(index, source, target, size):
        sems, next_place = (x_send, x_recv), wrapped(outer + 1, outers)

        def make(step):
            peer = wrapped(outer + step, outers)
            return copy_to(source(peer), target, sems, index, (peer, me))

        return Exchange(outers, make, copy_to(size, size, sems, index, (next_place, me)))

    def blocks_exchange(index, src, dst):
        size = dst.at[pl.ds(0, inner - 1)]
        return exchange(index, lambda peer: src.at[peer], lambda mine: dst.at[mine], size)

    def rows_exchange(index, src, dst, first, last):
        rows = pl.ds(first, last - first)
        size = dst.at[pl.ds(0, inner - 1), rows]
        return exchange(index, lambda peer: src.at[peer, rows], lambda mine: dst.at[mine, rows], size)

    some = pl.ds(0, inner - 1)
    send_skv = exchange(
        0, lambda peer: skv_s.at[peer], lambda mine: skv.at[outer, mine], skv.at[0, some]
    )
    send_kq = rows_exchange(1, gm, gr, K_ROW, V_ROW)
    send_vs = rows_exchange(2, gm, gr, V_ROW, G_ROWS)
    send_ns = blocks_exchange(3, ns_s, ns_r)
    send_r2 = exchange(4, lambda peer: r2_s.at[peer >> 2], lambda mine: r2_r.at[mine], r2_r.at[some])
    send_o = rows_exchange(5, r4_s, r4_r, K_ROW, Q_ROW)
    send_dq = rows_exchange(6, r4_s, r4_r, Q_ROW, V_ROW)
    send_dk = rows_exchange(7, r4_s, r4_r, V_ROW, S_ROW)
    send_oq = rows_exchange(8, r4_s, r4_r, S_ROW, G_ROWS)
    send_sg = blocks_exchange(9, sg_s, sg_r)
    forward = across(0, lambda peer: skv.at[outer], skv.at[outer], skv.at[pl.ds(0, outers - 1)])
    backward = across(1, lambda peer: xs.at[peer], xr.at[outer], xr.at[pl.ds(0, outers - 1)])

    barrier = pltpu.get_barrier_semaphore()
    with scope("load_start"):
        loads = [
            pltpu.make_async_copy(ref, loaded.at[a], load_sem.at[a])
            for a, ref in enumerate((k_hbm, q_hbm, v_hbm, c_hbm))
        ]
        loads.append(pltpu.make_async_copy(len_hbm, len_ref, load_sem.at[4]))
        for index in (4, 0, 2, 1, 3):
            loads[index].start()
    with scope("greet"):

        @pl.loop(1, inner)
        def _(step):
            pl.semaphore_signal(
                barrier, inc=1, device_id=(outer, wrapped(me + step, inner)), device_id_type=MESH
            )

        @pl.loop(1, outers)
        def _(step):
            pl.semaphore_signal(
                barrier, inc=1, device_id=(wrapped(outer + step, outers), me), device_id_type=MESH
            )

    perm = permute_matrix(False)
    eye = identity(LANES)
    with scope("load_wait"):
        loads[4].wait()
        loads[0].wait()
        loads[2].wait()
    with scope("prep_kv"):
        bias = key_bias(len_ref)
        xk = mm(perm, loaded[0])
        xv = mm(perm, loaded[2])
        groups = []
        for h in range(PAIRS):
            first = h // 2 * 32
            rows = slice(first, first + 32)
            tile, key_slide = prep_pair(xk, h, bias)
            tp[0, h] = tile.astype(BF)
            groups.append([tile[rows]])
            tile, value_slide = prep_pair(xv, h)
            tp[2, h] = tile.astype(BF)
            groups[h].append(tile[rows])
            both = jnp.concatenate([key_slide, value_slide], axis=0)
            lane = iota2(both.shape, 1)
            for index in range(2):
                part = bias[first + 16 * index : first + 16 * index + 16]
                both = jnp.where(lane == flag_lane(h) + 2 + index, part, both)
            skv_s[h] = both.astype(BF)
    with scope("barrier_wait"):
        pl.semaphore_wait(barrier, inner - 1 + outers - 1)
    with scope("send_skv"):
        send_skv.start()
        skv[outer, me] = skv_s[me]
    with scope("prep_qc"):
        loads[1].wait()
        loads[3].wait()
        xq = mm(perm, loaded[1])
        xc = mm(perm, loaded[3])
        for h in range(PAIRS):
            rows = slice(h // 2 * 32, h // 2 * 32 + 32)
            tile, query_slide = prep_pair(xq, h)
            tp[1, h] = tile.astype(BF)
            query = tile[rows]
            tile, cotan_slide = prep_pair(xc, h)
            tp[3, h] = tile.astype(BF)
            for index, value in enumerate((groups[h][0], query, groups[h][1])):
                gm[h, 32 * index : 32 * index + 32] = packed(value, tile[rows], index, h).astype(BF)
            gm[h, S_ROW:G_ROWS] = jnp.concatenate([query_slide, cotan_slide], axis=0).astype(BF)
    with scope("send_group"):
        send_kq.start()
        send_vs.start()
        gr[me] = gm[me]
    with scope("near_early"):
        for h in range(PAIRS):
            lse, delta = near_early(h, tp, pn, ad, kt, vt, eye)
            ns_s[h] = near_stats(h, me, lse, delta)
    with scope("send_ns"):
        send_ns.start()
        ns_r[me] = ns_s[me]
    with scope("skv_wait"):
        send_skv.wait_recv()
    with scope("forward"):
        forward.start()
    masks, flags = head_masks(p)
    row, lane = iota2((8, LANES), 0), iota2((8, LANES), 1)
    eye2 = identity(2 * LANES)

    def members(at):
        return gr[:, at : at + 32].reshape(inner * 32, LANES)

    def part(index):
        return slice(index * LANES, (index + 1) * LANES)

    free = free_lanes(iota2((1, LANES), 1), p)
    pair_mask = masks[0] + masks[1]
    unpack = unpack_matrix(p)
    with scope("kq_wait"):
        near_keys = skv[outer].astype(F32)
        near_keys = jnp.concatenate([near_keys, pltpu.roll(near_keys, LANES - 1, 2)], axis=1)
        group_bias = near_keys.reshape(inner * 32, LANES).astype(BF) * flags[2]
        send_kq.wait_recv()
    with scope("group_scores"):
        packed_k, packed_q = members(K_ROW), members(Q_ROW)
        k = packed_k * pair_mask + group_bias
        q2 = two_heads(packed_q, masks, [flags[2]] * 2)
        chunks = [branch(mm_t(k, q2[part(index)]) * SCALE) for index in range(4)]
        kt2 = mm_t(eye, two_heads(k, masks)).astype(BF)
    with scope("vs_wait"):
        send_vs.wait_recv()
    with scope("group_dp"):
        v = members(V_ROW)
        c = mm(jnp.concatenate([packed_k, packed_q, v], axis=1), unpack).astype(BF)
        c2 = two_heads(c, masks)
        vt2 = mm_t(eye, two_heads(v, masks)).astype(BF)
        dps, group_deltas = [], []
        for index, (weights, _, total, _) in enumerate(chunks):
            dps.append(mm_t(v, c2[part(index)]))
            group_deltas.append(jnp.sum(weights * dps[-1], axis=0, keepdims=True) / total)
    with scope("forward_wait"):
        forward.wait_recv()
    with scope("slide_scores"):
        skv_all, qs2, cs2, s, slide_dp = slide_scores(masks, flags, gr, skv)
        slide_weights, slide_peak, slide_total, slide_lse = branch(s)
        slide_delta = jnp.sum(slide_weights * slide_dp, axis=0, keepdims=True) / slide_total
        skv_t = mm_t(eye, skv_all).astype(BF)
    with scope("ns_wait"):
        send_ns.wait_recv()
    with scope("merge_lse"):
        near = near_of(row, lane, ns_r)
        other = crossed(row, lane, p, slide_lse, [chunk[3] for chunk in chunks], NEGATIVE_FILL)
        factors, shares = [], []
        for j in range(2):
            own = rows_of(row, chunks[j][3], chunks[2 + j][3], slide_lse)
            peak = rows_of(row, chunks[j][1], chunks[2 + j][1], slide_peak)
            best = jnp.maximum(jnp.maximum(near[j][0], own), other[j])
            parts = [jnp.exp(x - best) for x in (near[j][0], own, other[j])]
            total = parts[0] + parts[1] + parts[2]
            inverse = 1.0 / total
            factors.append(jnp.exp(peak - best - jnp.log(total)))
            shares.append([x * inverse for x in parts])
        lows = []
        for index, chunk in enumerate(chunks):
            e, j = divmod(index, 2)
            lows.append((chunk[0] * factors[j][e : e + 1]).astype(BF))
    with scope("merge_delta"):
        other = crossed(row, lane, p, slide_delta, group_deltas, 0.0)
        deltas = []
        for j in range(2):
            own = rows_of(row, group_deltas[j], group_deltas[2 + j], slide_delta)
            share = shares[j]
            deltas.append(share[0] * near[j][1] + share[1] * own + share[2] * other[j])
            r2_s[j] = jnp.where(row < 4, share[0], pltpu.roll(deltas[j] - near[j][1], 4, 0))

    def turned_sum(wide, parts):
        both = [jnp.concatenate(parts[2 * e : 2 * e + 2], axis=1) for e in range(2)]
        value = mm(wide, jnp.concatenate(both, axis=0)).astype(BF)
        return mm_t(eye2, value)

    def put(at, value, index):
        value = packed(value, value_grads, index, p).astype(BF)
        r4_s[:, at : at + 32] = value.reshape(inner, 32, LANES)

    with scope("group_out"):
        value_grads = mm(jnp.concatenate(lows, axis=1), c2)
        put(K_ROW, turned_sum(vt2, lows), 0)
    with scope("send_o"):
        send_o.start()
    with scope("slide_bwd"):
        weights = slide_weights * factors[0][2:3]
        grads = weights * (slide_dp - deltas[0][2:3]) * SCALE
        blocks = [x.reshape(-1, 8, LANES) for x in (grads, weights)]
        empty = jnp.zeros_like(blocks[0])
        mixed = jnp.concatenate(
            [
                jnp.concatenate([blocks[0], empty], axis=2),
                jnp.concatenate([empty, blocks[1]], axis=2),
            ],
            axis=1,
        )
        mixed = mixed.reshape(-1, 2 * LANES).astype(BF)
        xs[...] = mm(mixed, jnp.concatenate([qs2, cs2], axis=0)).astype(BF).reshape(xs.shape)
    with scope("send_x"):
        backward.start()
    with scope("send_r2"):
        send_r2.start()
        r2_r[me] = r2_s[me >> 2]
    with scope("group_dq"):
        grads = []
        for index, (weights, _, _, _) in enumerate(chunks):
            e, j = divmod(index, 2)
            weights = weights * factors[j][e : e + 1]
            grads.append((weights * (dps[index] - deltas[j][e : e + 1]) * SCALE).astype(BF))
        put(Q_ROW, turned_sum(kt2, grads), 1)
    with scope("send_dq"):
        send_dq.start()
    with scope("group_dk"):
        put(V_ROW, mm(jnp.concatenate(grads, axis=1), q2), 2)
    with scope("send_dk"):
        send_dk.start()
    with scope("slide_q"):
        both = mm_t(eye2, mm(skv_t, mixed).astype(BF))
        quarter = LANES // 2
        head0 = head_lanes(iota2((quarter, LANES), 1), p, 0)
        query = jnp.where(head0, both[0:quarter], both[quarter:LANES])
        out = jnp.where(head0, both[LANES : 3 * quarter], both[3 * quarter : 4 * quarter])
        blocks = [x.reshape(inner, 8, LANES) for x in (out, query)]
        r4_s[:, S_ROW:G_ROWS] = jnp.concatenate(blocks, axis=1).astype(BF)
    with scope("send_oq"):
        send_oq.start()
        r4_r[me] = r4_s[me]
    with scope("clear"):
        acc[0:2] = jnp.zeros((2,) + acc.shape[1:], F32)
    with scope("x_wait"):
        backward.wait_recv()
    with scope("x_sum"):
        total = xs[outer].astype(F32)
        for step in range(1, outers):
            total = total + xr[wrapped(outer + step, outers)].astype(F32)
        sg_s[...] = total.astype(BF)
    with scope("send_sg"):
        send_sg.start()
        sg_r[me] = sg_s[me]
    with scope("r2_wait"):
        send_r2.wait_recv()
    with scope("near_late1"):
        for h in range(PAIRS):
            near_late(h, me, r2_r, tp, pn, ad, kt, vt, late, turned)
    with scope("collect"):
        for a in range(2):
            for t in range(D_TILES):
                value = None
                for h in range(PAIRS):
                    for tile, first, last in pieces_of(h):
                        if tile == t:
                            piece = late[a, h]
                            lane_full = iota2(piece.shape, 1)
                            value = piece if value is None else jnp.where(lane_full >= first, piece, value)
                acc[2 + a, :, t * LANES : (t + 1) * LANES] = value
    with scope("drain"):
        for sent in (send_skv, send_kq, send_vs, send_ns, forward, send_r2, backward):
            sent.wait_send()
    for name, sent, out, part_index in (("o", send_o, 0, 0), ("dq", send_dq, 1, 1), ("dk", send_dk, 2, 2)):
        with scope(name + "_wait"):
            sent.wait_recv()
        with scope(name + "_add"):
            for h in range(PAIRS):
                add_group(acc, out, part_index, h, r4_r[h, 32 * part_index : 32 * part_index + 32])
    with scope("oq_wait"):
        send_oq.wait_recv()
    with scope("oq_add"):
        for h in range(PAIRS):
            add_slide(acc, (0, 1), h, r4_r[h, S_ROW:G_ROWS])
    with scope("sg_wait"):
        send_sg.wait_recv()
    with scope("sg_add"):
        for h in range(PAIRS):
            add_slide(acc, (2, 3), h, sg_r[h])
    with scope("drain_last"):
        for sent in (send_o, send_dq, send_dk, send_oq, send_sg):
            sent.wait_send()


D_TILES = HEADS * HEAD // LANES


def final_kernel(turned, acc, att_hbm, dq_hbm, dk_hbm, dv_hbm, done, sems):
    back = permute_matrix(True)
    copies = []
    for a, ref in enumerate((att_hbm, dq_hbm, dk_hbm, dv_hbm)):
        value = mm(back, acc[a].astype(BF))
        if a < 2:
            value = value + mm_t(back, turned[a])
        done[a] = value.astype(BF)
        copies.append(pltpu.make_async_copy(done.at[a], ref, sems.at[a]))
        copies[-1].start()
    for copy in copies:
        copy.wait()


def add_group(acc, out, part, h, block):
    block = block.astype(F32)
    start = h // 2 * 32
    lane = iota2(block.shape, 1)
    for t, first, last in pieces_of(h):
        cols = slice(t * LANES, (t + 1) * LANES)
        keep = (lane >= first) & (lane < last)
        acc[out, start : start + 32, cols] += jnp.where(keep, block, 0.0)
    t, first = divmod(PAIR * h + 32 * part, LANES)
    keep = (lane >= first) & (lane < first + 32)
    moved = pltpu.roll(block, LANES - 32 * (3 - part), 1)
    acc[3, start : start + 32, t * LANES : (t + 1) * LANES] += jnp.where(keep, moved, 0.0)


def add_slide(acc, outs, h, block):
    block = block.astype(F32)
    lane = iota2((8, LANES), 1)
    for index, out in enumerate(outs):
        small = block[8 * index : 8 * index + 8]
        for t, first, last in pieces_of(h):
            cols = slice(t * LANES, (t + 1) * LANES)
            for e in range(2):
                at = slide_row(2 * h + e)
                keep = (lane >= first) & (lane < last) & head_lanes(lane, h, e)
                acc[out, at : at + 8, cols] += jnp.where(keep, small, 0.0)


def fast_local(inner, outers, *args):
    row_lengths, tiles_in = args[4], args[:4]
    tiles, width = tiles_in[0].shape
    vmem = pl.BlockSpec(memory_space=pltpu.VMEM)
    hbm = pl.BlockSpec(memory_space=pltpu.HBM)

    def both(shape, dtype):
        return [pltpu.VMEM(shape, dtype)] * 2

    scratch = [
        pltpu.SMEM(row_lengths.shape, jnp.int32),
        pltpu.VMEM((4, tiles, width), BF),
        pltpu.SemaphoreType.DMA((5,)),
        pltpu.VMEM((4, PAIRS, tiles, LANES), BF),
    ]
    scratch += both((inner, G_ROWS, LANES), BF)
    scratch += [pltpu.VMEM((inner, 16, LANES), BF), pltpu.VMEM((outers, inner, 16, LANES), BF)]
    scratch += both((PAIRS, tiles, 2 * LANES), F32)
    scratch += both((PAIRS, LANES, 2 * LANES), BF)
    scratch += both((inner, 8, LANES), F32)
    scratch += [pltpu.VMEM((2, 8, LANES), F32), pltpu.VMEM((inner, 8, LANES), F32)]
    scratch += both((inner, G_ROWS, LANES), BF)
    scratch += both((outers, inner, 16, LANES), BF)
    scratch += both((inner, 16, LANES), BF)
    scratch += [pltpu.VMEM((2, PAIRS, tiles, LANES), F32)]
    scratch += [pltpu.SemaphoreType.DMA((10,))] * 2 + [pltpu.SemaphoreType.DMA((2,))] * 2
    in_hbm = [pltpu.with_memory_space_constraint(x, pltpu.HBM) for x in (row_lengths, *tiles_in)]
    shapes = (((2, width, tiles), BF), ((4, tiles, width), F32))
    between = pl.pallas_call(
        lambda *refs: whole_kernel(inner, outers, *refs),
        out_shape=[pltpu.VMEM(shape, dtype) for shape, dtype in shapes],
        in_specs=[hbm] * 5,
        out_specs=[vmem] * 2,
        scratch_shapes=scratch,
        compiler_params=pltpu.CompilerParams(
            collective_id=0, has_side_effects=True, vmem_limit_bytes=32 * 1024 * 1024
        ),
    )(*in_hbm)
    return tuple(
        pl.pallas_call(
            final_kernel,
            out_shape=[pltpu.HBM((tiles, width), BF)] * 4,
            in_specs=[vmem] * 2,
            out_specs=[hbm] * 4,
            scratch_shapes=[pltpu.VMEM((4, tiles, width), BF), pltpu.SemaphoreType.DMA((4,))],
            compiler_params=pltpu.CompilerParams(vmem_limit_bytes=32 * 1024 * 1024),
        )(*between)
    )


def solution(mesh):
    in_specs = (P(("outer", "inner"), None),) * 4 + (P(("outer", "inner")),)
    out_specs = (P(("outer", "inner"), None),) * 4
    inner, outers = mesh.shape["inner"], mesh.shape["outer"]

    def step(*args):
        fits = inner == PAIRS and outers == 4
        if fits and args[0].shape == (LANES, HEADS * HEAD):
            return fast_local(inner, outers, *args)
        return local(*args)

    return jax.shard_map(step, mesh=mesh, in_specs=in_specs, out_specs=out_specs, check_vma=False)
```

```python
import jax
import jax.numpy as jnp
import numpy as np
from jax import lax
from jax.experimental import pallas as pl
from jax.experimental.pallas import tpu as pltpu
from jax.sharding import PartitionSpec as P

HEADS = 16
HEAD = 48
ROW = 32
STRIDE_GROUP = 4
STRIDE_SLIDE = 16


NEGATIVE_FILL = -1e30
heads_at_once = 4


def as_sent(value):

    def short(part):
        return part.astype(jnp.bfloat16) if part.dtype == jnp.float32 else part

    return jax.tree.map(short, value)


def head_ranges(head_total):
    step_size = min(head_total, heads_at_once)
    return [(first_head, first_head + step_size) for first_head in range(0, head_total, step_size)]


def scores_of(query_block, key_block, score_scale):
    return (
        jnp.einsum("hdq,hdk->hqk", query_block, key_block, preferred_element_type=jnp.float32)
        * score_scale
    )


def branch_stats(query_heads, key_heads, value_heads, key_valid, score_scale):
    peak_list, total_list, sum_list = ([], [], [])
    for first_head, last_head in head_ranges(query_heads.shape[0]):
        raw_scores = scores_of(
            query_heads[first_head:last_head], key_heads[first_head:last_head], score_scale
        )
        key_keep = key_valid[first_head:last_head][:, None, :]
        masked = jnp.where(key_keep, raw_scores, NEGATIVE_FILL)
        row_peak = jnp.max(masked, axis=2)
        weights = jnp.where(key_keep, jnp.exp(masked - row_peak[:, :, None]), 0.0)
        peak_list.append(row_peak)
        total_list.append(jnp.sum(weights, axis=2))
        sum_list.append(
            jnp.einsum(
                "hqk,hdk->hdq",
                weights.astype(jnp.bfloat16),
                value_heads[first_head:last_head],
                preferred_element_type=jnp.float32,
            )
        )
    return (
        jnp.concatenate(peak_list, axis=0),
        jnp.concatenate(total_list, axis=0),
        jnp.concatenate(sum_list, axis=0),
    )


def branch_grads(
    query_heads,
    key_heads,
    value_heads,
    cotan_heads,
    log_norm,
    out_dot,
    key_valid,
    score_scale,
    want_query,
    want_keys,
):
    query_list, key_list, value_list = ([], [], [])
    for first_head, last_head in head_ranges(query_heads.shape[0]):
        query_block = query_heads[first_head:last_head]
        key_block = key_heads[first_head:last_head]
        cotan_block = cotan_heads[first_head:last_head]
        raw_scores = scores_of(query_block, key_block, score_scale)
        key_keep = key_valid[first_head:last_head][:, None, :]
        weights = jnp.where(
            key_keep, jnp.exp(raw_scores - log_norm[first_head:last_head][:, :, None]), 0.0
        )
        weight_grads = jnp.einsum(
            "hdq,hdk->hqk",
            cotan_block,
            value_heads[first_head:last_head],
            preferred_element_type=jnp.float32,
        )
        low_grads = (weights * (weight_grads - out_dot[first_head:last_head][:, :, None])).astype(
            jnp.bfloat16
        )
        if want_query:
            query_list.append(
                score_scale
                * jnp.einsum(
                    "hqk,hdk->hdq", low_grads, key_block, preferred_element_type=jnp.float32
                )
            )
        if want_keys:
            key_list.append(
                score_scale
                * jnp.einsum(
                    "hqk,hdq->hdk", low_grads, query_block, preferred_element_type=jnp.float32
                )
            )
            value_list.append(
                jnp.einsum(
                    "hqk,hdq->hdk",
                    weights.astype(jnp.bfloat16),
                    cotan_block,
                    preferred_element_type=jnp.float32,
                )
            )
    query_part = jnp.concatenate(query_list, axis=0) if want_query else None
    key_part = jnp.concatenate(key_list, axis=0) if want_keys else None
    value_part = jnp.concatenate(value_list, axis=0) if want_keys else None
    return (query_part, key_part, value_part)


def head_offsets(head_total, stride):
    return np.arange(head_total) * stride // head_total


def select_rows(array_in, stride):
    head_total = array_in.shape[0]
    offsets = head_offsets(head_total, stride)
    folded = array_in.reshape(array_in.shape[:-1] + (array_in.shape[-1] // stride, stride))
    return jnp.stack(
        [folded[head_index, ..., int(offsets[head_index])] for head_index in range(head_total)]
    )


def spread_rows(array_in, stride, fill_value):
    head_total = array_in.shape[0]
    chosen = np.arange(stride)[None, :] == head_offsets(head_total, stride)[:, None]
    chosen = chosen.reshape((head_total,) + (1,) * (array_in.ndim - 1) + (stride,))
    full = jnp.where(chosen, array_in[..., None], fill_value)
    return full.reshape(array_in.shape[:-1] + (array_in.shape[-1] * stride,))


def to_heads(flat_in):
    return jnp.transpose(flat_in.reshape(flat_in.shape[0], HEADS, -1), (1, 2, 0))


def to_flat(heads_in):
    return jnp.transpose(heads_in, (2, 0, 1)).reshape(heads_in.shape[2], -1)


def local(query_tiles, key_tiles, value_tiles, cotangent, row_lengths):
    tile_count = query_tiles.shape[0]
    score_scale = HEAD ** (-0.5)
    query_heads = to_heads(query_tiles)
    key_heads = to_heads(key_tiles)
    value_heads = to_heads(value_tiles)
    cotan_heads = to_heads(cotangent)
    tile_slot = jnp.arange(tile_count, dtype=jnp.int32)
    tile_valid = tile_slot % ROW < jnp.repeat(row_lengths, ROW, total_repeat_length=tile_count)
    valid_heads = jnp.broadcast_to(tile_valid[None, :], (HEADS, tile_count))
    group_query = select_rows(query_heads, STRIDE_GROUP)
    group_key = select_rows(key_heads, STRIDE_GROUP)
    group_value = select_rows(value_heads, STRIDE_GROUP)
    group_cotan = select_rows(cotan_heads, STRIDE_GROUP)
    group_valid = select_rows(valid_heads, STRIDE_GROUP)
    group_flag = group_valid.astype(jnp.bfloat16)[:, None, :]
    slide_query = select_rows(query_heads, STRIDE_SLIDE)
    slide_key = select_rows(key_heads, STRIDE_SLIDE)
    slide_value = select_rows(value_heads, STRIDE_SLIDE)
    slide_flag = select_rows(valid_heads, STRIDE_SLIDE).astype(jnp.bfloat16)[:, None, :]
    owned_query, owned_key, owned_value, owned_flag = (
        lax.all_to_all(slide_query, "outer", split_axis=0, concat_axis=2, tiled=True),
        lax.all_to_all(slide_key, "outer", split_axis=0, concat_axis=2, tiled=True),
        lax.all_to_all(slide_value, "outer", split_axis=0, concat_axis=2, tiled=True),
        lax.all_to_all(slide_flag, "outer", split_axis=0, concat_axis=2, tiled=True),
    )
    got_group = (
        lax.all_gather(group_key, "inner", axis=2, tiled=True),
        lax.all_gather(group_value, "inner", axis=2, tiled=True),
        lax.all_gather(group_flag, "inner", axis=2, tiled=True),
    )
    got_slide = (
        lax.all_gather(owned_key, "inner", axis=2, tiled=True),
        lax.all_gather(owned_value, "inner", axis=2, tiled=True),
        lax.all_gather(owned_flag, "inner", axis=2, tiled=True),
    )
    near_peak, near_total, near_sum = branch_stats(
        query_heads, key_heads, value_heads, valid_heads, score_scale
    )
    remote_group_key = got_group[0]
    remote_group_value = got_group[1]
    remote_group_valid = got_group[2][:, 0, :] > 0.5
    group_peak, group_total, group_sum = branch_stats(
        group_query, remote_group_key, remote_group_value, remote_group_valid, score_scale
    )
    slide_all_key = got_slide[0]
    slide_all_value = got_slide[1]
    slide_all_valid = got_slide[2][:, 0, :] > 0.5
    owner_peak, owner_total, owner_sum = branch_stats(
        owned_query, slide_all_key, slide_all_value, slide_all_valid, score_scale
    )
    slide_peak, slide_total, slide_sum = (
        lax.all_to_all(owner_peak[:, None, :], "outer", split_axis=2, concat_axis=0, tiled=True),
        lax.all_to_all(owner_total[:, None, :], "outer", split_axis=2, concat_axis=0, tiled=True),
        lax.all_to_all(owner_sum, "outer", split_axis=2, concat_axis=0, tiled=True),
    )
    slide_peak = slide_peak[:, 0, :]
    slide_total = slide_total[:, 0, :]
    group_peak_full = spread_rows(group_peak, STRIDE_GROUP, NEGATIVE_FILL)
    slide_peak_full = spread_rows(slide_peak, STRIDE_SLIDE, NEGATIVE_FILL)
    best_peak = jnp.maximum(jnp.maximum(near_peak, group_peak_full), slide_peak_full)
    near_weight = jnp.exp(near_peak - best_peak)
    group_weight = jnp.exp(group_peak_full - best_peak)
    slide_weight = jnp.exp(slide_peak_full - best_peak)
    denominator = (
        near_total * near_weight
        + spread_rows(group_total, STRIDE_GROUP, 0.0) * group_weight
        + spread_rows(slide_total, STRIDE_SLIDE, 0.0) * slide_weight
    )
    numerator = (
        near_sum * near_weight[:, None, :]
        + spread_rows(group_sum, STRIDE_GROUP, 0.0) * group_weight[:, None, :]
        + spread_rows(slide_sum, STRIDE_SLIDE, 0.0) * slide_weight[:, None, :]
    )
    attended = (numerator / denominator[:, None, :]).astype(jnp.bfloat16)
    log_norm = best_peak + jnp.log(denominator)
    out_dot = jnp.sum(cotan_heads.astype(jnp.float32) * attended.astype(jnp.float32), axis=1)
    near_query, near_key, near_value = branch_grads(
        query_heads,
        key_heads,
        value_heads,
        cotan_heads,
        log_norm,
        out_dot,
        valid_heads,
        score_scale,
        True,
        True,
    )
    group_lse = select_rows(log_norm, STRIDE_GROUP)
    group_dot = select_rows(out_dot, STRIDE_GROUP)
    group_query_grad = branch_grads(
        group_query,
        remote_group_key,
        remote_group_value,
        group_cotan,
        group_lse,
        group_dot,
        remote_group_valid,
        score_scale,
        True,
        False,
    )[0]
    got_group_rows = (
        lax.all_gather(group_query, "inner", axis=2, tiled=True),
        lax.all_gather(group_cotan, "inner", axis=2, tiled=True),
    )
    got_group_stats = (
        lax.all_gather(group_lse, "inner", axis=1, tiled=True),
        lax.all_gather(group_dot, "inner", axis=1, tiled=True),
    )
    unused_group, group_key_grad, group_value_grad = branch_grads(
        got_group_rows[0],
        group_key,
        group_value,
        got_group_rows[1],
        got_group_stats[0],
        got_group_stats[1],
        group_valid,
        score_scale,
        False,
        True,
    )
    slide_cotan = select_rows(cotan_heads, STRIDE_SLIDE)
    slide_lse = select_rows(log_norm, STRIDE_SLIDE)
    slide_dot = select_rows(out_dot, STRIDE_SLIDE)
    owned_cotan = lax.all_to_all(slide_cotan, "outer", split_axis=0, concat_axis=2, tiled=True)
    owned_lse, owned_dot = (
        lax.all_to_all(slide_lse, "outer", split_axis=0, concat_axis=1, tiled=True),
        lax.all_to_all(slide_dot, "outer", split_axis=0, concat_axis=1, tiled=True),
    )
    owned_query_grad, partial_key, partial_value = branch_grads(
        owned_query,
        slide_all_key,
        slide_all_value,
        owned_cotan,
        owned_lse,
        owned_dot,
        slide_all_valid,
        score_scale,
        True,
        True,
    )
    owned_key_grad, owned_value_grad = (
        lax.psum_scatter(
            partial_key.astype(jnp.bfloat16), "inner", scatter_dimension=2, tiled=True
        ).astype(jnp.float32),
        lax.psum_scatter(
            partial_value.astype(jnp.bfloat16), "inner", scatter_dimension=2, tiled=True
        ).astype(jnp.float32),
    )
    slide_query_grad, slide_key_grad, slide_value_grad = (
        lax.all_to_all(
            as_sent(owned_query_grad), "outer", split_axis=2, concat_axis=0, tiled=True
        ).astype(owned_query_grad.dtype),
        lax.all_to_all(
            owned_key_grad.astype(jnp.bfloat16), "outer", split_axis=2, concat_axis=0, tiled=True
        ).astype(owned_key_grad.dtype),
        lax.all_to_all(
            owned_value_grad.astype(jnp.bfloat16), "outer", split_axis=2, concat_axis=0, tiled=True
        ).astype(owned_value_grad.dtype),
    )
    query_grad = (
        near_query
        + spread_rows(group_query_grad, STRIDE_GROUP, 0.0)
        + spread_rows(slide_query_grad, STRIDE_SLIDE, 0.0)
    )
    key_grad = (
        near_key
        + spread_rows(group_key_grad, STRIDE_GROUP, 0.0)
        + spread_rows(slide_key_grad, STRIDE_SLIDE, 0.0)
    )
    value_grad = (
        near_value
        + spread_rows(group_value_grad, STRIDE_GROUP, 0.0)
        + spread_rows(slide_value_grad, STRIDE_SLIDE, 0.0)
    )
    return (
        to_flat(attended),
        to_flat(query_grad.astype(jnp.bfloat16)),
        to_flat(key_grad.astype(jnp.bfloat16)),
        to_flat(value_grad.astype(jnp.bfloat16)),
    )


BF = jnp.bfloat16
F32 = jnp.float32
LANES = 128
SCALE = HEAD ** (-0.5)
PAIR = 2 * HEAD
PAIRS = HEADS // 2
MESH = pl.DeviceIdType.MESH


def iota2(shape, axis):
    return lax.broadcasted_iota(jnp.int32, shape, axis)


def original_tile(j):
    return (j & 7) * 16 + ((j >> 3) & 3) * 4 + (j >> 5)


def permute_matrix(inverse):
    shape = (LANES, LANES)
    j, i = (iota2(shape, 1), iota2(shape, 0)) if inverse else (iota2(shape, 0), iota2(shape, 1))
    return (original_tile(j) == i).astype(F32).astype(BF)


def identity(size):
    shape = (size, size)
    return (iota2(shape, 0) == iota2(shape, 1)).astype(F32).astype(BF)


def key_bias(len_ref):
    tile = original_tile(iota2((LANES, LANES), 0))
    row = tile >> 5
    length = jnp.full((LANES, LANES), len_ref[0], jnp.int32)
    for index in range(1, 4):
        length = jnp.where(row == index, len_ref[index], length)
    return jnp.where((tile & 31) < length, 0.0, NEGATIVE_FILL).astype(F32)


def mm(a, b):
    return jnp.dot(a, b, preferred_element_type=F32)


def mm_t(a, b):
    return lax.dot_general(a, b, (((1,), (1,)), ((), ())), preferred_element_type=F32)


def slide_row(r):
    return (r % 4) * 32 + (r // 4) * 8


def head_lanes(lane, p, e):
    return ((lane - (PAIR * p + HEAD * e)) & (LANES - 1)) < HEAD


def flag_lane(p):
    return (PAIR * (p + 1)) & (LANES - 1)


def as_mask(keep):
    return keep.astype(F32).astype(BF)


def head_masks(p):
    lane = iota2((1, LANES), 1)
    masks = [as_mask(head_lanes(lane, p, e)) for e in range(2)]
    flags = [as_mask(lane == flag_lane(p) + e) for e in range(3)]
    return masks, flags


def two_heads(x, masks, flags=None):
    parts = [x * masks[e] for e in range(2)]
    if flags is not None:
        parts = [part + flag for part, flag in zip(parts, flags)]
    return jnp.concatenate(parts, axis=0)


def pieces_of(p):
    base, spot = p // 4 * 3, p % 4
    if spot == 0:
        return [(base, 0, 96)]
    if spot == 1:
        return [(base, 96, 128), (base + 1, 0, 64)]
    if spot == 2:
        return [(base + 1, 64, 128), (base + 2, 0, 32)]
    return [(base + 2, 32, 128)]


def pair_tile(x, p):
    parts = pieces_of(p)
    tiles = [x[:, t * LANES : (t + 1) * LANES] for t, _, _ in parts]
    if len(tiles) == 1:
        return tiles[0]
    lane = iota2(tiles[0].shape, 1)
    return jnp.where(lane >= parts[0][1], tiles[0], tiles[1])


SLOT_ROWS, S_ROW, G_ROWS = 48, 96, 112


def swapped(p):
    return jnp.where(lax.rem(2 * p, 5) == 0, 1, 0)


def head_of(h, slot):
    return slot ^ (1 if 2 * h % 5 == 0 else 0)


def relative(lane, p, e):
    return (lane - (PAIR * p + HEAD * e)) & (LANES - 1)


def roll_lanes(x, shift):
    return pltpu.roll(x, shift, x.ndim - 1)


def fold_rows(full, rel):
    low, high = full[..., 0:16, :], full[..., 16:32, :]
    return jnp.where((rel >= 32) & (rel < 96), low, roll_lanes(high, 64))


def unfold_rows(x):
    return jnp.concatenate([x, roll_lanes(x, 64)], axis=x.ndim - 2)


def packed(rel, q, k, v, c):
    first = jnp.where(rel < 48, q, jnp.where(rel < 96, roll_lanes(k, 48), roll_lanes(v, 96)))
    return first, fold_rows(jnp.where(rel < 48, v, roll_lanes(c, 48)), rel[:16])


def prep_pair(x, p, bias=None):
    tile = pair_tile(x, p)
    lane = iota2(tile.shape, 1)
    flag = flag_lane(p)
    if bias is not None:
        tile = jnp.where((lane == flag) | (lane == flag + 1), bias, tile)
    first, second = [tile[slide_row(2 * p + e) :][:8] for e in range(2)]
    lane = iota2(first.shape, 1)
    slide = jnp.where(head_lanes(lane, p, 1) | (lane == flag + 1), second, first)
    return tile, slide


def near_early(p, tp_ref, pn_ref, ad_ref, kt_ref, vt_ref, eye):
    k, q, v, c = [tp_ref[a, p] for a in range(4)]
    masks, flags = head_masks(p)
    s = mm_t(k, two_heads(q, masks, flags)) * SCALE
    dp = mm_t(v, two_heads(c, masks))
    kt_ref[p] = mm_t(eye, two_heads(k, masks)).astype(BF)
    vt_ref[p] = mm_t(eye, two_heads(v, masks)).astype(BF)
    peak = jnp.max(s, axis=0, keepdims=True)
    weights = jnp.exp(s - peak)
    total = jnp.sum(weights, axis=0, keepdims=True)
    weights = weights * (1.0 / total)
    delta = jnp.sum(weights * dp, axis=0, keepdims=True)
    pn_ref[p] = weights
    ad_ref[p] = weights * (dp - delta)
    return peak + jnp.log(total), delta


def turn(x, shift):
    return pltpu.roll(x, shift & (LANES - 1), 1)


def compact(lane, slots, slides):
    low = jnp.where(lane < 32, slots[0], slots[1])
    return jnp.where(lane < 64, low, jnp.where(lane < 72, slides[0], slides[1]))


def near_stats(p, lse, delta):
    shape = (8, LANES)
    row, lane = iota2(shape, 0), iota2(shape, 1)

    def wide(x, e):
        return jnp.broadcast_to(x[:, e * LANES : (e + 1) * LANES], shape)

    heads = [jnp.where(row == 0, wide(lse, e), wide(delta, e)) for e in range(2)]
    slots = [turn(heads[head_of(p, slot)], 32 * slot - p // 2 * 32) for slot in range(2)]
    slides = [turn(heads[e], 64 + 8 * e - slide_row(2 * p + e)) for e in range(2)]
    return compact(lane, slots, slides)[0:2]


def near_late(p, r2_ref, tp_ref, pn_ref, ad_ref, kt_ref, vt_ref, late_ref, turned_ref):
    tile = jnp.concatenate([r2_ref[p]] * 4, axis=0)
    lane = iota2((1, LANES), 1)
    start = p // 2 * 32
    in_group = (lane >= start) & (lane < start + 32)
    scales, shifts = [], []
    for e in range(2):
        at = slide_row(2 * p + e)
        group = turn(tile, start - 32 * head_of(p, e))
        slide = turn(tile, at - 64 - 8 * e)
        in_slide = (lane >= at) & (lane < at + 8)
        for index, (found, fill) in enumerate(((scales, 1.0), (shifts, 0.0))):
            value = jnp.where(in_slide, slide[index : index + 1], fill)
            found.append(jnp.where(in_group, group[index : index + 1], value))
    scale = jnp.concatenate(scales, axis=1)
    shift = jnp.concatenate(shifts, axis=1)
    weights = pn_ref[p]
    low = (weights * scale).astype(BF)
    grads = (ad_ref[p] * (scale * SCALE) - weights * (scale * shift * SCALE)).astype(BF)
    masks, _ = head_masks(p)
    late_ref[0, p] = mm(grads, two_heads(tp_ref[1, p], masks))
    late_ref[1, p] = mm(low, two_heads(tp_ref[3, p], masks))

    def stacked(x):
        return jnp.concatenate([x[:, :LANES], x[:, LANES:]], axis=0)

    for index, value in enumerate((mm(vt_ref[p], stacked(low)), mm(kt_ref[p], stacked(grads)))):
        value = value.astype(BF)
        for t, first, last in pieces_of(p):
            turned_ref[index, t * LANES + first : t * LANES + last] = value[first:last]


def branch(s):
    peak = jnp.max(s, axis=0, keepdims=True)
    weights = jnp.exp(s - peak)
    total = jnp.sum(weights, axis=0, keepdims=True)
    return weights, peak, total, peak + jnp.log(total)


def rows_of(row, first, second, third):
    first, second, third = [jnp.broadcast_to(x, row.shape) for x in (first, second, third)]
    return jnp.where(row == 0, first, jnp.where(row == 1, second, third))


def slide_scores(masks, flags, gr_ref, skv_ref):
    kv = skv_ref[...].reshape(-1, LANES)
    sources = gr_ref.shape[0]
    wide = gr_ref[:, S_ROW:G_ROWS].astype(F32)
    q, c = [wide[:, a : a + 8].reshape(sources * 8, LANES).astype(BF) for a in (0, 8)]
    q2, c2 = two_heads(q, masks, flags), two_heads(c, masks)
    both = mm_t(kv, jnp.concatenate([q2, c2], axis=0)).reshape(-1, 16, 2 * LANES)
    s = both[:, 0:8, :LANES].reshape(-1, LANES) * SCALE
    dp = both[:, 8:16, LANES:].reshape(-1, LANES)
    return kv, q2, c2, s, dp


def near_of(row, lane, ns_ref):
    slots, slide = [[None] * 2, [None] * 2], None

    def pick(keep, value, old):
        return value if old is None else jnp.where(keep, value, old)

    for source in range(8):
        j, q = divmod(source, 4)
        tile = jnp.concatenate([ns_ref[source]] * 4, axis=0)
        for slot in range(2):
            slots[slot][j] = pick((lane >> 5) == q, turn(tile, q * 32 - 32 * slot), slots[slot][j])
        first, second = [turn(tile, 64 * e + 8 * source - 64 - 8 * e) for e in range(2)]
        both = jnp.where(lane < 64, first, second)
        slide = pick(((lane & 63) >> 3) == source, both, slide)
    return [
        [rows_of(row, *[x[i : i + 1] for x in (slots[0][j], slots[1][j], slide)]) for i in range(2)]
        for j in range(2)
    ]


def crossed(row, lane, p, slide, group, fill):
    first = lax.rem(2 * p, 5) == 0
    any_head = jnp.logical_or(first, lax.rem(2 * p + 1, 5) == 0)
    e = jnp.where(first, 0, 1)
    at = p // 2 * 8
    source = jnp.broadcast_to(slide, row.shape)
    found, to_slide = [], None
    for j in range(2):
        chosen = jnp.broadcast_to(group[j], row.shape)
        to_group = None
        for q in range(4):
            here, there = q * 32 + at, (4 * j + q) * 8 + e * 64
            moved = turn(source, here - there + LANES)
            to_group = moved if q == 0 else jnp.where((lane >> 5) == q, moved, to_group)
            moved = turn(chosen, there - here + LANES)
            same = ((lane & 63) >> 3) == 4 * j + q
            to_slide = moved if to_slide is None else jnp.where(same, moved, to_slide)
        found.append(to_group)
    in_group = (row == 1) & ((lane & 31) >> 3 == p // 2) & any_head
    in_slide = (row == 2) & ((lane >> 6) == e) & any_head
    return [
        jnp.where(in_group | in_slide, jnp.where(row == 2, to_slide, to_group), fill)
        for to_group in found
    ]


class Slot:
    def __init__(self, p, e, gr_ref, at, group_bias, flag):
        sources = gr_ref.shape[0]
        lane = iota2((1, LANES), 1)
        self.rel = relative(lane, p, e)
        self.own, self.second = [as_mask((self.rel >= low) & (self.rel < low + 48)) for low in (0, 48)]
        head = self.rel < 48
        first = gr_ref[:, at : at + 32].reshape(sources * 32, LANES)
        rest = unfold_rows(gr_ref[:, at + 32 : at + 48].astype(F32)).reshape(sources * 32, LANES)
        wide = first.astype(F32)
        self.q = first * self.own + flag
        key = roll_lanes(wide, LANES - 48).astype(BF) * self.own
        self.k = key + group_bias
        self.v = jnp.where(self.rel < 32, roll_lanes(wide, 32), rest).astype(BF) * self.own
        self.c = roll_lanes(rest, LANES - 48).astype(BF) * self.own
        self.moved_k = first * self.second
        self.moved_c = rest.astype(BF) * self.second
        spread = jnp.where(self.rel >= 96, roll_lanes(wide, 96), wide)
        self.moved_q = spread.astype(BF) * as_mask((self.rel >= 96) | ((self.rel >= 32) & head))

    def scores(self, eye):
        self.parts = [
            branch(mm_t(self.k, self.q[j * LANES : (j + 1) * LANES]) * SCALE) for j in range(2)
        ]
        self.dps = [mm_t(self.v, self.c[j * LANES : (j + 1) * LANES]) for j in range(2)]
        self.deltas = [
            jnp.sum(part[0] * dp, axis=0, keepdims=True) / part[2]
            for part, dp in zip(self.parts, self.dps)
        ]
        both = jnp.concatenate([self.v, self.moved_k], axis=0)
        self.turned = mm_t(eye, both).astype(BF)

    def results(self, factors, deltas, eye2, sources):
        lows, grads = [], []
        for j, (part, dp) in enumerate(zip(self.parts, self.dps)):
            weights = part[0] * factors[j]
            lows.append(weights.astype(BF))
            grads.append((weights * (dp - deltas[j]) * SCALE).astype(BF))
        lows, grads = jnp.concatenate(lows, axis=1), jnp.concatenate(grads, axis=1)
        rest = mm(
            jnp.concatenate([grads, lows], axis=1), jnp.concatenate([self.moved_q, self.moved_c], axis=0)
        )
        first = mm(self.turned, jnp.concatenate([lows, grads], axis=0)).astype(BF)
        first = jnp.where(self.rel < 96, mm_t(eye2, first), rest)
        rest = fold_rows(rest.reshape(sources, 32, LANES), self.rel)
        return first.astype(BF).reshape(sources, 32, LANES), rest.astype(BF)


class Exchange:
    def __init__(self, count, make, every):
        self.count, self.make, self.every = count, make, every

    def start(self):
        @pl.loop(1, self.count)
        def _(step):
            self.make(step).start()

    def wait_recv(self):
        self.every.wait_recv()

    def wait_send(self):
        self.every.wait_send()


def wrapped(value, count):
    return jnp.where(value >= count, value - count, value)


def whole_kernel(
    inner, outers, len_hbm, q_hbm, k_hbm, v_hbm, c_hbm, turned, acc,
    len_ref, loaded, load_sem, tp, gm, gr, skv_s, skv, pn, ad, kt, vt, ns_s, ns_r, r2_s, r2_r,
    r4_s, r4_r, xs, xr, sg_s, sg_r, late, send_sem, recv_sem, x_send, x_recv,
):
    outer, me = lax.axis_index("outer"), lax.axis_index("inner")
    p = me

    def scope(name):
        return jax.named_scope(name)

    def copy_to(src, dst, sems, index, device):
        return pltpu.make_async_remote_copy(
            src_ref=src,
            dst_ref=dst,
            send_sem=sems[0].at[index],
            recv_sem=sems[1].at[index],
            device_id=device,
            device_id_type=MESH,
        )

    def exchange(index, source, target, size):
        sems, next_place = (send_sem, recv_sem), wrapped(me + 1, inner)

        def make(step):
            peer = step - jnp.where(step <= me, 1, 0)
            return copy_to(source(peer), target(me), sems, index, (outer, peer))

        return Exchange(inner, make, copy_to(size, size, sems, index, (outer, next_place)))

    def across(index, source, target, size):
        sems, next_place = (x_send, x_recv), wrapped(outer + 1, outers)

        def make(step):
            peer = step - jnp.where(step <= outer, 1, 0)
            return copy_to(source(peer), target, sems, index, (peer, me))

        return Exchange(outers, make, copy_to(size, size, sems, index, (next_place, me)))

    def blocks_exchange(index, src, dst):
        size = dst.at[pl.ds(0, inner - 1)]
        return exchange(index, lambda peer: src.at[peer], lambda mine: dst.at[mine], size)

    def rows_exchange(index, src, dst, first, last):
        rows = pl.ds(first, last - first)
        size = dst.at[pl.ds(0, inner - 1), rows]
        return exchange(index, lambda peer: src.at[peer, rows], lambda mine: dst.at[mine, rows], size)

    some = pl.ds(0, inner - 1)
    send_skv = exchange(
        0, lambda peer: skv_s.at[peer], lambda mine: skv.at[outer, mine], skv.at[0, some]
    )
    send_first = rows_exchange(1, gm, gr, 0, SLOT_ROWS)
    send_second = rows_exchange(2, gm, gr, SLOT_ROWS, S_ROW)
    send_qc = rows_exchange(9, gm, gr, S_ROW, G_ROWS)
    send_ns = blocks_exchange(3, ns_s, ns_r)
    send_r2 = blocks_exchange(4, r2_s, r2_r)
    back_first = rows_exchange(5, r4_s, r4_r, 0, SLOT_ROWS)
    back_second = rows_exchange(6, r4_s, r4_r, SLOT_ROWS, S_ROW)
    send_oq = rows_exchange(7, r4_s, r4_r, S_ROW, G_ROWS)
    send_sg = blocks_exchange(8, sg_s, sg_r)
    forward = across(0, lambda peer: skv.at[outer], skv.at[outer], skv.at[pl.ds(0, outers - 1)])
    backward = across(1, lambda peer: xs.at[peer], xr.at[outer], xr.at[pl.ds(0, outers - 1)])

    barrier = pltpu.get_barrier_semaphore()
    with scope("load_start"):
        loads = [
            pltpu.make_async_copy(ref, loaded.at[a], load_sem.at[a])
            for a, ref in enumerate((k_hbm, q_hbm, v_hbm, c_hbm))
        ]
        loads.append(pltpu.make_async_copy(len_hbm, len_ref, load_sem.at[4]))
        for index in (4, 0, 2, 1, 3):
            loads[index].start()
    with scope("greet"):

        @pl.loop(1, inner)
        def _(step):
            pl.semaphore_signal(
                barrier, inc=1, device_id=(outer, wrapped(me + step, inner)), device_id_type=MESH
            )

        @pl.loop(1, outers)
        def _(step):
            pl.semaphore_signal(
                barrier, inc=1, device_id=(wrapped(outer + step, outers), me), device_id_type=MESH
            )

    perm = permute_matrix(False)
    eye = identity(LANES)
    with scope("load_wait"):
        loads[4].wait()
        loads[0].wait()
        loads[2].wait()
    with scope("prep_kv"):
        bias = key_bias(len_ref)
        xk = mm(perm, loaded[0])
        xv = mm(perm, loaded[2])
        groups = []
        for h in range(PAIRS):
            first = h // 2 * 32
            rows = slice(first, first + 32)
            tile, key_slide = prep_pair(xk, h, bias)
            tp[0, h] = tile.astype(BF)
            groups.append([tile[rows]])
            tile, value_slide = prep_pair(xv, h)
            tp[2, h] = tile.astype(BF)
            groups[h].append(tile[rows])
            both = jnp.concatenate([key_slide, value_slide], axis=0)
            lane = iota2(both.shape, 1)
            for index in range(2):
                part = bias[first + 16 * index : first + 16 * index + 16]
                both = jnp.where(lane == flag_lane(h) + 2 + index, part, both)
            skv_s[h] = both.astype(BF)
    def pack_slot(h, slot):
        rel = relative(iota2((32, LANES), 1), h, head_of(h, slot))
        first, rest = packed(rel, *groups[h])
        at = SLOT_ROWS * slot
        gm[h, at : at + 32] = first.astype(BF)
        gm[h, at + 32 : at + 48] = rest.astype(BF)

    with scope("prep_qc"):
        loads[1].wait()
        loads[3].wait()
        xq = mm(perm, loaded[1])
        xc = mm(perm, loaded[3])
        slides = []
        for h in range(PAIRS):
            rows = slice(h // 2 * 32, h // 2 * 32 + 32)
            tile, query_slide = prep_pair(xq, h)
            tp[1, h] = tile.astype(BF)
            groups[h].insert(0, tile[rows])
            tile, cotan_slide = prep_pair(xc, h)
            tp[3, h] = tile.astype(BF)
            groups[h].append(tile[rows])
            slides.append(jnp.concatenate([query_slide, cotan_slide], axis=0))
            pack_slot(h, 0)
    with scope("prep_second"):
        for h in range(PAIRS):
            pack_slot(h, 1)
            gm[h, S_ROW:G_ROWS] = slides[h].astype(BF)
        gr[me] = gm[me]
        skv[outer, me] = skv_s[me]

    def near_forward():
        with scope("near_early"):
            for h in range(PAIRS):
                lse, delta = near_early(h, tp, pn, ad, kt, vt, eye)
                ns_s[h] = near_stats(h, lse, delta)

    ahead = me < inner // 2

    @pl.when(ahead)
    def _():
        near_forward()

    with scope("barrier_wait"):
        pl.semaphore_wait(barrier, inner - 1 + outers - 1)
    with scope("send_skv"):
        send_skv.start()

    @pl.when(jnp.logical_not(ahead))
    def _():
        near_forward()

    with scope("send_first"):
        send_first.start()
    with scope("send_ns"):
        send_ns.start()
        send_qc.start()
        ns_r[me] = ns_s[me]
    with scope("skv_wait"):
        send_skv.wait_recv()
    with scope("forward"):
        forward.start()
    with scope("send_second"):
        send_second.start()
    masks, flags = head_masks(p)
    row, lane = iota2((8, LANES), 0), iota2((8, LANES), 1)
    eye2 = identity(2 * LANES)

    swap = swapped(p)
    with scope("bias"):
        near_keys = skv[outer].astype(F32)
        near_keys = jnp.concatenate([near_keys, pltpu.roll(near_keys, LANES - 1, 2)], axis=1)
        group_bias = near_keys.reshape(inner * 32, LANES).astype(BF) * flags[2]
    with scope("first_wait"):
        send_first.wait_recv()
    with scope("first_scores"):
        first = Slot(p, swap, gr, 0, group_bias, flags[2])
        first.scores(eye)
    with scope("ns_wait"):
        send_ns.wait_recv()
    with scope("first_merge"):
        near = near_of(row, lane, ns_r)
        first_factors, first_deltas, first_shares = [], [], []
        for j in range(2):
            near_lse, near_delta = near[j][0][0:1], near[j][1][0:1]
            _, peak, _, own = first.parts[j]
            best = jnp.maximum(near_lse, own)
            parts = [jnp.exp(x - best) for x in (near_lse, own)]
            total = parts[0] + parts[1]
            inverse = 1.0 / total
            first_factors.append(jnp.exp(peak - best - jnp.log(total)))
            first_deltas.append((parts[0] * near_delta + parts[1] * first.deltas[j]) * inverse)
            first_shares.append(parts[0] * inverse)
    with scope("first_results"):
        main, rest = first.results(first_factors, first_deltas, eye2, inner)
        r4_s[:, 0:32] = main
        r4_s[:, 32:48] = rest
    with scope("first_back"):
        back_first.start()
    with scope("forward_wait"):
        forward.wait_recv()
        send_qc.wait_recv()
    with scope("slide_scores"):
        skv_all, qs2, cs2, s, slide_dp = slide_scores(masks, flags, gr, skv)
        slide_weights, slide_peak, slide_total, slide_lse = branch(s)
        slide_delta = jnp.sum(slide_weights * slide_dp, axis=0, keepdims=True) / slide_total
        skv_t = mm_t(eye, skv_all).astype(BF)
    with scope("second_wait"):
        send_second.wait_recv()
    with scope("second_scores"):
        second = Slot(p, 1 - swap, gr, SLOT_ROWS, group_bias, flags[2])
        second.scores(eye)
    with scope("second_merge"):
        other = crossed(row, lane, p, slide_lse, [x[3] for x in second.parts], NEGATIVE_FILL)
        other_delta = crossed(row, lane, p, slide_delta, second.deltas, 0.0)

        def on_rows(group, slide):
            return jnp.where(row == 2, slide, group)

        factors, deltas, own_shares, own_moved = [], [], [], []
        for j in range(2):
            _, peak, _, group_lse = second.parts[j]
            own = on_rows(group_lse, slide_lse)
            best = jnp.maximum(jnp.maximum(near[j][0], own), other[j])
            parts = [jnp.exp(x - best) for x in (near[j][0], own, other[j])]
            total = parts[0] + parts[1] + parts[2]
            inverse = 1.0 / total
            factors.append(jnp.exp(on_rows(peak, slide_peak) - best - jnp.log(total)))
            delta = parts[0] * near[j][1] + parts[2] * other_delta[j]
            delta = (delta + parts[1] * on_rows(second.deltas[j], slide_delta)) * inverse
            deltas.append(delta)
            own_shares.append(parts[0] * inverse)
            own_moved.append(delta - near[j][1])
        first_moved = [first_deltas[j] - near[j][1][0:1] for j in range(2)]
        for source in range(inner):
            j, q = divmod(source, 4)
            tiles = [jnp.where(row == 0, first_shares[j], first_moved[j])]
            for at in (1, 2):
                pair = [x[j][at : at + 1] for x in (own_shares, own_moved)]
                tiles.append(jnp.where(row == 0, *pair))
            slots = [turn(tiles[slot], 32 * slot - 32 * q) for slot in range(2)]
            slides = [turn(tiles[2], 64 + 8 * e - 64 * e - 8 * source) for e in range(2)]
            r2_s[source] = compact(lane, slots, slides)[0:2]
    with scope("send_r2"):
        send_r2.start()
        r2_r[me] = r2_s[me]
    with scope("slide_bwd"):
        weights = slide_weights * factors[0][2:3]
        grads = weights * (slide_dp - deltas[0][2:3]) * SCALE
        blocks = [x.reshape(-1, 8, LANES) for x in (grads, weights)]
        empty = jnp.zeros_like(blocks[0])
        mixed = jnp.concatenate(
            [
                jnp.concatenate([blocks[0], empty], axis=2),
                jnp.concatenate([empty, blocks[1]], axis=2),
            ],
            axis=1,
        )
        mixed = mixed.reshape(-1, 2 * LANES).astype(BF)
        xs[...] = mm(mixed, jnp.concatenate([qs2, cs2], axis=0)).astype(BF).reshape(xs.shape)
    with scope("send_x"):
        backward.start()
    with scope("second_results"):
        main, rest = second.results(
            [x[1:2] for x in factors], [x[1:2] for x in deltas], eye2, inner
        )
        r4_s[:, 48:80] = main
        r4_s[:, 80:96] = rest
    with scope("second_back"):
        back_second.start()
    with scope("slide_q"):
        both = mm_t(eye2, mm(skv_t, mixed).astype(BF))
        quarter = LANES // 2
        head0 = head_lanes(iota2((quarter, LANES), 1), p, 0)
        query = jnp.where(head0, both[0:quarter], both[quarter:LANES])
        out = jnp.where(head0, both[LANES : 3 * quarter], both[3 * quarter : 4 * quarter])
        blocks = [x.reshape(inner, 8, LANES) for x in (out, query)]
        r4_s[:, S_ROW:G_ROWS] = jnp.concatenate(blocks, axis=1).astype(BF)
    with scope("send_oq"):
        send_oq.start()
        r4_r[me] = r4_s[me]
    with scope("clear"):
        acc[0:2] = jnp.zeros((2,) + acc.shape[1:], F32)
    with scope("x_wait"):
        backward.wait_recv()
    with scope("x_sum"):
        total = xs[outer].astype(F32)
        for step in range(1, outers):
            total = total + xr[wrapped(outer + step, outers)].astype(F32)
        sg_s[...] = total.astype(BF)
    with scope("send_sg"):
        send_sg.start()
        sg_r[me] = sg_s[me]
    with scope("r2_wait"):
        send_r2.wait_recv()
    with scope("near_late1"):
        for h in range(PAIRS):
            near_late(h, r2_r, tp, pn, ad, kt, vt, late, turned)
    with scope("collect"):
        for a in range(2):
            for t in range(D_TILES):
                value = None
                for h in range(PAIRS):
                    for tile, first, last in pieces_of(h):
                        if tile == t:
                            piece = late[a, h]
                            lane_full = iota2(piece.shape, 1)
                            value = piece if value is None else jnp.where(lane_full >= first, piece, value)
                acc[2 + a, :, t * LANES : (t + 1) * LANES] = value
    with scope("drain"):
        for sent in (send_skv, send_first, send_second, send_qc, send_ns, forward, send_r2, backward):
            sent.wait_send()
    for slot, sent in enumerate((back_first, back_second)):
        with scope("back_wait%d" % slot):
            sent.wait_recv()
        with scope("back_add%d" % slot):
            at = SLOT_ROWS * slot
            for h in range(PAIRS):
                add_group(acc, h, head_of(h, slot), r4_r[h, at : at + 32], r4_r[h, at + 32 : at + 48])
    with scope("oq_wait"):
        send_oq.wait_recv()
    with scope("oq_add"):
        for h in range(PAIRS):
            add_slide(acc, (0, 1), h, r4_r[h, S_ROW:G_ROWS])
    with scope("sg_wait"):
        send_sg.wait_recv()
    with scope("sg_add"):
        for h in range(PAIRS):
            add_slide(acc, (2, 3), h, sg_r[h])
    with scope("drain_last"):
        for sent in (back_first, back_second, send_oq, send_sg):
            sent.wait_send()


D_TILES = HEADS * HEAD // LANES


def final_kernel(turned, acc, att_hbm, dq_hbm, dk_hbm, dv_hbm, done, sems):
    back = permute_matrix(True)
    copies = []
    for a, ref in enumerate((att_hbm, dq_hbm, dk_hbm, dv_hbm)):
        value = mm(back, acc[a].astype(BF))
        if a < 2:
            value = value + mm_t(back, turned[a])
        done[a] = value.astype(BF)
        copies.append(pltpu.make_async_copy(done.at[a], ref, sems.at[a]))
        copies[-1].start()
    for copy in copies:
        copy.wait()


def add_group(acc, h, e, first, rest):
    first, rest = first.astype(F32), unfold_rows(rest.astype(F32))
    start = h // 2 * 32
    lane = iota2(first.shape, 1)
    rel = relative(lane, h, e)
    key = jnp.where(rel < 32, roll_lanes(first, 32), rest)
    values = (first, roll_lanes(first, LANES - 48), key, roll_lanes(rest, LANES - 48))
    for out, value in enumerate(values):
        for t, low, high in pieces_of(h):
            keep = (lane >= low) & (lane < high) & (rel < HEAD)
            cols = slice(t * LANES, (t + 1) * LANES)
            acc[out, start : start + 32, cols] += jnp.where(keep, value, 0.0)


def add_slide(acc, outs, h, block):
    block = block.astype(F32)
    lane = iota2((8, LANES), 1)
    for index, out in enumerate(outs):
        small = block[8 * index : 8 * index + 8]
        for t, first, last in pieces_of(h):
            cols = slice(t * LANES, (t + 1) * LANES)
            for e in range(2):
                at = slide_row(2 * h + e)
                keep = (lane >= first) & (lane < last) & head_lanes(lane, h, e)
                acc[out, at : at + 8, cols] += jnp.where(keep, small, 0.0)


def fast_local(inner, outers, *args):
    row_lengths, tiles_in = args[4], args[:4]
    tiles, width = tiles_in[0].shape
    vmem = pl.BlockSpec(memory_space=pltpu.VMEM)
    hbm = pl.BlockSpec(memory_space=pltpu.HBM)

    def both(shape, dtype):
        return [pltpu.VMEM(shape, dtype)] * 2

    scratch = [
        pltpu.SMEM(row_lengths.shape, jnp.int32),
        pltpu.VMEM((4, tiles, width), BF),
        pltpu.SemaphoreType.DMA((5,)),
        pltpu.VMEM((4, PAIRS, tiles, LANES), BF),
    ]
    scratch += both((inner, G_ROWS, LANES), BF)
    scratch += [pltpu.VMEM((inner, 16, LANES), BF), pltpu.VMEM((outers, inner, 16, LANES), BF)]
    scratch += both((PAIRS, tiles, 2 * LANES), F32)
    scratch += both((PAIRS, LANES, 2 * LANES), BF)
    scratch += both((inner, 2, LANES), F32) + both((inner, 2, LANES), F32)
    scratch += both((inner, G_ROWS, LANES), BF)
    scratch += both((outers, inner, 16, LANES), BF)
    scratch += both((inner, 16, LANES), BF)
    scratch += [pltpu.VMEM((2, PAIRS, tiles, LANES), F32)]
    scratch += [pltpu.SemaphoreType.DMA((10,))] * 2 + [pltpu.SemaphoreType.DMA((2,))] * 2
    in_hbm = [pltpu.with_memory_space_constraint(x, pltpu.HBM) for x in (row_lengths, *tiles_in)]
    shapes = (((2, width, tiles), BF), ((4, tiles, width), F32))
    between = pl.pallas_call(
        lambda *refs: whole_kernel(inner, outers, *refs),
        out_shape=[pltpu.VMEM(shape, dtype) for shape, dtype in shapes],
        in_specs=[hbm] * 5,
        out_specs=[vmem] * 2,
        scratch_shapes=scratch,
        compiler_params=pltpu.CompilerParams(
            collective_id=0, has_side_effects=True, vmem_limit_bytes=32 * 1024 * 1024
        ),
    )(*in_hbm)
    return tuple(
        pl.pallas_call(
            final_kernel,
            out_shape=[pltpu.HBM((tiles, width), BF)] * 4,
            in_specs=[vmem] * 2,
            out_specs=[hbm] * 4,
            scratch_shapes=[pltpu.VMEM((4, tiles, width), BF), pltpu.SemaphoreType.DMA((4,))],
            compiler_params=pltpu.CompilerParams(vmem_limit_bytes=32 * 1024 * 1024),
        )(*between)
    )


def solution(mesh):
    in_specs = (P(("outer", "inner"), None),) * 4 + (P(("outer", "inner")),)
    out_specs = (P(("outer", "inner"), None),) * 4
    inner, outers = mesh.shape["inner"], mesh.shape["outer"]

    def step(*args):
        fits = inner == PAIRS and outers == 4
        if fits and args[0].shape == (LANES, HEADS * HEAD):
            return fast_local(inner, outers, *args)
        return local(*args)

    return jax.shard_map(step, mesh=mesh, in_specs=in_specs, out_specs=out_specs, check_vma=False)
```

```python
import jax
import jax.numpy as jnp
import numpy as np
from jax import lax
from jax.experimental import pallas as pl
from jax.experimental.pallas import tpu as pltpu
from jax.sharding import PartitionSpec as P

HEADS = 16
HEAD = 48
ROW = 32
STRIDE_GROUP = 4
STRIDE_SLIDE = 16


NEGATIVE_FILL = -1e30
heads_at_once = 4


def as_sent(value):

    def short(part):
        return part.astype(jnp.bfloat16) if part.dtype == jnp.float32 else part

    return jax.tree.map(short, value)


def head_ranges(head_total):
    step_size = min(head_total, heads_at_once)
    return [(first_head, first_head + step_size) for first_head in range(0, head_total, step_size)]


def scores_of(query_block, key_block, score_scale):
    return (
        jnp.einsum("hdq,hdk->hqk", query_block, key_block, preferred_element_type=jnp.float32)
        * score_scale
    )


def branch_stats(query_heads, key_heads, value_heads, key_valid, score_scale):
    peak_list, total_list, sum_list = ([], [], [])
    for first_head, last_head in head_ranges(query_heads.shape[0]):
        raw_scores = scores_of(
            query_heads[first_head:last_head], key_heads[first_head:last_head], score_scale
        )
        key_keep = key_valid[first_head:last_head][:, None, :]
        masked = jnp.where(key_keep, raw_scores, NEGATIVE_FILL)
        row_peak = jnp.max(masked, axis=2)
        weights = jnp.where(key_keep, jnp.exp(masked - row_peak[:, :, None]), 0.0)
        peak_list.append(row_peak)
        total_list.append(jnp.sum(weights, axis=2))
        sum_list.append(
            jnp.einsum(
                "hqk,hdk->hdq",
                weights.astype(jnp.bfloat16),
                value_heads[first_head:last_head],
                preferred_element_type=jnp.float32,
            )
        )
    return (
        jnp.concatenate(peak_list, axis=0),
        jnp.concatenate(total_list, axis=0),
        jnp.concatenate(sum_list, axis=0),
    )


def branch_grads(
    query_heads,
    key_heads,
    value_heads,
    cotan_heads,
    log_norm,
    out_dot,
    key_valid,
    score_scale,
    want_query,
    want_keys,
):
    query_list, key_list, value_list = ([], [], [])
    for first_head, last_head in head_ranges(query_heads.shape[0]):
        query_block = query_heads[first_head:last_head]
        key_block = key_heads[first_head:last_head]
        cotan_block = cotan_heads[first_head:last_head]
        raw_scores = scores_of(query_block, key_block, score_scale)
        key_keep = key_valid[first_head:last_head][:, None, :]
        weights = jnp.where(
            key_keep, jnp.exp(raw_scores - log_norm[first_head:last_head][:, :, None]), 0.0
        )
        weight_grads = jnp.einsum(
            "hdq,hdk->hqk",
            cotan_block,
            value_heads[first_head:last_head],
            preferred_element_type=jnp.float32,
        )
        low_grads = (weights * (weight_grads - out_dot[first_head:last_head][:, :, None])).astype(
            jnp.bfloat16
        )
        if want_query:
            query_list.append(
                score_scale
                * jnp.einsum(
                    "hqk,hdk->hdq", low_grads, key_block, preferred_element_type=jnp.float32
                )
            )
        if want_keys:
            key_list.append(
                score_scale
                * jnp.einsum(
                    "hqk,hdq->hdk", low_grads, query_block, preferred_element_type=jnp.float32
                )
            )
            value_list.append(
                jnp.einsum(
                    "hqk,hdq->hdk",
                    weights.astype(jnp.bfloat16),
                    cotan_block,
                    preferred_element_type=jnp.float32,
                )
            )
    query_part = jnp.concatenate(query_list, axis=0) if want_query else None
    key_part = jnp.concatenate(key_list, axis=0) if want_keys else None
    value_part = jnp.concatenate(value_list, axis=0) if want_keys else None
    return (query_part, key_part, value_part)


def head_offsets(head_total, stride):
    return np.arange(head_total) * stride // head_total


def select_rows(array_in, stride):
    head_total = array_in.shape[0]
    offsets = head_offsets(head_total, stride)
    folded = array_in.reshape(array_in.shape[:-1] + (array_in.shape[-1] // stride, stride))
    return jnp.stack(
        [folded[head_index, ..., int(offsets[head_index])] for head_index in range(head_total)]
    )


def spread_rows(array_in, stride, fill_value):
    head_total = array_in.shape[0]
    chosen = np.arange(stride)[None, :] == head_offsets(head_total, stride)[:, None]
    chosen = chosen.reshape((head_total,) + (1,) * (array_in.ndim - 1) + (stride,))
    full = jnp.where(chosen, array_in[..., None], fill_value)
    return full.reshape(array_in.shape[:-1] + (array_in.shape[-1] * stride,))


def to_heads(flat_in):
    return jnp.transpose(flat_in.reshape(flat_in.shape[0], HEADS, -1), (1, 2, 0))


def to_flat(heads_in):
    return jnp.transpose(heads_in, (2, 0, 1)).reshape(heads_in.shape[2], -1)


def local(query_tiles, key_tiles, value_tiles, cotangent, row_lengths):
    tile_count = query_tiles.shape[0]
    score_scale = HEAD ** (-0.5)
    query_heads = to_heads(query_tiles)
    key_heads = to_heads(key_tiles)
    value_heads = to_heads(value_tiles)
    cotan_heads = to_heads(cotangent)
    tile_slot = jnp.arange(tile_count, dtype=jnp.int32)
    tile_valid = tile_slot % ROW < jnp.repeat(row_lengths, ROW, total_repeat_length=tile_count)
    valid_heads = jnp.broadcast_to(tile_valid[None, :], (HEADS, tile_count))
    group_query = select_rows(query_heads, STRIDE_GROUP)
    group_key = select_rows(key_heads, STRIDE_GROUP)
    group_value = select_rows(value_heads, STRIDE_GROUP)
    group_cotan = select_rows(cotan_heads, STRIDE_GROUP)
    group_valid = select_rows(valid_heads, STRIDE_GROUP)
    group_flag = group_valid.astype(jnp.bfloat16)[:, None, :]
    slide_query = select_rows(query_heads, STRIDE_SLIDE)
    slide_key = select_rows(key_heads, STRIDE_SLIDE)
    slide_value = select_rows(value_heads, STRIDE_SLIDE)
    slide_flag = select_rows(valid_heads, STRIDE_SLIDE).astype(jnp.bfloat16)[:, None, :]
    owned_query, owned_key, owned_value, owned_flag = (
        lax.all_to_all(slide_query, "outer", split_axis=0, concat_axis=2, tiled=True),
        lax.all_to_all(slide_key, "outer", split_axis=0, concat_axis=2, tiled=True),
        lax.all_to_all(slide_value, "outer", split_axis=0, concat_axis=2, tiled=True),
        lax.all_to_all(slide_flag, "outer", split_axis=0, concat_axis=2, tiled=True),
    )
    got_group = (
        lax.all_gather(group_key, "inner", axis=2, tiled=True),
        lax.all_gather(group_value, "inner", axis=2, tiled=True),
        lax.all_gather(group_flag, "inner", axis=2, tiled=True),
    )
    got_slide = (
        lax.all_gather(owned_key, "inner", axis=2, tiled=True),
        lax.all_gather(owned_value, "inner", axis=2, tiled=True),
        lax.all_gather(owned_flag, "inner", axis=2, tiled=True),
    )
    near_peak, near_total, near_sum = branch_stats(
        query_heads, key_heads, value_heads, valid_heads, score_scale
    )
    remote_group_key = got_group[0]
    remote_group_value = got_group[1]
    remote_group_valid = got_group[2][:, 0, :] > 0.5
    group_peak, group_total, group_sum = branch_stats(
        group_query, remote_group_key, remote_group_value, remote_group_valid, score_scale
    )
    slide_all_key = got_slide[0]
    slide_all_value = got_slide[1]
    slide_all_valid = got_slide[2][:, 0, :] > 0.5
    owner_peak, owner_total, owner_sum = branch_stats(
        owned_query, slide_all_key, slide_all_value, slide_all_valid, score_scale
    )
    slide_peak, slide_total, slide_sum = (
        lax.all_to_all(owner_peak[:, None, :], "outer", split_axis=2, concat_axis=0, tiled=True),
        lax.all_to_all(owner_total[:, None, :], "outer", split_axis=2, concat_axis=0, tiled=True),
        lax.all_to_all(owner_sum, "outer", split_axis=2, concat_axis=0, tiled=True),
    )
    slide_peak = slide_peak[:, 0, :]
    slide_total = slide_total[:, 0, :]
    group_peak_full = spread_rows(group_peak, STRIDE_GROUP, NEGATIVE_FILL)
    slide_peak_full = spread_rows(slide_peak, STRIDE_SLIDE, NEGATIVE_FILL)
    best_peak = jnp.maximum(jnp.maximum(near_peak, group_peak_full), slide_peak_full)
    near_weight = jnp.exp(near_peak - best_peak)
    group_weight = jnp.exp(group_peak_full - best_peak)
    slide_weight = jnp.exp(slide_peak_full - best_peak)
    denominator = (
        near_total * near_weight
        + spread_rows(group_total, STRIDE_GROUP, 0.0) * group_weight
        + spread_rows(slide_total, STRIDE_SLIDE, 0.0) * slide_weight
    )
    numerator = (
        near_sum * near_weight[:, None, :]
        + spread_rows(group_sum, STRIDE_GROUP, 0.0) * group_weight[:, None, :]
        + spread_rows(slide_sum, STRIDE_SLIDE, 0.0) * slide_weight[:, None, :]
    )
    attended = (numerator / denominator[:, None, :]).astype(jnp.bfloat16)
    log_norm = best_peak + jnp.log(denominator)
    out_dot = jnp.sum(cotan_heads.astype(jnp.float32) * attended.astype(jnp.float32), axis=1)
    near_query, near_key, near_value = branch_grads(
        query_heads,
        key_heads,
        value_heads,
        cotan_heads,
        log_norm,
        out_dot,
        valid_heads,
        score_scale,
        True,
        True,
    )
    group_lse = select_rows(log_norm, STRIDE_GROUP)
    group_dot = select_rows(out_dot, STRIDE_GROUP)
    group_query_grad = branch_grads(
        group_query,
        remote_group_key,
        remote_group_value,
        group_cotan,
        group_lse,
        group_dot,
        remote_group_valid,
        score_scale,
        True,
        False,
    )[0]
    got_group_rows = (
        lax.all_gather(group_query, "inner", axis=2, tiled=True),
        lax.all_gather(group_cotan, "inner", axis=2, tiled=True),
    )
    got_group_stats = (
        lax.all_gather(group_lse, "inner", axis=1, tiled=True),
        lax.all_gather(group_dot, "inner", axis=1, tiled=True),
    )
    unused_group, group_key_grad, group_value_grad = branch_grads(
        got_group_rows[0],
        group_key,
        group_value,
        got_group_rows[1],
        got_group_stats[0],
        got_group_stats[1],
        group_valid,
        score_scale,
        False,
        True,
    )
    slide_cotan = select_rows(cotan_heads, STRIDE_SLIDE)
    slide_lse = select_rows(log_norm, STRIDE_SLIDE)
    slide_dot = select_rows(out_dot, STRIDE_SLIDE)
    owned_cotan = lax.all_to_all(slide_cotan, "outer", split_axis=0, concat_axis=2, tiled=True)
    owned_lse, owned_dot = (
        lax.all_to_all(slide_lse, "outer", split_axis=0, concat_axis=1, tiled=True),
        lax.all_to_all(slide_dot, "outer", split_axis=0, concat_axis=1, tiled=True),
    )
    owned_query_grad, partial_key, partial_value = branch_grads(
        owned_query,
        slide_all_key,
        slide_all_value,
        owned_cotan,
        owned_lse,
        owned_dot,
        slide_all_valid,
        score_scale,
        True,
        True,
    )
    owned_key_grad, owned_value_grad = (
        lax.psum_scatter(
            partial_key.astype(jnp.bfloat16), "inner", scatter_dimension=2, tiled=True
        ).astype(jnp.float32),
        lax.psum_scatter(
            partial_value.astype(jnp.bfloat16), "inner", scatter_dimension=2, tiled=True
        ).astype(jnp.float32),
    )
    slide_query_grad, slide_key_grad, slide_value_grad = (
        lax.all_to_all(
            as_sent(owned_query_grad), "outer", split_axis=2, concat_axis=0, tiled=True
        ).astype(owned_query_grad.dtype),
        lax.all_to_all(
            owned_key_grad.astype(jnp.bfloat16), "outer", split_axis=2, concat_axis=0, tiled=True
        ).astype(owned_key_grad.dtype),
        lax.all_to_all(
            owned_value_grad.astype(jnp.bfloat16), "outer", split_axis=2, concat_axis=0, tiled=True
        ).astype(owned_value_grad.dtype),
    )
    query_grad = (
        near_query
        + spread_rows(group_query_grad, STRIDE_GROUP, 0.0)
        + spread_rows(slide_query_grad, STRIDE_SLIDE, 0.0)
    )
    key_grad = (
        near_key
        + spread_rows(group_key_grad, STRIDE_GROUP, 0.0)
        + spread_rows(slide_key_grad, STRIDE_SLIDE, 0.0)
    )
    value_grad = (
        near_value
        + spread_rows(group_value_grad, STRIDE_GROUP, 0.0)
        + spread_rows(slide_value_grad, STRIDE_SLIDE, 0.0)
    )
    return (
        to_flat(attended),
        to_flat(query_grad.astype(jnp.bfloat16)),
        to_flat(key_grad.astype(jnp.bfloat16)),
        to_flat(value_grad.astype(jnp.bfloat16)),
    )


BF = jnp.bfloat16
F32 = jnp.float32
LANES = 128
SCALE = HEAD ** (-0.5)
PAIR = 2 * HEAD
PAIRS = HEADS // 2
MESH = pl.DeviceIdType.MESH


def iota2(shape, axis):
    return lax.broadcasted_iota(jnp.int32, shape, axis)


def original_tile(j):
    return (j & 7) * 16 + ((j >> 3) & 3) * 4 + (j >> 5)


def permute_matrix(inverse):
    shape = (LANES, LANES)
    j, i = (iota2(shape, 1), iota2(shape, 0)) if inverse else (iota2(shape, 0), iota2(shape, 1))
    return (original_tile(j) == i).astype(F32).astype(BF)


def identity(size):
    shape = (size, size)
    return (iota2(shape, 0) == iota2(shape, 1)).astype(F32).astype(BF)


def key_bias(len_ref):
    tile = original_tile(iota2((LANES, LANES), 0))
    row = tile >> 5
    length = jnp.full((LANES, LANES), len_ref[0], jnp.int32)
    for index in range(1, 4):
        length = jnp.where(row == index, len_ref[index], length)
    return jnp.where((tile & 31) < length, 0.0, NEGATIVE_FILL).astype(F32)


def mm(a, b):
    return jnp.dot(a, b, preferred_element_type=F32)


def mm_t(a, b):
    return lax.dot_general(a, b, (((1,), (1,)), ((), ())), preferred_element_type=F32)


def slide_row(r):
    return (r % 4) * 32 + (r // 4) * 8


def head_lanes(lane, p, e):
    return ((lane - (PAIR * p + HEAD * e)) & (LANES - 1)) < HEAD


def flag_lane(p):
    return (PAIR * (p + 1)) & (LANES - 1)


def as_mask(keep):
    return keep.astype(F32).astype(BF)


def head_masks(p):
    lane = iota2((1, LANES), 1)
    masks = [as_mask(head_lanes(lane, p, e)) for e in range(2)]
    flags = [as_mask(lane == flag_lane(p) + e) for e in range(3)]
    return masks, flags


def two_heads(x, masks, flags=None):
    parts = [x * masks[e] for e in range(2)]
    if flags is not None:
        parts = [part + flag for part, flag in zip(parts, flags)]
    return jnp.concatenate(parts, axis=0)


def pieces_of(p):
    base, spot = p // 4 * 3, p % 4
    if spot == 0:
        return [(base, 0, 96)]
    if spot == 1:
        return [(base, 96, 128), (base + 1, 0, 64)]
    if spot == 2:
        return [(base + 1, 64, 128), (base + 2, 0, 32)]
    return [(base + 2, 32, 128)]


def pair_tile(x, p):
    parts = pieces_of(p)
    tiles = [x[:, t * LANES : (t + 1) * LANES] for t, _, _ in parts]
    if len(tiles) == 1:
        return tiles[0]
    lane = iota2(tiles[0].shape, 1)
    return jnp.where(lane >= parts[0][1], tiles[0], tiles[1])


SLOT_ROWS, S_ROW, G_ROWS = 48, 96, 112
SOON = 2


def swapped(p):
    return jnp.where(lax.rem(2 * p, 5) == 0, 1, 0)


def head_of(h, slot):
    return slot ^ (1 if 2 * h % 5 == 0 else 0)


def relative(lane, p, e):
    return (lane - (PAIR * p + HEAD * e)) & (LANES - 1)


def roll_lanes(x, shift):
    return pltpu.roll(x, shift, x.ndim - 1)


def fold_rows(full, rel):
    low, high = full[..., 0:16, :], full[..., 16:32, :]
    return jnp.where((rel >= 32) & (rel < 96), low, roll_lanes(high, 64))


def unfold_rows(x):
    return jnp.concatenate([x, roll_lanes(x, 64)], axis=x.ndim - 2)


def packed(rel, q, k, v, c):
    first = jnp.where(rel < 48, q, jnp.where(rel < 96, roll_lanes(k, 48), roll_lanes(v, 96)))
    return first, fold_rows(jnp.where(rel < 48, v, roll_lanes(c, 48)), rel[:16])


def prep_pair(x, p, bias=None):
    tile = pair_tile(x, p)
    lane = iota2(tile.shape, 1)
    flag = flag_lane(p)
    if bias is not None:
        tile = jnp.where((lane == flag) | (lane == flag + 1), bias, tile)
    first, second = [tile[slide_row(2 * p + e) :][:8] for e in range(2)]
    lane = iota2(first.shape, 1)
    slide = jnp.where(head_lanes(lane, p, 1) | (lane == flag + 1), second, first)
    return tile, slide


def near_early(p, tp_ref, pn_ref, ad_ref, kt_ref, vt_ref, eye):
    k, q, v, c = [tp_ref[a, p] for a in range(4)]
    masks, flags = head_masks(p)
    s = mm_t(k, two_heads(q, masks, flags)) * SCALE
    dp = mm_t(v, two_heads(c, masks))
    kt_ref[p] = mm_t(eye, two_heads(k, masks)).astype(BF)
    vt_ref[p] = mm_t(eye, two_heads(v, masks)).astype(BF)
    peak = jnp.max(s, axis=0, keepdims=True)
    weights = jnp.exp(s - peak)
    total = jnp.sum(weights, axis=0, keepdims=True)
    weights = weights * (1.0 / total)
    delta = jnp.sum(weights * dp, axis=0, keepdims=True)
    pn_ref[p] = weights
    ad_ref[p] = weights * (dp - delta)
    return peak + jnp.log(total), delta


def turn(x, shift):
    return pltpu.roll(x, shift & (LANES - 1), 1)


def compact(lane, slots, slides):
    low = jnp.where(lane < 32, slots[0], slots[1])
    return jnp.where(lane < 64, low, jnp.where(lane < 72, slides[0], slides[1]))


def near_stats(p, lse, delta):
    shape = (8, LANES)
    row, lane = iota2(shape, 0), iota2(shape, 1)

    def wide(x, e):
        return jnp.broadcast_to(x[:, e * LANES : (e + 1) * LANES], shape)

    heads = [jnp.where(row == 0, wide(lse, e), wide(delta, e)) for e in range(2)]
    slots = [turn(heads[head_of(p, slot)], 32 * slot - p // 2 * 32) for slot in range(2)]
    slides = [turn(heads[e], 64 + 8 * e - slide_row(2 * p + e)) for e in range(2)]
    return compact(lane, slots, slides)[0:2]


def near_late(p, r2_ref, tp_ref, pn_ref, ad_ref, kt_ref, vt_ref, late_ref, turned_ref):
    tile = jnp.concatenate([r2_ref[p]] * 4, axis=0)
    lane = iota2((1, LANES), 1)
    start = p // 2 * 32
    in_group = (lane >= start) & (lane < start + 32)
    scales, shifts = [], []
    for e in range(2):
        at = slide_row(2 * p + e)
        group = turn(tile, start - 32 * head_of(p, e))
        slide = turn(tile, at - 64 - 8 * e)
        in_slide = (lane >= at) & (lane < at + 8)
        for index, (found, fill) in enumerate(((scales, 1.0), (shifts, 0.0))):
            value = jnp.where(in_slide, slide[index : index + 1], fill)
            found.append(jnp.where(in_group, group[index : index + 1], value))
    scale = jnp.concatenate(scales, axis=1)
    shift = jnp.concatenate(shifts, axis=1)
    weights = pn_ref[p]
    low = (weights * scale).astype(BF)
    grads = (ad_ref[p] * (scale * SCALE) - weights * (scale * shift * SCALE)).astype(BF)
    masks, _ = head_masks(p)
    late_ref[0, p] = mm(grads, two_heads(tp_ref[1, p], masks))
    late_ref[1, p] = mm(low, two_heads(tp_ref[3, p], masks))

    def stacked(x):
        return jnp.concatenate([x[:, :LANES], x[:, LANES:]], axis=0)

    for index, value in enumerate((mm(vt_ref[p], stacked(low)), mm(kt_ref[p], stacked(grads)))):
        value = value.astype(BF)
        for t, first, last in pieces_of(p):
            turned_ref[index, t * LANES + first : t * LANES + last] = value[first:last]


def branch(s):
    peak = jnp.max(s, axis=0, keepdims=True)
    weights = jnp.exp(s - peak)
    total = jnp.sum(weights, axis=0, keepdims=True)
    return weights, peak, total, peak + jnp.log(total)


def rows_of(row, first, second, third):
    first, second, third = [jnp.broadcast_to(x, row.shape) for x in (first, second, third)]
    return jnp.where(row == 0, first, jnp.where(row == 1, second, third))


def slide_scores(masks, flags, gr_ref, skv_ref):
    kv = skv_ref[...].reshape(-1, LANES)
    sources = gr_ref.shape[0]
    wide = gr_ref[:, S_ROW:G_ROWS].astype(F32)
    q, c = [wide[:, a : a + 8].reshape(sources * 8, LANES).astype(BF) for a in (0, 8)]
    q2, c2 = two_heads(q, masks, flags), two_heads(c, masks)
    both = mm_t(kv, jnp.concatenate([q2, c2], axis=0)).reshape(-1, 16, 2 * LANES)
    s = both[:, 0:8, :LANES].reshape(-1, LANES) * SCALE
    dp = both[:, 8:16, LANES:].reshape(-1, LANES)
    return kv, q2, c2, s, dp


def near_of(row, lane, ns_ref):
    slots, slide = [[None] * 2, [None] * 2], None

    def pick(keep, value, old):
        return value if old is None else jnp.where(keep, value, old)

    for source in range(8):
        j, q = divmod(source, 4)
        tile = jnp.concatenate([ns_ref[source]] * 4, axis=0)
        for slot in range(2):
            slots[slot][j] = pick((lane >> 5) == q, turn(tile, q * 32 - 32 * slot), slots[slot][j])
        first, second = [turn(tile, 64 * e + 8 * source - 64 - 8 * e) for e in range(2)]
        both = jnp.where(lane < 64, first, second)
        slide = pick(((lane & 63) >> 3) == source, both, slide)
    return [
        [rows_of(row, *[x[i : i + 1] for x in (slots[0][j], slots[1][j], slide)]) for i in range(2)]
        for j in range(2)
    ]


def crossed(row, lane, p, slide, group, fill):
    first = lax.rem(2 * p, 5) == 0
    any_head = jnp.logical_or(first, lax.rem(2 * p + 1, 5) == 0)
    e = jnp.where(first, 0, 1)
    at = p // 2 * 8
    source = jnp.broadcast_to(slide, row.shape)
    found, to_slide = [], None
    for j in range(2):
        chosen = jnp.broadcast_to(group[j], row.shape)
        to_group = None
        for q in range(4):
            here, there = q * 32 + at, (4 * j + q) * 8 + e * 64
            moved = turn(source, here - there + LANES)
            to_group = moved if q == 0 else jnp.where((lane >> 5) == q, moved, to_group)
            moved = turn(chosen, there - here + LANES)
            same = ((lane & 63) >> 3) == 4 * j + q
            to_slide = moved if to_slide is None else jnp.where(same, moved, to_slide)
        found.append(to_group)
    in_group = (row == 1) & ((lane & 31) >> 3 == p // 2) & any_head
    in_slide = (row == 2) & ((lane >> 6) == e) & any_head
    return [
        jnp.where(in_group | in_slide, jnp.where(row == 2, to_slide, to_group), fill)
        for to_group in found
    ]


class Slot:
    def __init__(self, p, e, gr_ref, at, group_bias, flag):
        sources = gr_ref.shape[0]
        lane = iota2((1, LANES), 1)
        self.rel = relative(lane, p, e)
        self.own, self.second = [as_mask((self.rel >= low) & (self.rel < low + 48)) for low in (0, 48)]
        head = self.rel < 48
        first = gr_ref[:, at : at + 32].reshape(sources * 32, LANES)
        rest = unfold_rows(gr_ref[:, at + 32 : at + 48].astype(F32)).reshape(sources * 32, LANES)
        wide = first.astype(F32)
        self.q = first * self.own + flag
        key = roll_lanes(wide, LANES - 48).astype(BF) * self.own
        self.k = key + group_bias
        self.v = jnp.where(self.rel < 32, roll_lanes(wide, 32), rest).astype(BF) * self.own
        self.c = roll_lanes(rest, LANES - 48).astype(BF) * self.own
        self.moved_k = first * self.second
        self.moved_c = rest.astype(BF) * self.second
        spread = jnp.where(self.rel >= 96, roll_lanes(wide, 96), wide)
        self.moved_q = spread.astype(BF) * as_mask((self.rel >= 96) | ((self.rel >= 32) & head))

    def scores(self, eye):
        self.parts = [
            branch(mm_t(self.k, self.q[j * LANES : (j + 1) * LANES]) * SCALE) for j in range(2)
        ]
        self.dps = [mm_t(self.v, self.c[j * LANES : (j + 1) * LANES]) for j in range(2)]
        self.deltas = [
            jnp.sum(part[0] * dp, axis=0, keepdims=True) / part[2]
            for part, dp in zip(self.parts, self.dps)
        ]
        both = jnp.concatenate([self.v, self.moved_k], axis=0)
        self.turned = mm_t(eye, both).astype(BF)

    def results(self, factors, deltas, eye2, sources):
        lows, grads = [], []
        for j, (part, dp) in enumerate(zip(self.parts, self.dps)):
            weights = part[0] * factors[j]
            lows.append(weights.astype(BF))
            grads.append((weights * (dp - deltas[j]) * SCALE).astype(BF))
        lows, grads = jnp.concatenate(lows, axis=1), jnp.concatenate(grads, axis=1)
        rest = mm(
            jnp.concatenate([grads, lows], axis=1), jnp.concatenate([self.moved_q, self.moved_c], axis=0)
        )
        first = mm(self.turned, jnp.concatenate([lows, grads], axis=0)).astype(BF)
        first = jnp.where(self.rel < 96, mm_t(eye2, first), rest)
        rest = fold_rows(rest.reshape(sources, 32, LANES), self.rel)
        return first.astype(BF).reshape(sources, 32, LANES), rest.astype(BF)


class Exchange:
    def __init__(self, count, make, every, first=1):
        self.count, self.make, self.every, self.first = count, make, every, first

    def start(self):
        @pl.loop(self.first, self.count)
        def _(step):
            self.make(step).start()

    def wait_recv(self):
        self.every.wait_recv()

    def wait_send(self):
        self.every.wait_send()


def wrapped(value, count):
    return jnp.where(value >= count, value - count, value)


def whole_kernel(
    inner, outers, len_hbm, q_hbm, k_hbm, v_hbm, c_hbm, att_ref, dq_ref, dk_ref, dv_ref,
    len_ref, loaded, load_sem, tp, gm, gr, skv_s, skv, pn, ad, kt, vt, ns_s, ns_r, r2_s, r2_r,
    r4_s, r4_r, xs, xr, sg_s, sg_r, late, turned, acc, whole, send_sem, recv_sem, x_send, x_recv,
):
    outer, me = lax.axis_index("outer"), lax.axis_index("inner")
    p = me

    def scope(name):
        return jax.named_scope(name)

    def copy_to(src, dst, sems, index, device):
        return pltpu.make_async_remote_copy(
            src_ref=src,
            dst_ref=dst,
            send_sem=sems[0].at[index],
            recv_sem=sems[1].at[index],
            device_id=device,
            device_id_type=MESH,
        )

    def exchange(index, source, target, size):
        sems, next_place = (send_sem, recv_sem), wrapped(me + 1, inner)

        def make(step):
            peer = step - jnp.where(step <= me, 1, 0)
            return copy_to(source(peer), target(me), sems, index, (outer, peer))

        return Exchange(inner, make, copy_to(size, size, sems, index, (outer, next_place)))

    def across(index, source, target, size):
        sems, next_place = (x_send, x_recv), wrapped(outer + 1, outers)

        def make(step):
            peer = step - jnp.where(step <= outer, 1, 0)
            return copy_to(source(peer), target, sems, index, (peer, me))

        return Exchange(outers, make, copy_to(size, size, sems, index, (next_place, me)))

    def blocks_exchange(index, src, dst):
        size = dst.at[pl.ds(0, inner - 1)]
        return exchange(index, lambda peer: src.at[peer], lambda mine: dst.at[mine], size)

    def rows_exchange(index, src, dst, first, last):
        rows = pl.ds(first, last - first)
        size = dst.at[pl.ds(0, inner - 1), rows]
        return exchange(index, lambda peer: src.at[peer, rows], lambda mine: dst.at[mine, rows], size)

    some = pl.ds(0, inner - 1)
    half = inner // 2
    mine = me // half * half
    away = half - mine

    def skv_copy(peer, index):
        return copy_to(skv_s.at[peer], skv.at[outer, me], (send_sem, recv_sem), index, (outer, peer))

    skv_size = skv.at[0, pl.ds(0, half)]
    far_skv = Exchange(
        half,
        lambda step: skv_copy(away + step, 0),
        copy_to(skv_size, skv_size, (send_sem, recv_sem), 0, (outer, away)),
        0,
    )
    skv_size = skv.at[0, pl.ds(0, half - 1)]
    close_skv = Exchange(
        half,
        lambda step: skv_copy(mine + wrapped(me - mine + step, half), 10),
        copy_to(skv_size, skv_size, (send_sem, recv_sem), 10, (outer, mine + wrapped(me - mine + 1, half))),
    )
    send_first = rows_exchange(1, gm, gr, 0, SLOT_ROWS)
    send_second = rows_exchange(2, gm, gr, SLOT_ROWS, S_ROW)
    send_qc = rows_exchange(9, gm, gr, S_ROW, G_ROWS)
    send_ns = blocks_exchange(3, ns_s, ns_r)
    send_r2 = blocks_exchange(4, r2_s, r2_r)
    back_first = rows_exchange(5, r4_s, r4_r, 0, SLOT_ROWS)
    back_second = rows_exchange(6, r4_s, r4_r, SLOT_ROWS, S_ROW)
    send_oq = rows_exchange(7, r4_s, r4_r, S_ROW, G_ROWS)
    send_sg = blocks_exchange(8, sg_s, sg_r)
    forwards = []
    for index, first in ((0, mine), (2, away)):
        part = skv.at[outer, pl.ds(first, half)]
        size = skv.at[pl.ds(0, outers - 1), pl.ds(0, half)]
        forwards.append(across(index, lambda peer, part=part: part, part, size))
    backwards = []
    for index, first, last in ((1, 0, SOON), (3, SOON, inner)):
        places = pl.ds(first, last - first)
        size = xr.at[pl.ds(0, outers - 1), places]
        backwards.append(
            across(index, lambda peer, places=places: xs.at[peer, places], xr.at[outer, places], size)
        )

    barrier = pltpu.get_barrier_semaphore()
    with scope("load_start"):
        loads = [
            pltpu.make_async_copy(ref, loaded.at[a], load_sem.at[a])
            for a, ref in enumerate((k_hbm, q_hbm, v_hbm, c_hbm))
        ]
        loads.append(pltpu.make_async_copy(len_hbm, len_ref, load_sem.at[4]))
        for index in (4, 0, 2, 1, 3):
            loads[index].start()
    with scope("greet"):

        @pl.loop(1, inner)
        def _(step):
            pl.semaphore_signal(
                barrier, inc=1, device_id=(outer, wrapped(me + step, inner)), device_id_type=MESH
            )

        @pl.loop(1, outers)
        def _(step):
            pl.semaphore_signal(
                barrier, inc=1, device_id=(wrapped(outer + step, outers), me), device_id_type=MESH
            )

    perm = permute_matrix(False)
    eye = identity(LANES)
    with scope("load_wait"):
        loads[4].wait()
        loads[0].wait()
        loads[2].wait()
    with scope("prep_kv"):
        bias = key_bias(len_ref)
        xk = mm(perm, loaded[0])
        xv = mm(perm, loaded[2])
        groups = []
        for h in range(PAIRS):
            first = h // 2 * 32
            rows = slice(first, first + 32)
            tile, key_slide = prep_pair(xk, h, bias)
            tp[0, h] = tile.astype(BF)
            groups.append([tile[rows]])
            tile, value_slide = prep_pair(xv, h)
            tp[2, h] = tile.astype(BF)
            groups[h].append(tile[rows])
            both = jnp.concatenate([key_slide, value_slide], axis=0)
            lane = iota2(both.shape, 1)
            for index in range(2):
                part = bias[first + 16 * index : first + 16 * index + 16]
                both = jnp.where(lane == flag_lane(h) + 2 + index, part, both)
            skv_s[h] = both.astype(BF)
    def pack_slot(h, slot):
        rel = relative(iota2((32, LANES), 1), h, head_of(h, slot))
        first, rest = packed(rel, *groups[h])
        at = SLOT_ROWS * slot
        gm[h, at : at + 32] = first.astype(BF)
        gm[h, at + 32 : at + 48] = rest.astype(BF)

    with scope("prep_qc"):
        loads[1].wait()
        loads[3].wait()
        xq = mm(perm, loaded[1])
        xc = mm(perm, loaded[3])
        slides = []
        for h in range(PAIRS):
            rows = slice(h // 2 * 32, h // 2 * 32 + 32)
            tile, query_slide = prep_pair(xq, h)
            tp[1, h] = tile.astype(BF)
            groups[h].insert(0, tile[rows])
            tile, cotan_slide = prep_pair(xc, h)
            tp[3, h] = tile.astype(BF)
            groups[h].append(tile[rows])
            slides.append(jnp.concatenate([query_slide, cotan_slide], axis=0))
            pack_slot(h, 0)
    with scope("prep_second"):
        for h in range(PAIRS):
            pack_slot(h, 1)
            gm[h, S_ROW:G_ROWS] = slides[h].astype(BF)
        gr[me] = gm[me]
        skv[outer, me] = skv_s[me]

    def near_forward():
        with scope("near_early"):
            for h in range(PAIRS):
                lse, delta = near_early(h, tp, pn, ad, kt, vt, eye)
                ns_s[h] = near_stats(h, lse, delta)

    ahead = me < inner // 2

    @pl.when(ahead)
    def _():
        near_forward()

    with scope("barrier_wait"):
        pl.semaphore_wait(barrier, inner - 1 + outers - 1)
    with scope("send_skv"):
        far_skv.start()
        close_skv.start()

    @pl.when(jnp.logical_not(ahead))
    def _():
        near_forward()

    with scope("send_first"):
        send_ns.start()
        send_first.start()
    with scope("send_ns"):
        send_qc.start()
        ns_r[me] = ns_s[me]
    with scope("close_wait"):
        close_skv.wait_recv()
    with scope("forward"):
        forwards[0].start()
    with scope("send_second"):
        send_second.start()
    with scope("far_wait"):
        far_skv.wait_recv()
    with scope("forward2"):
        forwards[1].start()
    masks, flags = head_masks(p)
    row, lane = iota2((8, LANES), 0), iota2((8, LANES), 1)
    eye2 = identity(2 * LANES)

    swap = swapped(p)
    with scope("bias"):
        near_keys = skv[outer].astype(F32)
        near_keys = jnp.concatenate([near_keys, pltpu.roll(near_keys, LANES - 1, 2)], axis=1)
        group_bias = near_keys.reshape(inner * 32, LANES).astype(BF) * flags[2]
    with scope("first_wait"):
        send_first.wait_recv()
    with scope("first_scores"):
        first = Slot(p, swap, gr, 0, group_bias, flags[2])
        first.scores(eye)
    with scope("ns_wait"):
        send_ns.wait_recv()
    with scope("first_merge"):
        near = near_of(row, lane, ns_r)
        first_factors, first_deltas, first_shares = [], [], []
        for j in range(2):
            near_lse, near_delta = near[j][0][0:1], near[j][1][0:1]
            _, peak, _, own = first.parts[j]
            best = jnp.maximum(near_lse, own)
            parts = [jnp.exp(x - best) for x in (near_lse, own)]
            total = parts[0] + parts[1]
            inverse = 1.0 / total
            first_factors.append(jnp.exp(peak - best - jnp.log(total)))
            first_deltas.append((parts[0] * near_delta + parts[1] * first.deltas[j]) * inverse)
            first_shares.append(parts[0] * inverse)
    with scope("first_results"):
        main, rest = first.results(first_factors, first_deltas, eye2, inner)
        r4_s[:, 0:32] = main
        r4_s[:, 32:48] = rest
    with scope("first_back"):
        back_first.start()
    with scope("forward_wait"):
        for sent in forwards:
            sent.wait_recv()
        send_qc.wait_recv()
    with scope("slide_scores"):
        skv_all, qs2, cs2, s, slide_dp = slide_scores(masks, flags, gr, skv)
        slide_weights, slide_peak, slide_total, slide_lse = branch(s)
        slide_delta = jnp.sum(slide_weights * slide_dp, axis=0, keepdims=True) / slide_total
        skv_t = mm_t(eye, skv_all).astype(BF)
    with scope("second_wait"):
        send_second.wait_recv()
    with scope("second_scores"):
        second = Slot(p, 1 - swap, gr, SLOT_ROWS, group_bias, flags[2])
        second.scores(eye)
    with scope("second_merge"):
        other = crossed(row, lane, p, slide_lse, [x[3] for x in second.parts], NEGATIVE_FILL)
        other_delta = crossed(row, lane, p, slide_delta, second.deltas, 0.0)

        def on_rows(group, slide):
            return jnp.where(row == 2, slide, group)

        factors, deltas, own_shares, own_moved = [], [], [], []
        for j in range(2):
            _, peak, _, group_lse = second.parts[j]
            own = on_rows(group_lse, slide_lse)
            best = jnp.maximum(jnp.maximum(near[j][0], own), other[j])
            parts = [jnp.exp(x - best) for x in (near[j][0], own, other[j])]
            total = parts[0] + parts[1] + parts[2]
            inverse = 1.0 / total
            factors.append(jnp.exp(on_rows(peak, slide_peak) - best - jnp.log(total)))
            delta = parts[0] * near[j][1] + parts[2] * other_delta[j]
            delta = (delta + parts[1] * on_rows(second.deltas[j], slide_delta)) * inverse
            deltas.append(delta)
            own_shares.append(parts[0] * inverse)
            own_moved.append(delta - near[j][1])
    with scope("slide_bwd"):
        weights = slide_weights * factors[0][2:3]
        grads = weights * (slide_dp - deltas[0][2:3]) * SCALE
        blocks = [x.reshape(-1, 8, LANES) for x in (grads, weights)]
        empty = jnp.zeros_like(blocks[0])
        mixed = jnp.concatenate(
            [
                jnp.concatenate([blocks[0], empty], axis=2),
                jnp.concatenate([empty, blocks[1]], axis=2),
            ],
            axis=1,
        )
        mixed = mixed.reshape(-1, 2 * LANES).astype(BF)
        xs[...] = mm(mixed, jnp.concatenate([qs2, cs2], axis=0)).astype(BF).reshape(xs.shape)
    with scope("send_x"):
        for sent in backwards:
            sent.start()
    with scope("r2_tiles"):
        first_moved = [first_deltas[j] - near[j][1][0:1] for j in range(2)]
        for source in range(inner):
            j, q = divmod(source, 4)
            tiles = [jnp.where(row == 0, first_shares[j], first_moved[j])]
            for at in (1, 2):
                pair = [x[j][at : at + 1] for x in (own_shares, own_moved)]
                tiles.append(jnp.where(row == 0, *pair))
            slots = [turn(tiles[slot], 32 * slot - 32 * q) for slot in range(2)]
            slides = [turn(tiles[2], 64 + 8 * e - 64 * e - 8 * source) for e in range(2)]
            r2_s[source] = compact(lane, slots, slides)[0:2]
    with scope("send_r2"):
        send_r2.start()
        r2_r[me] = r2_s[me]
    with scope("second_results"):
        main, rest = second.results(
            [x[1:2] for x in factors], [x[1:2] for x in deltas], eye2, inner
        )
        r4_s[:, 48:80] = main
        r4_s[:, 80:96] = rest
    with scope("second_back"):
        back_second.start()
    with scope("slide_q"):
        both = mm_t(eye2, mm(skv_t, mixed).astype(BF))
        quarter = LANES // 2
        head0 = head_lanes(iota2((quarter, LANES), 1), p, 0)
        query = jnp.where(head0, both[0:quarter], both[quarter:LANES])
        out = jnp.where(head0, both[LANES : 3 * quarter], both[3 * quarter : 4 * quarter])
        blocks = [x.reshape(inner, 8, LANES) for x in (out, query)]
        r4_s[:, S_ROW:G_ROWS] = jnp.concatenate(blocks, axis=1).astype(BF)
    with scope("send_oq"):
        send_oq.start()
        r4_r[me] = r4_s[me]
    with scope("clear"):
        acc[0:2] = jnp.zeros((2,) + acc.shape[1:], F32)
    soon = jnp.where(me < SOON, SOON, SOON + 1)
    for sent, places, steps in (
        (backwards[0], slice(0, SOON), (1, soon)),
        (backwards[1], slice(SOON, inner), (soon, inner)),
    ):
        with scope("x_wait"):
            sent.wait_recv()
        with scope("x_sum"):
            total = xs[outer, places].astype(F32)
            for step in range(1, outers):
                total = total + xr[wrapped(outer + step, outers), places].astype(F32)
            sg_s[places] = total.astype(BF)
        with scope("send_sg"):

            @pl.loop(*steps)
            def _(step):
                send_sg.make(step).start()

    sg_r[me] = sg_s[me]
    with scope("r2_wait"):
        send_r2.wait_recv()
    with scope("near_late1"):
        for h in range(PAIRS):
            near_late(h, r2_r, tp, pn, ad, kt, vt, late, turned)
    with scope("collect"):
        for a in range(2):
            for t in range(D_TILES):
                value = None
                for h in range(PAIRS):
                    for tile, first, last in pieces_of(h):
                        if tile == t:
                            piece = late[a, h]
                            lane_full = iota2(piece.shape, 1)
                            value = piece if value is None else jnp.where(lane_full >= first, piece, value)
                acc[2 + a, :, t * LANES : (t + 1) * LANES] = value
    with scope("drain"):
        for sent in (far_skv, close_skv, send_first, send_second, send_qc, send_ns, *forwards, send_r2, *backwards):
            sent.wait_send()
    for slot, sent in enumerate((back_first, back_second)):
        with scope("back_wait%d" % slot):
            sent.wait_recv()
        with scope("back_add%d" % slot):
            at = SLOT_ROWS * slot
            for h in range(PAIRS):
                add_group(acc, h, head_of(h, slot), r4_r[h, at : at + 32], r4_r[h, at + 32 : at + 48])
    with scope("place"):
        back = permute_matrix(True)
        for a in range(4):
            value = mm(back, acc[a].astype(BF))
            value = value + mm_t(back, turned[a]) if a < 2 else value
            for t in range(D_TILES):
                whole[a, t] = value[:, t * LANES : (t + 1) * LANES]
    for name, waited, blocks, outs in (
        ("oq", send_oq, lambda h: r4_r[h, S_ROW:G_ROWS], ((0, att_ref), (1, dq_ref))),
        ("sg", send_sg, lambda h: sg_r[h], ((2, dk_ref), (3, dv_ref))),
    ):
        with scope(name + "_wait"):
            waited.wait_recv()
        with scope(name + "_add"):
            for h in range(PAIRS):
                add_slide(whole, outs, h, blocks(h))
            for a, ref in outs:
                for t in range(D_TILES):
                    ref[:, t * LANES : (t + 1) * LANES] = whole[a, t].astype(BF)
    with scope("drain_last"):
        for sent in (back_first, back_second, send_oq, send_sg):
            sent.wait_send()


D_TILES = HEADS * HEAD // LANES


def write_kernel(*refs):
    count = len(refs) // 2
    copies = [pltpu.make_async_copy(refs[a], refs[count + a], refs[-1].at[a]) for a in range(count)]
    for copy in copies:
        copy.start()
    for copy in copies:
        copy.wait()


def add_group(acc, h, e, first, rest):
    first, rest = first.astype(F32), unfold_rows(rest.astype(F32))
    start = h // 2 * 32
    lane = iota2(first.shape, 1)
    rel = relative(lane, h, e)
    key = jnp.where(rel < 32, roll_lanes(first, 32), rest)
    values = (first, roll_lanes(first, LANES - 48), key, roll_lanes(rest, LANES - 48))
    for out, value in enumerate(values):
        for t, low, high in pieces_of(h):
            keep = (lane >= low) & (lane < high) & (rel < HEAD)
            cols = slice(t * LANES, (t + 1) * LANES)
            acc[out, start : start + 32, cols] += jnp.where(keep, value, 0.0)


def add_slide(whole, outs, h, block):
    block = block.astype(F32)
    lane = iota2((8, LANES), 1)
    for index, (out, _) in enumerate(outs):
        small = block[8 * index : 8 * index + 8]
        for e in range(2):
            rows = pl.ds(2 * h + e, 8, stride=HEADS)
            for t, first, last in pieces_of(h):
                if max(first, (PAIR * h + HEAD * e) - t * LANES) >= min(last, PAIR * h + HEAD * (e + 1) - t * LANES):
                    continue
                keep = (lane >= first) & (lane < last) & head_lanes(lane, h, e)
                whole[out, t, rows] += jnp.where(keep, small, 0.0)


def fast_local(inner, outers, *args):
    row_lengths, tiles_in = args[4], args[:4]
    tiles, width = tiles_in[0].shape
    vmem = pl.BlockSpec(memory_space=pltpu.VMEM)
    hbm = pl.BlockSpec(memory_space=pltpu.HBM)

    def both(shape, dtype):
        return [pltpu.VMEM(shape, dtype)] * 2

    scratch = [
        pltpu.SMEM(row_lengths.shape, jnp.int32),
        pltpu.VMEM((4, tiles, width), BF),
        pltpu.SemaphoreType.DMA((5,)),
        pltpu.VMEM((4, PAIRS, tiles, LANES), BF),
    ]
    scratch += both((inner, G_ROWS, LANES), BF)
    scratch += [pltpu.VMEM((inner, 16, LANES), BF), pltpu.VMEM((outers, inner, 16, LANES), BF)]
    scratch += both((PAIRS, tiles, 2 * LANES), F32)
    scratch += both((PAIRS, LANES, 2 * LANES), BF)
    scratch += both((inner, 2, LANES), F32) + both((inner, 2, LANES), F32)
    scratch += both((inner, G_ROWS, LANES), BF)
    scratch += both((outers, inner, 16, LANES), BF)
    scratch += both((inner, 16, LANES), BF)
    scratch += [pltpu.VMEM((2, PAIRS, tiles, LANES), F32), pltpu.VMEM((2, width, tiles), BF)]
    scratch += [pltpu.VMEM((4, tiles, width), F32), pltpu.VMEM((4, D_TILES, tiles, LANES), F32)]
    scratch += [pltpu.SemaphoreType.DMA((11,))] * 2 + [pltpu.SemaphoreType.DMA((4,))] * 2
    in_hbm = [pltpu.with_memory_space_constraint(x, pltpu.HBM) for x in (row_lengths, *tiles_in)]
    out = [pltpu.VMEM((tiles, width), BF)] * 4
    in_vmem = pl.pallas_call(
        lambda *refs: whole_kernel(inner, outers, *refs),
        out_shape=out,
        in_specs=[hbm] * 5,
        out_specs=[vmem] * 4,
        scratch_shapes=scratch,
        compiler_params=pltpu.CompilerParams(
            collective_id=0, has_side_effects=True, vmem_limit_bytes=32 * 1024 * 1024
        ),
    )(*in_hbm)
    return tuple(
        pl.pallas_call(
            write_kernel,
            out_shape=[pltpu.HBM((tiles, width), BF)] * 4,
            in_specs=[vmem] * 4,
            out_specs=[hbm] * 4,
            scratch_shapes=[pltpu.SemaphoreType.DMA((4,))],
            compiler_params=pltpu.CompilerParams(vmem_limit_bytes=16 * 1024 * 1024),
        )(*in_vmem)
    )


def solution(mesh):
    in_specs = (P(("outer", "inner"), None),) * 4 + (P(("outer", "inner")),)
    out_specs = (P(("outer", "inner"), None),) * 4
    inner, outers = mesh.shape["inner"], mesh.shape["outer"]

    def step(*args):
        fits = inner == PAIRS and outers == 4
        if fits and args[0].shape == (LANES, HEADS * HEAD):
            return fast_local(inner, outers, *args)
        return local(*args)

    return jax.shard_map(step, mesh=mesh, in_specs=in_specs, out_specs=out_specs, check_vma=False)
```

```python
import jax
import jax.numpy as jnp
import numpy as np
from jax import lax
from jax.experimental import pallas as pl
from jax.experimental.pallas import tpu as pltpu
from jax.sharding import PartitionSpec as P

HEADS = 16
HEAD = 48
ROW = 32
STRIDE_GROUP = 4
STRIDE_SLIDE = 16


NEGATIVE_FILL = -1e30
heads_at_once = 4


def as_sent(value):

    def short(part):
        return part.astype(jnp.bfloat16) if part.dtype == jnp.float32 else part

    return jax.tree.map(short, value)


def head_ranges(head_total):
    step_size = min(head_total, heads_at_once)
    return [(first_head, first_head + step_size) for first_head in range(0, head_total, step_size)]


def scores_of(query_block, key_block, score_scale):
    return (
        jnp.einsum("hdq,hdk->hqk", query_block, key_block, preferred_element_type=jnp.float32)
        * score_scale
    )


def branch_stats(query_heads, key_heads, value_heads, key_valid, score_scale):
    peak_list, total_list, sum_list = ([], [], [])
    for first_head, last_head in head_ranges(query_heads.shape[0]):
        raw_scores = scores_of(
            query_heads[first_head:last_head], key_heads[first_head:last_head], score_scale
        )
        key_keep = key_valid[first_head:last_head][:, None, :]
        masked = jnp.where(key_keep, raw_scores, NEGATIVE_FILL)
        row_peak = jnp.max(masked, axis=2)
        weights = jnp.where(key_keep, jnp.exp(masked - row_peak[:, :, None]), 0.0)
        peak_list.append(row_peak)
        total_list.append(jnp.sum(weights, axis=2))
        sum_list.append(
            jnp.einsum(
                "hqk,hdk->hdq",
                weights.astype(jnp.bfloat16),
                value_heads[first_head:last_head],
                preferred_element_type=jnp.float32,
            )
        )
    return (
        jnp.concatenate(peak_list, axis=0),
        jnp.concatenate(total_list, axis=0),
        jnp.concatenate(sum_list, axis=0),
    )


def branch_grads(
    query_heads,
    key_heads,
    value_heads,
    cotan_heads,
    log_norm,
    out_dot,
    key_valid,
    score_scale,
    want_query,
    want_keys,
):
    query_list, key_list, value_list = ([], [], [])
    for first_head, last_head in head_ranges(query_heads.shape[0]):
        query_block = query_heads[first_head:last_head]
        key_block = key_heads[first_head:last_head]
        cotan_block = cotan_heads[first_head:last_head]
        raw_scores = scores_of(query_block, key_block, score_scale)
        key_keep = key_valid[first_head:last_head][:, None, :]
        weights = jnp.where(
            key_keep, jnp.exp(raw_scores - log_norm[first_head:last_head][:, :, None]), 0.0
        )
        weight_grads = jnp.einsum(
            "hdq,hdk->hqk",
            cotan_block,
            value_heads[first_head:last_head],
            preferred_element_type=jnp.float32,
        )
        low_grads = (weights * (weight_grads - out_dot[first_head:last_head][:, :, None])).astype(
            jnp.bfloat16
        )
        if want_query:
            query_list.append(
                score_scale
                * jnp.einsum(
                    "hqk,hdk->hdq", low_grads, key_block, preferred_element_type=jnp.float32
                )
            )
        if want_keys:
            key_list.append(
                score_scale
                * jnp.einsum(
                    "hqk,hdq->hdk", low_grads, query_block, preferred_element_type=jnp.float32
                )
            )
            value_list.append(
                jnp.einsum(
                    "hqk,hdq->hdk",
                    weights.astype(jnp.bfloat16),
                    cotan_block,
                    preferred_element_type=jnp.float32,
                )
            )
    query_part = jnp.concatenate(query_list, axis=0) if want_query else None
    key_part = jnp.concatenate(key_list, axis=0) if want_keys else None
    value_part = jnp.concatenate(value_list, axis=0) if want_keys else None
    return (query_part, key_part, value_part)


def head_offsets(head_total, stride):
    return np.arange(head_total) * stride // head_total


def select_rows(array_in, stride):
    head_total = array_in.shape[0]
    offsets = head_offsets(head_total, stride)
    folded = array_in.reshape(array_in.shape[:-1] + (array_in.shape[-1] // stride, stride))
    return jnp.stack(
        [folded[head_index, ..., int(offsets[head_index])] for head_index in range(head_total)]
    )


def spread_rows(array_in, stride, fill_value):
    head_total = array_in.shape[0]
    chosen = np.arange(stride)[None, :] == head_offsets(head_total, stride)[:, None]
    chosen = chosen.reshape((head_total,) + (1,) * (array_in.ndim - 1) + (stride,))
    full = jnp.where(chosen, array_in[..., None], fill_value)
    return full.reshape(array_in.shape[:-1] + (array_in.shape[-1] * stride,))


def to_heads(flat_in):
    return jnp.transpose(flat_in.reshape(flat_in.shape[0], HEADS, -1), (1, 2, 0))


def to_flat(heads_in):
    return jnp.transpose(heads_in, (2, 0, 1)).reshape(heads_in.shape[2], -1)


def local(query_tiles, key_tiles, value_tiles, cotangent, row_lengths):
    tile_count = query_tiles.shape[0]
    score_scale = HEAD ** (-0.5)
    query_heads = to_heads(query_tiles)
    key_heads = to_heads(key_tiles)
    value_heads = to_heads(value_tiles)
    cotan_heads = to_heads(cotangent)
    tile_slot = jnp.arange(tile_count, dtype=jnp.int32)
    tile_valid = tile_slot % ROW < jnp.repeat(row_lengths, ROW, total_repeat_length=tile_count)
    valid_heads = jnp.broadcast_to(tile_valid[None, :], (HEADS, tile_count))
    group_query = select_rows(query_heads, STRIDE_GROUP)
    group_key = select_rows(key_heads, STRIDE_GROUP)
    group_value = select_rows(value_heads, STRIDE_GROUP)
    group_cotan = select_rows(cotan_heads, STRIDE_GROUP)
    group_valid = select_rows(valid_heads, STRIDE_GROUP)
    group_flag = group_valid.astype(jnp.bfloat16)[:, None, :]
    slide_query = select_rows(query_heads, STRIDE_SLIDE)
    slide_key = select_rows(key_heads, STRIDE_SLIDE)
    slide_value = select_rows(value_heads, STRIDE_SLIDE)
    slide_flag = select_rows(valid_heads, STRIDE_SLIDE).astype(jnp.bfloat16)[:, None, :]
    owned_query, owned_key, owned_value, owned_flag = (
        lax.all_to_all(slide_query, "outer", split_axis=0, concat_axis=2, tiled=True),
        lax.all_to_all(slide_key, "outer", split_axis=0, concat_axis=2, tiled=True),
        lax.all_to_all(slide_value, "outer", split_axis=0, concat_axis=2, tiled=True),
        lax.all_to_all(slide_flag, "outer", split_axis=0, concat_axis=2, tiled=True),
    )
    got_group = (
        lax.all_gather(group_key, "inner", axis=2, tiled=True),
        lax.all_gather(group_value, "inner", axis=2, tiled=True),
        lax.all_gather(group_flag, "inner", axis=2, tiled=True),
    )
    got_slide = (
        lax.all_gather(owned_key, "inner", axis=2, tiled=True),
        lax.all_gather(owned_value, "inner", axis=2, tiled=True),
        lax.all_gather(owned_flag, "inner", axis=2, tiled=True),
    )
    near_peak, near_total, near_sum = branch_stats(
        query_heads, key_heads, value_heads, valid_heads, score_scale
    )
    remote_group_key = got_group[0]
    remote_group_value = got_group[1]
    remote_group_valid = got_group[2][:, 0, :] > 0.5
    group_peak, group_total, group_sum = branch_stats(
        group_query, remote_group_key, remote_group_value, remote_group_valid, score_scale
    )
    slide_all_key = got_slide[0]
    slide_all_value = got_slide[1]
    slide_all_valid = got_slide[2][:, 0, :] > 0.5
    owner_peak, owner_total, owner_sum = branch_stats(
        owned_query, slide_all_key, slide_all_value, slide_all_valid, score_scale
    )
    slide_peak, slide_total, slide_sum = (
        lax.all_to_all(owner_peak[:, None, :], "outer", split_axis=2, concat_axis=0, tiled=True),
        lax.all_to_all(owner_total[:, None, :], "outer", split_axis=2, concat_axis=0, tiled=True),
        lax.all_to_all(owner_sum, "outer", split_axis=2, concat_axis=0, tiled=True),
    )
    slide_peak = slide_peak[:, 0, :]
    slide_total = slide_total[:, 0, :]
    group_peak_full = spread_rows(group_peak, STRIDE_GROUP, NEGATIVE_FILL)
    slide_peak_full = spread_rows(slide_peak, STRIDE_SLIDE, NEGATIVE_FILL)
    best_peak = jnp.maximum(jnp.maximum(near_peak, group_peak_full), slide_peak_full)
    near_weight = jnp.exp(near_peak - best_peak)
    group_weight = jnp.exp(group_peak_full - best_peak)
    slide_weight = jnp.exp(slide_peak_full - best_peak)
    denominator = (
        near_total * near_weight
        + spread_rows(group_total, STRIDE_GROUP, 0.0) * group_weight
        + spread_rows(slide_total, STRIDE_SLIDE, 0.0) * slide_weight
    )
    numerator = (
        near_sum * near_weight[:, None, :]
        + spread_rows(group_sum, STRIDE_GROUP, 0.0) * group_weight[:, None, :]
        + spread_rows(slide_sum, STRIDE_SLIDE, 0.0) * slide_weight[:, None, :]
    )
    attended = (numerator / denominator[:, None, :]).astype(jnp.bfloat16)
    log_norm = best_peak + jnp.log(denominator)
    out_dot = jnp.sum(cotan_heads.astype(jnp.float32) * attended.astype(jnp.float32), axis=1)
    near_query, near_key, near_value = branch_grads(
        query_heads,
        key_heads,
        value_heads,
        cotan_heads,
        log_norm,
        out_dot,
        valid_heads,
        score_scale,
        True,
        True,
    )
    group_lse = select_rows(log_norm, STRIDE_GROUP)
    group_dot = select_rows(out_dot, STRIDE_GROUP)
    group_query_grad = branch_grads(
        group_query,
        remote_group_key,
        remote_group_value,
        group_cotan,
        group_lse,
        group_dot,
        remote_group_valid,
        score_scale,
        True,
        False,
    )[0]
    got_group_rows = (
        lax.all_gather(group_query, "inner", axis=2, tiled=True),
        lax.all_gather(group_cotan, "inner", axis=2, tiled=True),
    )
    got_group_stats = (
        lax.all_gather(group_lse, "inner", axis=1, tiled=True),
        lax.all_gather(group_dot, "inner", axis=1, tiled=True),
    )
    unused_group, group_key_grad, group_value_grad = branch_grads(
        got_group_rows[0],
        group_key,
        group_value,
        got_group_rows[1],
        got_group_stats[0],
        got_group_stats[1],
        group_valid,
        score_scale,
        False,
        True,
    )
    slide_cotan = select_rows(cotan_heads, STRIDE_SLIDE)
    slide_lse = select_rows(log_norm, STRIDE_SLIDE)
    slide_dot = select_rows(out_dot, STRIDE_SLIDE)
    owned_cotan = lax.all_to_all(slide_cotan, "outer", split_axis=0, concat_axis=2, tiled=True)
    owned_lse, owned_dot = (
        lax.all_to_all(slide_lse, "outer", split_axis=0, concat_axis=1, tiled=True),
        lax.all_to_all(slide_dot, "outer", split_axis=0, concat_axis=1, tiled=True),
    )
    owned_query_grad, partial_key, partial_value = branch_grads(
        owned_query,
        slide_all_key,
        slide_all_value,
        owned_cotan,
        owned_lse,
        owned_dot,
        slide_all_valid,
        score_scale,
        True,
        True,
    )
    owned_key_grad, owned_value_grad = (
        lax.psum_scatter(
            partial_key.astype(jnp.bfloat16), "inner", scatter_dimension=2, tiled=True
        ).astype(jnp.float32),
        lax.psum_scatter(
            partial_value.astype(jnp.bfloat16), "inner", scatter_dimension=2, tiled=True
        ).astype(jnp.float32),
    )
    slide_query_grad, slide_key_grad, slide_value_grad = (
        lax.all_to_all(
            as_sent(owned_query_grad), "outer", split_axis=2, concat_axis=0, tiled=True
        ).astype(owned_query_grad.dtype),
        lax.all_to_all(
            owned_key_grad.astype(jnp.bfloat16), "outer", split_axis=2, concat_axis=0, tiled=True
        ).astype(owned_key_grad.dtype),
        lax.all_to_all(
            owned_value_grad.astype(jnp.bfloat16), "outer", split_axis=2, concat_axis=0, tiled=True
        ).astype(owned_value_grad.dtype),
    )
    query_grad = (
        near_query
        + spread_rows(group_query_grad, STRIDE_GROUP, 0.0)
        + spread_rows(slide_query_grad, STRIDE_SLIDE, 0.0)
    )
    key_grad = (
        near_key
        + spread_rows(group_key_grad, STRIDE_GROUP, 0.0)
        + spread_rows(slide_key_grad, STRIDE_SLIDE, 0.0)
    )
    value_grad = (
        near_value
        + spread_rows(group_value_grad, STRIDE_GROUP, 0.0)
        + spread_rows(slide_value_grad, STRIDE_SLIDE, 0.0)
    )
    return (
        to_flat(attended),
        to_flat(query_grad.astype(jnp.bfloat16)),
        to_flat(key_grad.astype(jnp.bfloat16)),
        to_flat(value_grad.astype(jnp.bfloat16)),
    )


BF = jnp.bfloat16
F32 = jnp.float32
LANES = 128
SCALE = HEAD ** (-0.5)
PAIR = 2 * HEAD
PAIRS = HEADS // 2
MESH = pl.DeviceIdType.MESH


def iota2(shape, axis):
    return lax.broadcasted_iota(jnp.int32, shape, axis)


def original_tile(j):
    return (j & 7) * 16 + ((j >> 3) & 3) * 4 + (j >> 5)


def permute_matrix(inverse):
    shape = (LANES, LANES)
    j, i = (iota2(shape, 1), iota2(shape, 0)) if inverse else (iota2(shape, 0), iota2(shape, 1))
    return (original_tile(j) == i).astype(F32).astype(BF)


def identity(size):
    shape = (size, size)
    return (iota2(shape, 0) == iota2(shape, 1)).astype(F32).astype(BF)


def key_bias(len_ref):
    tile = original_tile(iota2((LANES, LANES), 0))
    row = tile >> 5
    length = jnp.full((LANES, LANES), len_ref[0], jnp.int32)
    for index in range(1, 4):
        length = jnp.where(row == index, len_ref[index], length)
    return jnp.where((tile & 31) < length, 0.0, NEGATIVE_FILL).astype(F32)


def mm(a, b):
    return jnp.dot(a, b, preferred_element_type=F32)


def mm_t(a, b):
    return lax.dot_general(a, b, (((1,), (1,)), ((), ())), preferred_element_type=F32)


def slide_row(r):
    return (r % 4) * 32 + (r // 4) * 8


def head_lanes(lane, p, e):
    return ((lane - (PAIR * p + HEAD * e)) & (LANES - 1)) < HEAD


def flag_lane(p):
    return (PAIR * (p + 1)) & (LANES - 1)


def as_mask(keep):
    return keep.astype(F32).astype(BF)


def head_masks(p):
    lane = iota2((1, LANES), 1)
    masks = [as_mask(head_lanes(lane, p, e)) for e in range(2)]
    flags = [as_mask(lane == flag_lane(p) + e) for e in range(3)]
    return masks, flags


def two_heads(x, masks, flags=None):
    parts = [x * masks[e] for e in range(2)]
    if flags is not None:
        parts = [part + flag for part, flag in zip(parts, flags)]
    return jnp.concatenate(parts, axis=0)


def pieces_of(p):
    base, spot = p // 4 * 3, p % 4
    if spot == 0:
        return [(base, 0, 96)]
    if spot == 1:
        return [(base, 96, 128), (base + 1, 0, 64)]
    if spot == 2:
        return [(base + 1, 64, 128), (base + 2, 0, 32)]
    return [(base + 2, 32, 128)]


def pair_tile(x, p):
    parts = pieces_of(p)
    tiles = [x[:, t * LANES : (t + 1) * LANES] for t, _, _ in parts]
    if len(tiles) == 1:
        return tiles[0]
    lane = iota2(tiles[0].shape, 1)
    return jnp.where(lane >= parts[0][1], tiles[0], tiles[1])


SLOT_ROWS, S_ROW, G_ROWS = 48, 96, 112
SOON = 1


def swapped(p):
    return jnp.where(lax.rem(2 * p, 5) == 0, 1, 0)


def head_of(h, slot):
    return slot ^ (1 if 2 * h % 5 == 0 else 0)


def relative(lane, p, e):
    return (lane - (PAIR * p + HEAD * e)) & (LANES - 1)


def roll_lanes(x, shift):
    return pltpu.roll(x, shift, x.ndim - 1)


def fold_rows(full, rel):
    low, high = full[..., 0:16, :], full[..., 16:32, :]
    return jnp.where((rel >= 32) & (rel < 96), low, roll_lanes(high, 64))


def unfold_rows(x):
    return jnp.concatenate([x, roll_lanes(x, 64)], axis=x.ndim - 2)


def packed(rel, q, k, v, c):
    first = jnp.where(rel < 48, q, jnp.where(rel < 96, roll_lanes(k, 48), roll_lanes(v, 96)))
    return first, fold_rows(jnp.where(rel < 48, v, roll_lanes(c, 48)), rel[:16])


def prep_pair(x, p, bias=None):
    tile = pair_tile(x, p)
    lane = iota2(tile.shape, 1)
    flag = flag_lane(p)
    if bias is not None:
        tile = jnp.where((lane == flag) | (lane == flag + 1), bias, tile)
    first, second = [tile[slide_row(2 * p + e) :][:8] for e in range(2)]
    lane = iota2(first.shape, 1)
    slide = jnp.where(head_lanes(lane, p, 1) | (lane == flag + 1), second, first)
    return tile, slide


def near_early(p, tp_ref, pn_ref, ad_ref, kt_ref, vt_ref, eye):
    k, q, v, c = [tp_ref[a, p] for a in range(4)]
    masks, flags = head_masks(p)
    s = mm_t(k, two_heads(q, masks, flags)) * SCALE
    dp = mm_t(v, two_heads(c, masks))
    kt_ref[p] = mm_t(eye, two_heads(k, masks)).astype(BF)
    vt_ref[p] = mm_t(eye, two_heads(v, masks)).astype(BF)
    peak = jnp.max(s, axis=0, keepdims=True)
    weights = jnp.exp(s - peak)
    total = jnp.sum(weights, axis=0, keepdims=True)
    weights = weights * (1.0 / total)
    delta = jnp.sum(weights * dp, axis=0, keepdims=True)
    pn_ref[p] = weights
    ad_ref[p] = weights * (dp - delta)
    return peak + jnp.log(total), delta


def turn(x, shift):
    return pltpu.roll(x, shift & (LANES - 1), 1)


def compact(lane, slots, slides):
    low = jnp.where(lane < 32, slots[0], slots[1])
    return jnp.where(lane < 64, low, jnp.where(lane < 72, slides[0], slides[1]))


def near_stats(p, lse, delta):
    shape = (8, LANES)
    row, lane = iota2(shape, 0), iota2(shape, 1)

    def wide(x, e):
        return jnp.broadcast_to(x[:, e * LANES : (e + 1) * LANES], shape)

    heads = [jnp.where(row == 0, wide(lse, e), wide(delta, e)) for e in range(2)]
    slots = [turn(heads[head_of(p, slot)], 32 * slot - p // 2 * 32) for slot in range(2)]
    slides = [turn(heads[e], 64 + 8 * e - slide_row(2 * p + e)) for e in range(2)]
    return compact(lane, slots, slides)[0:2]


def near_late(p, r2_ref, tp_ref, pn_ref, ad_ref, kt_ref, vt_ref, late_ref, turned_ref):
    tile = jnp.concatenate([r2_ref[p]] * 4, axis=0)
    lane = iota2((1, LANES), 1)
    start = p // 2 * 32
    in_group = (lane >= start) & (lane < start + 32)
    scales, shifts = [], []
    for e in range(2):
        at = slide_row(2 * p + e)
        group = turn(tile, start - 32 * head_of(p, e))
        slide = turn(tile, at - 64 - 8 * e)
        in_slide = (lane >= at) & (lane < at + 8)
        for index, (found, fill) in enumerate(((scales, 1.0), (shifts, 0.0))):
            value = jnp.where(in_slide, slide[index : index + 1], fill)
            found.append(jnp.where(in_group, group[index : index + 1], value))
    scale = jnp.concatenate(scales, axis=1)
    shift = jnp.concatenate(shifts, axis=1)
    weights = pn_ref[p]
    low = (weights * scale).astype(BF)
    grads = (ad_ref[p] * (scale * SCALE) - weights * (scale * shift * SCALE)).astype(BF)
    masks, _ = head_masks(p)
    late_ref[0, p] = mm(grads, two_heads(tp_ref[1, p], masks))
    late_ref[1, p] = mm(low, two_heads(tp_ref[3, p], masks))

    def stacked(x):
        return jnp.concatenate([x[:, :LANES], x[:, LANES:]], axis=0)

    for index, value in enumerate((mm(vt_ref[p], stacked(low)), mm(kt_ref[p], stacked(grads)))):
        value = value.astype(BF)
        for t, first, last in pieces_of(p):
            turned_ref[index, t * LANES + first : t * LANES + last] = value[first:last]


def branch(s):
    peak = jnp.max(s, axis=0, keepdims=True)
    weights = jnp.exp(s - peak)
    total = jnp.sum(weights, axis=0, keepdims=True)
    return weights, peak, total, peak + jnp.log(total)


def rows_of(row, first, second, third):
    first, second, third = [jnp.broadcast_to(x, row.shape) for x in (first, second, third)]
    return jnp.where(row == 0, first, jnp.where(row == 1, second, third))


def slide_scores(masks, flags, gr_ref, skv_ref):
    kv = skv_ref[...].reshape(-1, LANES)
    sources = gr_ref.shape[0]
    wide = gr_ref[:, S_ROW:G_ROWS].astype(F32)
    q, c = [wide[:, a : a + 8].reshape(sources * 8, LANES).astype(BF) for a in (0, 8)]
    q2, c2 = two_heads(q, masks, flags), two_heads(c, masks)
    both = mm_t(kv, jnp.concatenate([q2, c2], axis=0)).reshape(-1, 16, 2 * LANES)
    s = both[:, 0:8, :LANES].reshape(-1, LANES) * SCALE
    dp = both[:, 8:16, LANES:].reshape(-1, LANES)
    return kv, q2, c2, s, dp


def near_of(row, lane, ns_ref):
    slots, slide = [[None] * 2, [None] * 2], None

    def pick(keep, value, old):
        return value if old is None else jnp.where(keep, value, old)

    for source in range(8):
        j, q = divmod(source, 4)
        tile = jnp.concatenate([ns_ref[source]] * 4, axis=0)
        for slot in range(2):
            slots[slot][j] = pick((lane >> 5) == q, turn(tile, q * 32 - 32 * slot), slots[slot][j])
        first, second = [turn(tile, 64 * e + 8 * source - 64 - 8 * e) for e in range(2)]
        both = jnp.where(lane < 64, first, second)
        slide = pick(((lane & 63) >> 3) == source, both, slide)
    return [
        [rows_of(row, *[x[i : i + 1] for x in (slots[0][j], slots[1][j], slide)]) for i in range(2)]
        for j in range(2)
    ]


def crossed(row, lane, p, slide, group, fill):
    first = lax.rem(2 * p, 5) == 0
    any_head = jnp.logical_or(first, lax.rem(2 * p + 1, 5) == 0)
    e = jnp.where(first, 0, 1)
    at = p // 2 * 8
    source = jnp.broadcast_to(slide, row.shape)
    found, to_slide = [], None
    for j in range(2):
        chosen = jnp.broadcast_to(group[j], row.shape)
        to_group = None
        for q in range(4):
            here, there = q * 32 + at, (4 * j + q) * 8 + e * 64
            moved = turn(source, here - there + LANES)
            to_group = moved if q == 0 else jnp.where((lane >> 5) == q, moved, to_group)
            moved = turn(chosen, there - here + LANES)
            same = ((lane & 63) >> 3) == 4 * j + q
            to_slide = moved if to_slide is None else jnp.where(same, moved, to_slide)
        found.append(to_group)
    in_group = (row == 1) & ((lane & 31) >> 3 == p // 2) & any_head
    in_slide = (row == 2) & ((lane >> 6) == e) & any_head
    return [
        jnp.where(in_group | in_slide, jnp.where(row == 2, to_slide, to_group), fill)
        for to_group in found
    ]


class Slot:
    def __init__(self, p, e, gr_ref, at, group_bias, flag):
        sources = gr_ref.shape[0]
        lane = iota2((1, LANES), 1)
        self.rel = relative(lane, p, e)
        self.own, self.second = [as_mask((self.rel >= low) & (self.rel < low + 48)) for low in (0, 48)]
        head = self.rel < 48
        first = gr_ref[:, at : at + 32].reshape(sources * 32, LANES)
        rest = unfold_rows(gr_ref[:, at + 32 : at + 48].astype(F32)).reshape(sources * 32, LANES)
        wide = first.astype(F32)
        self.q = first * self.own + flag
        key = roll_lanes(wide, LANES - 48).astype(BF) * self.own
        self.k = key + group_bias
        self.v = jnp.where(self.rel < 32, roll_lanes(wide, 32), rest).astype(BF) * self.own
        self.c = roll_lanes(rest, LANES - 48).astype(BF) * self.own
        self.moved_k = first * self.second
        self.moved_c = rest.astype(BF) * self.second
        spread = jnp.where(self.rel >= 96, roll_lanes(wide, 96), wide)
        self.moved_q = spread.astype(BF) * as_mask((self.rel >= 96) | ((self.rel >= 32) & head))

    def scores(self, eye):
        self.parts = [
            branch(mm_t(self.k, self.q[j * LANES : (j + 1) * LANES]) * SCALE) for j in range(2)
        ]
        self.dps = [mm_t(self.v, self.c[j * LANES : (j + 1) * LANES]) for j in range(2)]
        self.deltas = [
            jnp.sum(part[0] * dp, axis=0, keepdims=True) / part[2]
            for part, dp in zip(self.parts, self.dps)
        ]
        both = jnp.concatenate([self.v, self.moved_k], axis=0)
        self.turned = mm_t(eye, both).astype(BF)

    def results(self, factors, deltas, eye2, sources):
        lows, grads = [], []
        for j, (part, dp) in enumerate(zip(self.parts, self.dps)):
            weights = part[0] * factors[j]
            lows.append(weights.astype(BF))
            grads.append((weights * (dp - deltas[j]) * SCALE).astype(BF))
        lows, grads = jnp.concatenate(lows, axis=1), jnp.concatenate(grads, axis=1)
        rest = mm(
            jnp.concatenate([grads, lows], axis=1), jnp.concatenate([self.moved_q, self.moved_c], axis=0)
        )
        first = mm(self.turned, jnp.concatenate([lows, grads], axis=0)).astype(BF)
        first = jnp.where(self.rel < 96, mm_t(eye2, first), rest)
        rest = fold_rows(rest.reshape(sources, 32, LANES), self.rel)
        return first.astype(BF).reshape(sources, 32, LANES), rest.astype(BF)


class Exchange:
    def __init__(self, count, make, every, first=1):
        self.count, self.make, self.every, self.first = count, make, every, first

    def start(self):
        @pl.loop(self.first, self.count)
        def _(step):
            self.make(step).start()

    def wait_recv(self):
        self.every.wait_recv()

    def wait_send(self):
        self.every.wait_send()


def wrapped(value, count):
    return jnp.where(value >= count, value - count, value)


def whole_kernel(
    inner, outers, len_hbm, q_hbm, k_hbm, v_hbm, c_hbm, att_ref, dq_ref, dk_ref, dv_ref,
    len_ref, loaded, load_sem, tp, gm, gr, skv_s, skv, pn, ad, kt, vt, ns_s, ns_r, r2_s, r2_r,
    r4_s, r4_r, xs, xr, sg_s, sg_r, late, turned, acc, whole, sent_wide, sent_small,
    send_sem, recv_sem, x_recv,
):
    outer, me = lax.axis_index("outer"), lax.axis_index("inner")
    p = me

    def scope(name):
        return jax.named_scope(name)

    def copy_to(src, dst, sems, index, device):
        return pltpu.make_async_remote_copy(
            src_ref=src,
            dst_ref=dst,
            send_sem=send_sem.at[1 if sems[0] is send_sem and index in (3, 4) else 0],
            recv_sem=sems[1].at[index],
            device_id=device,
            device_id_type=MESH,
        )

    def exchange(index, source, target, size):
        sems, next_place = (send_sem, recv_sem), wrapped(me + 1, inner)

        def make(step):
            peer = step - jnp.where(step <= me, 1, 0) if index > 3 and index != 9 else wrapped(me + step, inner)
            return copy_to(source(peer), target(me), sems, index, (outer, peer))

        return Exchange(inner, make, copy_to(size, size, sems, index, (outer, next_place)))

    def across(index, source, target, size):
        sems, next_place = (None, x_recv), wrapped(outer + 1, outers)

        def make(step):
            peer = step - jnp.where(step <= outer, 1, 0)
            return copy_to(source(peer), target, sems, index, (peer, me))

        return Exchange(outers, make, copy_to(size, size, sems, index, (next_place, me)))

    def blocks_exchange(index, src, dst):
        size = dst.at[pl.ds(0, inner - 1)]
        return exchange(index, lambda peer: src.at[peer], lambda mine: dst.at[mine], size)

    def rows_exchange(index, src, dst, first, last):
        rows = pl.ds(first, last - first)
        size = dst.at[pl.ds(0, inner - 1), rows]
        return exchange(index, lambda peer: src.at[peer, rows], lambda mine: dst.at[mine, rows], size)

    some = pl.ds(0, inner - 1)
    half = inner // 2
    mine = me // half * half
    away = half - mine

    def skv_copy(peer, index):
        return copy_to(skv_s.at[peer], skv.at[outer, me], (send_sem, recv_sem), index, (outer, peer))

    skv_size = skv.at[0, pl.ds(0, half)]
    far_skv = Exchange(
        half,
        lambda step: skv_copy(away + step, 0),
        copy_to(skv_size, skv_size, (send_sem, recv_sem), 0, (outer, away)),
        0,
    )
    skv_size = skv.at[0, pl.ds(0, half - 1)]
    close_skv = Exchange(
        half,
        lambda step: skv_copy(mine + wrapped(me - mine + step, half), 10),
        copy_to(skv_size, skv_size, (send_sem, recv_sem), 10, (outer, mine + wrapped(me - mine + 1, half))),
    )
    send_first = rows_exchange(1, gm, gr, 0, SLOT_ROWS)
    send_second = rows_exchange(2, gm, gr, SLOT_ROWS, S_ROW)
    send_qc = rows_exchange(9, gm, gr, S_ROW, G_ROWS)
    send_ns = blocks_exchange(3, ns_s, ns_r)
    send_r2 = blocks_exchange(4, r2_s, r2_r)
    back_first = rows_exchange(5, r4_s, r4_r, 0, SLOT_ROWS)
    back_second = rows_exchange(6, r4_s, r4_r, SLOT_ROWS, S_ROW)
    send_oq = rows_exchange(7, r4_s, r4_r, S_ROW, G_ROWS)
    send_sg = blocks_exchange(8, sg_s, sg_r)
    forwards = []
    for index, first in ((0, mine), (2, away)):
        part = skv.at[outer, pl.ds(first, half)]
        size = skv.at[pl.ds(0, outers - 1), pl.ds(0, half)]
        forwards.append(across(index, lambda peer, part=part: part, part, size))
    backwards = []
    for index, first, last in ((1, 0, SOON), (3, SOON, inner)):
        places = pl.ds(first, last - first)
        size = xr.at[pl.ds(0, outers - 1), places]
        backwards.append(
            across(index, lambda peer, places=places: xs.at[peer, places], xr.at[outer, places], size)
        )

    barrier = pltpu.get_barrier_semaphore()
    with scope("load_start"):
        loads = [
            pltpu.make_async_copy(ref, loaded.at[a], load_sem.at[a])
            for a, ref in enumerate((k_hbm, q_hbm, v_hbm, c_hbm))
        ]
        loads.append(pltpu.make_async_copy(len_hbm, len_ref, load_sem.at[4]))
        for index in (4, 0, 2, 1, 3):
            loads[index].start()
    with scope("greet"):

        @pl.loop(1, inner)
        def _(step):
            pl.semaphore_signal(
                barrier, inc=1, device_id=(outer, wrapped(me + step, inner)), device_id_type=MESH
            )

        @pl.loop(1, outers)
        def _(step):
            pl.semaphore_signal(
                barrier, inc=1, device_id=(wrapped(outer + step, outers), me), device_id_type=MESH
            )

    perm = permute_matrix(False)
    eye = identity(LANES)
    with scope("load_wait"):
        loads[4].wait()
        loads[0].wait()
        loads[2].wait()
    with scope("prep_kv"):
        bias = key_bias(len_ref)
        xk = mm(perm, loaded[0])
        xv = mm(perm, loaded[2])
        groups = []
        for h in range(PAIRS):
            first = h // 2 * 32
            rows = slice(first, first + 32)
            tile, key_slide = prep_pair(xk, h, bias)
            tp[0, h] = tile.astype(BF)
            groups.append([tile[rows]])
            tile, value_slide = prep_pair(xv, h)
            tp[2, h] = tile.astype(BF)
            groups[h].append(tile[rows])
            both = jnp.concatenate([key_slide, value_slide], axis=0)
            lane = iota2(both.shape, 1)
            for index in range(2):
                part = bias[first + 16 * index : first + 16 * index + 16]
                both = jnp.where(lane == flag_lane(h) + 2 + index, part, both)
            skv_s[h] = both.astype(BF)
    def pack_slot(h, slot):
        rel = relative(iota2((32, LANES), 1), h, head_of(h, slot))
        first, rest = packed(rel, *groups[h])
        at = SLOT_ROWS * slot
        gm[h, at : at + 32] = first.astype(BF)
        gm[h, at + 32 : at + 48] = rest.astype(BF)

    with scope("prep_qc"):
        loads[1].wait()
        loads[3].wait()
        xq = mm(perm, loaded[1])
        xc = mm(perm, loaded[3])
        slides = []
        for h in range(PAIRS):
            rows = slice(h // 2 * 32, h // 2 * 32 + 32)
            tile, query_slide = prep_pair(xq, h)
            tp[1, h] = tile.astype(BF)
            groups[h].insert(0, tile[rows])
            tile, cotan_slide = prep_pair(xc, h)
            tp[3, h] = tile.astype(BF)
            groups[h].append(tile[rows])
            slides.append(jnp.concatenate([query_slide, cotan_slide], axis=0))
            pack_slot(h, 0)
    with scope("prep_second"):
        for h in range(PAIRS):
            pack_slot(h, 1)
            gm[h, S_ROW:G_ROWS] = slides[h].astype(BF)
        gr[me] = gm[me]
        skv[outer, me] = skv_s[me]

    def near_forward():
        with scope("near_early"):
            for h in range(PAIRS):
                lse, delta = near_early(h, tp, pn, ad, kt, vt, eye)
                ns_s[h] = near_stats(h, lse, delta)

    ahead = me < inner // 2

    @pl.when(ahead)
    def _():
        near_forward()

    with scope("barrier_wait"):
        pl.semaphore_wait(barrier, inner - 1 + outers - 1)
    with scope("send_skv"):
        far_skv.start()
        close_skv.start()

    @pl.when(jnp.logical_not(ahead))
    def _():
        near_forward()

    with scope("send_first"):
        send_ns.start()
        send_first.start()
    with scope("send_ns"):
        send_qc.start()
        ns_r[me] = ns_s[me]
    with scope("close_wait"):
        close_skv.wait_recv()
    with scope("forward"):
        forwards[0].start()
    with scope("send_second"):
        send_second.start()
    with scope("far_wait"):
        far_skv.wait_recv()
    with scope("forward2"):
        forwards[1].start()
    masks, flags = head_masks(p)
    row, lane = iota2((8, LANES), 0), iota2((8, LANES), 1)
    eye2 = identity(2 * LANES)

    swap = swapped(p)
    with scope("bias"):
        near_keys = skv[outer].astype(F32)
        near_keys = jnp.concatenate([near_keys, pltpu.roll(near_keys, LANES - 1, 2)], axis=1)
        group_bias = near_keys.reshape(inner * 32, LANES).astype(BF) * flags[2]
    with scope("first_wait"):
        send_first.wait_recv()
    with scope("first_scores"):
        first = Slot(p, swap, gr, 0, group_bias, flags[2])
        first.scores(eye)
    with scope("ns_wait"):
        send_ns.wait_recv()
    with scope("first_merge"):
        near = near_of(row, lane, ns_r)
        first_factors, first_deltas, first_shares = [], [], []
        for j in range(2):
            near_lse, near_delta = near[j][0][0:1], near[j][1][0:1]
            _, peak, _, own = first.parts[j]
            best = jnp.maximum(near_lse, own)
            parts = [jnp.exp(x - best) for x in (near_lse, own)]
            total = parts[0] + parts[1]
            inverse = 1.0 / total
            first_factors.append(jnp.exp(peak - best - jnp.log(total)))
            first_deltas.append((parts[0] * near_delta + parts[1] * first.deltas[j]) * inverse)
            first_shares.append(parts[0] * inverse)
    with scope("first_results"):
        main, rest = first.results(first_factors, first_deltas, eye2, inner)
        r4_s[:, 0:32] = main
        r4_s[:, 32:48] = rest
    with scope("first_back"):
        back_first.start()
    with scope("forward_wait"):
        for sent in forwards:
            sent.wait_recv()
        send_qc.wait_recv()
    with scope("slide_scores"):
        skv_all, qs2, cs2, s, slide_dp = slide_scores(masks, flags, gr, skv)
        slide_weights, slide_peak, slide_total, slide_lse = branch(s)
        slide_delta = jnp.sum(slide_weights * slide_dp, axis=0, keepdims=True) / slide_total
        skv_t = mm_t(eye, skv_all).astype(BF)
    with scope("second_wait"):
        send_second.wait_recv()
    with scope("second_scores"):
        second = Slot(p, 1 - swap, gr, SLOT_ROWS, group_bias, flags[2])
        second.scores(eye)
    with scope("second_merge"):
        other = crossed(row, lane, p, slide_lse, [x[3] for x in second.parts], NEGATIVE_FILL)
        other_delta = crossed(row, lane, p, slide_delta, second.deltas, 0.0)

        def on_rows(group, slide):
            return jnp.where(row == 2, slide, group)

        factors, deltas, own_shares, own_moved = [], [], [], []
        for j in range(2):
            _, peak, _, group_lse = second.parts[j]
            own = on_rows(group_lse, slide_lse)
            best = jnp.maximum(jnp.maximum(near[j][0], own), other[j])
            parts = [jnp.exp(x - best) for x in (near[j][0], own, other[j])]
            total = parts[0] + parts[1] + parts[2]
            inverse = 1.0 / total
            factors.append(jnp.exp(on_rows(peak, slide_peak) - best - jnp.log(total)))
            delta = parts[0] * near[j][1] + parts[2] * other_delta[j]
            delta = (delta + parts[1] * on_rows(second.deltas[j], slide_delta)) * inverse
            deltas.append(delta)
            own_shares.append(parts[0] * inverse)
            own_moved.append(delta - near[j][1])
    with scope("slide_bwd"):
        weights = slide_weights * factors[0][2:3]
        grads = weights * (slide_dp - deltas[0][2:3]) * SCALE
        blocks = [x.reshape(-1, 8, LANES) for x in (grads, weights)]
        empty = jnp.zeros_like(blocks[0])
        mixed = jnp.concatenate(
            [
                jnp.concatenate([blocks[0], empty], axis=2),
                jnp.concatenate([empty, blocks[1]], axis=2),
            ],
            axis=1,
        )
        mixed = mixed.reshape(-1, 2 * LANES).astype(BF)
        xs[...] = mm(mixed, jnp.concatenate([qs2, cs2], axis=0)).astype(BF).reshape(xs.shape)
    with scope("send_x"):
        for sent in backwards:
            sent.start()
    with scope("r2_tiles"):
        first_moved = [first_deltas[j] - near[j][1][0:1] for j in range(2)]
        for source in range(inner):
            j, q = divmod(source, 4)
            tiles = [jnp.where(row == 0, first_shares[j], first_moved[j])]
            for at in (1, 2):
                pair = [x[j][at : at + 1] for x in (own_shares, own_moved)]
                tiles.append(jnp.where(row == 0, *pair))
            slots = [turn(tiles[slot], 32 * slot - 32 * q) for slot in range(2)]
            slides = [turn(tiles[2], 64 + 8 * e - 64 * e - 8 * source) for e in range(2)]
            r2_s[source] = compact(lane, slots, slides)[0:2]
    with scope("send_r2"):
        send_r2.start()
        r2_r[me] = r2_s[me]
    with scope("second_results"):
        main, rest = second.results(
            [x[1:2] for x in factors], [x[1:2] for x in deltas], eye2, inner
        )
        r4_s[:, 48:80] = main
        r4_s[:, 80:96] = rest
    with scope("second_back"):
        back_second.start()
    with scope("slide_q"):
        both = mm_t(eye2, mm(skv_t, mixed).astype(BF))
        quarter = LANES // 2
        head0 = head_lanes(iota2((quarter, LANES), 1), p, 0)
        query = jnp.where(head0, both[0:quarter], both[quarter:LANES])
        out = jnp.where(head0, both[LANES : 3 * quarter], both[3 * quarter : 4 * quarter])
        blocks = [x.reshape(inner, 8, LANES) for x in (out, query)]
        r4_s[:, S_ROW:G_ROWS] = jnp.concatenate(blocks, axis=1).astype(BF)
    with scope("send_oq"):
        send_oq.start()
        r4_r[me] = r4_s[me]
    with scope("clear"):
        acc[0:2] = jnp.zeros((2,) + acc.shape[1:], F32)
    soon = jnp.where(me < SOON, SOON, SOON + 1)
    for sent, places, steps in (
        (backwards[0], slice(0, SOON), (1, soon)),
        (backwards[1], slice(SOON, inner), (soon, inner)),
    ):
        with scope("x_wait"):
            sent.wait_recv()
        with scope("x_sum"):
            total = xs[outer, places].astype(F32)
            for step in range(1, outers):
                total = total + xr[wrapped(outer + step, outers), places].astype(F32)
            sg_s[places] = total.astype(BF)
        with scope("send_sg"):

            @pl.loop(*steps)
            def _(step):
                send_sg.make(step).start()

    sg_r[me] = sg_s[me]
    with scope("r2_wait"):
        send_r2.wait_recv()
    with scope("near_late1"):
        for h in range(PAIRS):
            near_late(h, r2_r, tp, pn, ad, kt, vt, late, turned)
    with scope("collect"):
        for a in range(2):
            for t in range(D_TILES):
                value = None
                for h in range(PAIRS):
                    for tile, first, last in pieces_of(h):
                        if tile == t:
                            piece = late[a, h]
                            lane_full = iota2(piece.shape, 1)
                            value = piece if value is None else jnp.where(lane_full >= first, piece, value)
                acc[2 + a, :, t * LANES : (t + 1) * LANES] = value
    for slot, sent in enumerate((back_first, back_second)):
        with scope("back_wait%d" % slot):
            sent.wait_recv()
        with scope("back_add%d" % slot):
            at = SLOT_ROWS * slot
            for h in range(PAIRS):
                add_group(acc, h, head_of(h, slot), r4_r[h, at : at + 32], r4_r[h, at + 32 : at + 48])
    with scope("place"):
        back = permute_matrix(True)
        for a in range(4):
            value = mm(back, acc[a].astype(BF))
            value = value + mm_t(back, turned[a]) if a < 2 else value
            for t in range(D_TILES):
                whole[a, t] = value[:, t * LANES : (t + 1) * LANES]
    for name, waited, blocks, outs in (
        ("oq", send_oq, lambda h: r4_r[h, S_ROW:G_ROWS], ((0, att_ref), (1, dq_ref))),
        ("sg", send_sg, lambda h: sg_r[h], ((2, dk_ref), (3, dv_ref))),
    ):
        with scope(name + "_wait"):
            waited.wait_recv()
        with scope(name + "_add"):
            for h in range(PAIRS):
                add_slide(whole, outs, h, blocks(h))
            for a, ref in outs:
                for t in range(D_TILES):
                    ref[:, t * LANES : (t + 1) * LANES] = whole[a, t].astype(BF)
    for index, sent in enumerate((sent_wide, sent_small)):
        copy_to(sent, sent, (send_sem, recv_sem), 3 * index, (outer, wrapped(me + 1, inner))).wait_send()


D_TILES = HEADS * HEAD // LANES


def write_kernel(*refs):
    count = len(refs) // 2
    copies = [pltpu.make_async_copy(refs[a], refs[count + a], refs[-1].at[a]) for a in range(count)]
    for copy in copies:
        copy.start()
    for copy in copies:
        copy.wait()


def add_group(acc, h, e, first, rest):
    first, rest = first.astype(F32), unfold_rows(rest.astype(F32))
    start = h // 2 * 32
    lane = iota2(first.shape, 1)
    rel = relative(lane, h, e)
    key = jnp.where(rel < 32, roll_lanes(first, 32), rest)
    values = (first, roll_lanes(first, LANES - 48), key, roll_lanes(rest, LANES - 48))
    for out, value in enumerate(values):
        for t, low, high in pieces_of(h):
            keep = (lane >= low) & (lane < high) & (rel < HEAD)
            cols = slice(t * LANES, (t + 1) * LANES)
            acc[out, start : start + 32, cols] += jnp.where(keep, value, 0.0)


def add_slide(whole, outs, h, block):
    block = block.astype(F32)
    lane = iota2((8, LANES), 1)
    for index, (out, _) in enumerate(outs):
        small = block[8 * index : 8 * index + 8]
        for e in range(2):
            rows = pl.ds(2 * h + e, 8, stride=HEADS)
            for t, first, last in pieces_of(h):
                if max(first, (PAIR * h + HEAD * e) - t * LANES) >= min(last, PAIR * h + HEAD * (e + 1) - t * LANES):
                    continue
                keep = (lane >= first) & (lane < last) & head_lanes(lane, h, e)
                whole[out, t, rows] += jnp.where(keep, small, 0.0)


def fast_local(inner, outers, *args):
    row_lengths, tiles_in = args[4], args[:4]
    tiles, width = tiles_in[0].shape
    vmem = pl.BlockSpec(memory_space=pltpu.VMEM)
    hbm = pl.BlockSpec(memory_space=pltpu.HBM)

    def both(shape, dtype):
        return [pltpu.VMEM(shape, dtype)] * 2

    scratch = [
        pltpu.SMEM(row_lengths.shape, jnp.int32),
        pltpu.VMEM((4, tiles, width), BF),
        pltpu.SemaphoreType.DMA((5,)),
        pltpu.VMEM((4, PAIRS, tiles, LANES), BF),
    ]
    scratch += both((inner, G_ROWS, LANES), BF)
    scratch += [pltpu.VMEM((inner, 16, LANES), BF), pltpu.VMEM((outers, inner, 16, LANES), BF)]
    scratch += both((PAIRS, tiles, 2 * LANES), F32)
    scratch += both((PAIRS, LANES, 2 * LANES), BF)
    scratch += both((inner, 2, LANES), F32) + both((inner, 2, LANES), F32)
    scratch += both((inner, G_ROWS, LANES), BF)
    scratch += both((outers, inner, 16, LANES), BF)
    scratch += both((inner, 16, LANES), BF)
    scratch += [pltpu.VMEM((2, PAIRS, tiles, LANES), F32), pltpu.VMEM((2, width, tiles), BF)]
    scratch += [pltpu.VMEM((4, tiles, width), F32), pltpu.VMEM((4, D_TILES, tiles, LANES), F32)]
    wide = 16 * (inner - 1) + 2 * (outers - 1) * inner
    scratch += [pltpu.VMEM((wide, 16, LANES), BF), pltpu.VMEM((2 * (inner - 1), 2, LANES), F32)]
    scratch += [pltpu.SemaphoreType.DMA((count,)) for count in (2, 11, 4)]
    in_hbm = [pltpu.with_memory_space_constraint(x, pltpu.HBM) for x in (row_lengths, *tiles_in)]
    out = [pltpu.VMEM((tiles, width), BF)] * 4
    in_vmem = pl.pallas_call(
        lambda *refs: whole_kernel(inner, outers, *refs),
        out_shape=out,
        in_specs=[hbm] * 5,
        out_specs=[vmem] * 4,
        scratch_shapes=scratch,
        compiler_params=pltpu.CompilerParams(
            collective_id=0, has_side_effects=True, vmem_limit_bytes=32 * 1024 * 1024
        ),
    )(*in_hbm)
    return tuple(
        pl.pallas_call(
            write_kernel,
            out_shape=[pltpu.HBM((tiles, width), BF)] * 4,
            in_specs=[vmem] * 4,
            out_specs=[hbm] * 4,
            scratch_shapes=[pltpu.SemaphoreType.DMA((4,))],
            compiler_params=pltpu.CompilerParams(vmem_limit_bytes=16 * 1024 * 1024),
        )(*in_vmem)
    )


def solution(mesh):
    in_specs = (P(("outer", "inner"), None),) * 4 + (P(("outer", "inner")),)
    out_specs = (P(("outer", "inner"), None),) * 4
    inner, outers = mesh.shape["inner"], mesh.shape["outer"]

    def step(*args):
        fits = inner == PAIRS and outers == 4
        if fits and args[0].shape == (LANES, HEADS * HEAD):
            return fast_local(inner, outers, *args)
        return local(*args)

    return jax.shard_map(step, mesh=mesh, in_specs=in_specs, out_specs=out_specs, check_vma=False)
```
